32 devices in a mesh: shard: 8 (over z, y), tp: 4 (over x, core).
Axes of the slice: x: 2, y: 2, z: 4, core: 2. Of those that a mesh axis runs over, the one named last changes fastest.
Arguments:
- tokens: bfloat16 [2048, 8, 1536], P('tp', 'shard'), may hold values from -6 to 6
- w_query: float32 [1536, 1536], P('shard', 'tp'), may hold values from -0.15625 to 0.15625
- w_keyval: float32 [1536, 256], P('shard'), may hold values from -0.15625 to 0.15625
- w_out: float32 [1536, 1536], P('tp', 'shard'), may hold values from -0.875 to 0.875
- w_gate: float32 [1536, 4608], P('shard', 'tp'), may hold values from -0.15625 to 0.15625
- w_up: float32 [1536, 4608], P('shard', 'tp'), may hold values from -0.15625 to 0.15625
- w_down: float32 [4608, 1536], P('tp', 'shard'), may hold values from -0.09375 to 0.09375
- gain_attn: float32 [1536], P('shard'), may hold values from 0.5 to 1.5
- gain_mlp: float32 [1536], P('shard'), may hold values from 0.5 to 1.5
- cotangent: bfloat16 [2048, 8, 1536], P(None, 'shard'), may hold values from -6 to 6
Outputs:
- output: bfloat16 [2048, 8, 1536], P('tp', 'shard')
- grad_tokens: float32 [2048, 8, 1536], P('tp', 'shard')
- grad_query: float32 [1536, 1536], P('shard', 'tp')
- grad_keyval: float32 [1536, 256], P('shard')
- grad_out: float32 [1536, 1536], P('tp', 'shard')
- grad_gate: float32 [1536, 4608], P('shard', 'tp')
- up_weight_gradient: float32 [1536, 4608], P('shard', 'tp')
- down_weight_gradient: float32 [4608, 1536], P('tp', 'shard')
- grad_gain_attn: float32 [1536], P('shard')
- grad_gain_mlp: float32 [1536], P('shard')
The draws below stay inside these ranges and needn't reach their ends.
All inputs are finite; a program needn't handle non-finite values.
Results may differ from the reference program's by a relative error of at most 0.02.
Values may be sent and summed in bfloat16 or wider, within the bound.
No kernel may reach another device: no remote copies, remote signals or barrier semaphores. Data moves between devices by JAX's collectives and lax.ppermute only.
A program may use at most 192 MiB of HBM per device.

```python
import jax
import jax.numpy as jnp
from jax import lax

D = 1536
H = 12
HD = 128
FF = 4608
WINDOW = 1024
BLOCK = 512
LEN = 2048
SEQS = 8


def level_of(own_key, dims, split, smallest, top_value):
    def one(axis_at, shards_of):
        steps = jax.random.uniform(jax.random.fold_in(jax.random.fold_in(own_key, 6), axis_at), (shards_of,), jnp.float32, smallest / len(split), top_value / len(split))
        return jnp.repeat(jnp.exp(steps), dims[axis_at] // shards_of).reshape((-1,) + (1,) * (len(dims) - axis_at - 1))

    factor_of = one(*split[0])
    for cut in split[1:]:
        factor_of = factor_of * one(*cut)
    return factor_of


def scatter_about(stream_key, extent, width, bound, cuts=(), kind=jnp.bfloat16):
    entries = jax.random.normal(stream_key, extent, jnp.float32) * width
    if len(cuts) > 0:
        entries = level_of(stream_key, extent, cuts, -0.22, 0.18) * entries
    return jnp.clip(entries, min=-bound, max=bound).astype(kind)


def setup_inputs(seed: int = 0) -> dict:
    key_list = jax.random.split(jax.random.key(seed), 11)
    return {
        "tokens": scatter_about(key_list[0], (LEN, SEQS, D), 1.0, 6.0, ((0, 4), (1, 8))),
        "w_query": scatter_about(key_list[1], (D, H * HD), D ** -0.5, 0.15625, ((0, 8), (1, 4)), jnp.float32),
        "w_keyval": scatter_about(key_list[2], (D, 2 * HD), D ** -0.5, 0.15625, ((0, 8),), jnp.float32),
        "w_out": scatter_about(key_list[3], (H * HD, D), (H * HD // 32) ** -0.5, 0.875, ((0, 4), (1, 8)), jnp.float32),
        "w_gate": scatter_about(key_list[4], (D, FF), D ** -0.5, 0.15625, ((0, 8), (1, 4)), jnp.float32),
        "w_up": scatter_about(key_list[5], (D, FF), D ** -0.5, 0.15625, ((0, 8), (1, 4)), jnp.float32),
        "w_down": scatter_about(key_list[6], (FF, D), FF ** -0.5, 0.09375, ((0, 4), (1, 8)), jnp.float32),
        "gain_attn": jnp.clip(1.0 + 0.1 * jax.random.normal(key_list[7], (D,), jnp.float32), 0.5, 1.5),
        "gain_mlp": jnp.clip(1.0 + 0.1 * jax.random.normal(key_list[8], (D,), jnp.float32), 0.5, 1.5),
        "cotangent": scatter_about(key_list[9], (LEN, SEQS, D), 1.0, 6.0, ((1, 8),)),
    }


@jax.custom_vjp
def low(v):
    return lax.optimization_barrier(v.astype(jnp.bfloat16)).astype(jnp.float32)

@jax.custom_vjp
def low_back(v):
    return v

def low_keep(v):
    return (low(v), None)

def low_pass(kept, grad):
    return (grad,)

def back_keep(v):
    return (v, None)

def back_low(kept, grad):
    return (low(grad),)
low.defvjp(low_keep, low_pass)
low_back.defvjp(back_keep, back_low)
EPS = 1e-06
HIGHEST = lax.Precision.HIGHEST

def rms_scale(hidden, weight_gain):
    return hidden * lax.rsqrt(lax.optimization_barrier(jnp.mean(hidden * hidden, axis=-1, keepdims=True)) + EPS) * weight_gain

def block_mask(start):
    row_index = jnp.arange(BLOCK, dtype=jnp.int32)[:, None]
    col_index = jnp.arange(WINDOW + BLOCK, dtype=jnp.int32)[None, :]
    offset = row_index + WINDOW - col_index
    return (offset >= 0) & (offset < WINDOW) & (col_index >= WINDOW - start)

def window_attention(query, keys, values):
    padding = jnp.zeros((WINDOW, HD), jnp.float32)
    key_pad = jnp.concatenate([padding, keys], 0)
    value_pad = jnp.concatenate([padding, values], 0)
    blocks = LEN // BLOCK
    query_blocks = query.reshape(blocks, BLOCK, H, HD)
    starts = jnp.arange(blocks, dtype=jnp.int32) * BLOCK

    def one_block(element):
        query_block, start = element
        key_block = lax.dynamic_slice_in_dim(key_pad, start.astype(jnp.int32), WINDOW + BLOCK, 0)
        value_block = lax.dynamic_slice_in_dim(value_pad, start.astype(jnp.int32), WINDOW + BLOCK, 0)
        scores = HD ** (-0.5) * jnp.einsum('ahd,cd->hac', query_block, key_block, precision=HIGHEST)
        scores = low_back(scores)
        scores = jnp.where(block_mask(start)[None], scores, -1e+30)
        maximum = lax.optimization_barrier(jnp.max(scores, axis=-1, keepdims=True))
        logsum = maximum + jnp.log(lax.optimization_barrier(jnp.sum(jnp.exp(scores - maximum), axis=-1, keepdims=True)))
        probs = low(jnp.exp(scores - logsum))
        return jnp.einsum('hac,cd->ahd', probs, value_block, precision=HIGHEST)
    mixed = lax.map(jax.checkpoint(one_block), (query_blocks, starts))
    return mixed.reshape(LEN, H * HD)

def forward(tokens, w_query, w_keyval, w_out, w_gate, w_up, w_down, gain_attn, gain_mlp):
    normed = low(rms_scale(tokens, low(gain_attn)))
    query = low(low_back(jnp.dot(normed, low(w_query), precision=HIGHEST)))
    keyval = low(low_back(jnp.dot(normed, low(w_keyval), precision=HIGHEST)))
    mixed = window_attention(query.reshape(LEN, H, HD), keyval[:, :HD], keyval[:, HD:])
    mixed = low(low_back(mixed))
    branch = low_back(jnp.dot(mixed, low(w_out), precision=HIGHEST))
    hidden = tokens + branch
    feedforward_normed_input = low(rms_scale(hidden, low(gain_mlp)))
    gate = low_back(jnp.dot(feedforward_normed_input, low(w_gate), precision=HIGHEST))
    upward = low_back(jnp.dot(feedforward_normed_input, low(w_up), precision=HIGHEST))
    gated_product = low(jax.nn.gelu(gate) * upward)
    return hidden + low_back(jnp.dot(gated_product, low(w_down), precision=HIGHEST))

def reference(tokens, w_query, w_keyval, w_out, w_gate, w_up, w_down, gain_attn, gain_mlp, cotangent):
    weights = (w_query, w_keyval, w_out, w_gate, w_up, w_down, gain_attn, gain_mlp)

    def one_sequence(totals, element):
        sequence, seq_grad = element
        result, pullback = jax.vjp(forward, sequence.astype(jnp.float32), *weights)
        grads = pullback(seq_grad.astype(jnp.float32))
        totals = tuple((total + grad for total, grad in zip(totals, grads[1:])))
        return (totals, (result.astype(jnp.bfloat16), grads[0]))
    zeros = tuple((jnp.zeros(weight.shape, jnp.float32) for weight in weights))
    totals, (results, grad_inputs) = lax.scan(one_sequence, zeros, (jnp.moveaxis(tokens, 1, 0), jnp.moveaxis(cotangent, 1, 0)))
    return (jnp.moveaxis(results, 0, 1), jnp.moveaxis(grad_inputs, 0, 1), totals[0], totals[1], totals[2], totals[3], totals[4], totals[5], totals[6], totals[7])
```

```python
import functools

import jax
import jax.numpy as jnp
from jax import lax
from jax.experimental import pallas as pl
from jax.experimental.pallas import tpu as pltpu
from jax.sharding import PartitionSpec as P

HD = 128
WINDOW = 1024
QB = 256
GROUP = 3
EPS = 1e-06
LOG2E = 1.4426950408889634
LN2 = 0.6931471805599453
NEG = -1e30
BF = jnp.bfloat16
F32 = jnp.float32
NT = (((1,), (1,)), ((), ()))
TN = (((0,), (0,)), ((), ()))
NN = (((1,), (0,)), ((), ()))


def dot(a, b, dims=NN):
    return lax.dot_general(a, b, dims, preferred_element_type=F32)


def after(value, *others):
    return lax.optimization_barrier((value, *others))[0]


def forward_attention_kernel(chip_ref, q_ref, k_ref, vt_ref, o_ref, lse_ref):
    block = pl.program_id(0)
    chunks = WINDOW // QB
    key_row = lax.broadcasted_iota(jnp.int32, (QB, QB), 0)
    query_col = lax.broadcasted_iota(jnp.int32, (QB, QB), 1)

    def rows_of(chunk):
        return pl.ds(pl.multiple_of((block + chunk) * QB, QB), QB)

    def finish(head, top, total, mixed):
        cols = slice(head * HD, (head + 1) * HD)
        o_ref[:, cols] = jnp.transpose(mixed / total).astype(BF)
        lse_ref[head : head + 1, :] = top + jnp.log(total) * LOG2E

    @pl.when(chip_ref[0] != 0)
    def _():
        for head in range(GROUP):
            query = q_ref[:, head * HD : (head + 1) * HD]
            scores = []
            for chunk in range(chunks + 1):
                part = dot(k_ref[rows_of(chunk), :], query, NT)
                if chunk == 0:
                    part = jnp.where(key_row > query_col, part, NEG)
                if chunk == chunks:
                    part = jnp.where(key_row <= query_col, part, NEG)
                scores.append(part)
            top = jnp.max(functools.reduce(jnp.maximum, scores), axis=0, keepdims=True)
            total = jnp.zeros((1, QB), F32)
            mixed = jnp.zeros((HD, QB), F32)
            for chunk in range(chunks + 1):
                probs = jnp.exp2(scores[chunk] - top)
                total = total + jnp.sum(probs, axis=0, keepdims=True)
                mixed = mixed + dot(vt_ref[:, rows_of(chunk)], probs.astype(BF))
            finish(head, top, total, mixed)

    @pl.when(chip_ref[0] == 0)
    def _():
        for head in range(GROUP):
            query = q_ref[:, head * HD : (head + 1) * HD]

            def step(chunk, carry):
                top, total, mixed = carry
                part = dot(k_ref[rows_of(chunk), :], query, NT)
                part = jnp.where((key_row <= query_col) | (chunk < chunks), part, NEG)
                new_top = jnp.maximum(top, jnp.max(part, axis=0, keepdims=True))
                shrink = jnp.exp2(top - new_top)
                probs = jnp.exp2(part - new_top)
                total = total * shrink + jnp.sum(probs, axis=0, keepdims=True)
                mixed = mixed * shrink + dot(vt_ref[:, rows_of(chunk)], probs.astype(BF))
                return (new_top, total, mixed)

            first = (jnp.full((1, QB), NEG, F32), jnp.zeros((1, QB), F32), jnp.zeros((HD, QB), F32))
            top, total, mixed = lax.fori_loop(chunks - block, chunks + 1, step, first)
            finish(head, top, total, mixed)


def forward_attention(chip, query, keys, values_t):
    rows = query.shape[0]
    width = GROUP * HD
    return pl.pallas_call(
        forward_attention_kernel,
        grid_spec=pltpu.PrefetchScalarGridSpec(
            num_scalar_prefetch=1,
            grid=(rows // QB,),
            in_specs=[
                pl.BlockSpec((QB, width), lambda b, s: (b, 0)),
                pl.BlockSpec((2 * rows, HD), lambda b, s: (0, 0)),
                pl.BlockSpec((HD, 2 * rows), lambda b, s: (0, 0)),
            ],
            out_specs=[
                pl.BlockSpec((QB, width), lambda b, s: (b, 0)),
                pl.BlockSpec((8, QB), lambda b, s: (0, b)),
            ],
        ),
        out_shape=(
            jax.ShapeDtypeStruct((rows, width), BF),
            jax.ShapeDtypeStruct((8, rows), F32),
        ),
        compiler_params=pltpu.CompilerParams(vmem_limit_bytes=40 << 20),
        cost_estimate=pl.CostEstimate(
            flops=9_000_000_000, transcendentals=4_000_000, bytes_accessed=4_000_000
        ),
        name="attention_forward",
    )(chip, query, keys, values_t)


def backward_attention_kernel(
    chip_ref, q_ref, g_ref, o_ref, lse_ref, k_ref, kt_ref, v_ref, dq_ref, dk_ref, dv_ref
):
    block = pl.program_id(0)
    chunks = WINDOW // QB
    key_row = lax.broadcasted_iota(jnp.int32, (QB, QB), 0)
    query_col = lax.broadcasted_iota(jnp.int32, (QB, QB), 1)

    @pl.when(block == 0)
    def _():
        dk_ref[...] = jnp.zeros_like(dk_ref)
        dv_ref[...] = jnp.zeros_like(dv_ref)

    def rows_of(chunk):
        return pl.ds(pl.multiple_of((block + chunk) * QB, QB), QB)

    deltas = []
    for head in range(GROUP):
        cols = slice(head * HD, (head + 1) * HD)
        both = g_ref[:, cols].astype(F32) * o_ref[:, cols].astype(F32)
        deltas.append(jnp.sum(jnp.transpose(both), axis=0, keepdims=True))

    def one_chunk(chunk, keep, totals):
        rows = rows_of(chunk)
        keys = k_ref[rows, :]
        values = v_ref[rows, :]
        keys_t = kt_ref[:, rows]
        grad_keys = jnp.zeros((QB, HD), F32)
        grad_values = jnp.zeros((QB, HD), F32)
        new = []
        for head in range(GROUP):
            cols = slice(head * HD, (head + 1) * HD)
            query = q_ref[:, cols]
            grad = g_ref[:, cols]
            probs = jnp.exp2(dot(keys, query, NT) - lse_ref[head : head + 1, :])
            if keep is not None:
                probs = jnp.where(keep, probs, 0.0)
            grad_scores = (probs * (dot(values, grad, NT) - deltas[head])).astype(BF)
            grad_values = grad_values + dot(probs.astype(BF), grad)
            grad_keys = grad_keys + dot(grad_scores, query)
            new.append(totals[head] + dot(keys_t, grad_scores))
        dk_ref[rows, :] += grad_keys
        dv_ref[rows, :] += grad_values
        return tuple(new)

    def finish(totals):
        for head in range(GROUP):
            cols = slice(head * HD, (head + 1) * HD)
            dq_ref[:, cols] = (jnp.transpose(totals[head]) * HD ** (-0.5)).astype(BF)

    zeros = tuple(jnp.zeros((HD, QB), F32) for _ in range(GROUP))

    @pl.when(chip_ref[0] != 0)
    def _():
        totals = zeros
        for chunk in range(chunks + 1):
            keep = None
            if chunk == 0:
                keep = key_row > query_col
            if chunk == chunks:
                keep = key_row <= query_col
            totals = one_chunk(chunk, keep, totals)
        finish(totals)

    @pl.when(chip_ref[0] == 0)
    def _():
        def step(chunk, totals):
            return one_chunk(chunk, (key_row <= query_col) | (chunk < chunks), totals)

        finish(lax.fori_loop(chunks - block, chunks + 1, step, zeros))


def backward_attention(chip, query, grad, mixed, lse, keys, keys_t, values):
    rows = query.shape[0]
    width = GROUP * HD
    wide = pl.BlockSpec((QB, width), lambda b, s: (b, 0))
    whole = pl.BlockSpec((2 * rows, HD), lambda b, s: (0, 0))
    return pl.pallas_call(
        backward_attention_kernel,
        grid_spec=pltpu.PrefetchScalarGridSpec(
            num_scalar_prefetch=1,
            grid=(rows // QB,),
            in_specs=[
                wide,
                wide,
                wide,
                pl.BlockSpec((8, QB), lambda b, s: (0, b)),
                whole,
                pl.BlockSpec((HD, 2 * rows), lambda b, s: (0, 0)),
                whole,
            ],
            out_specs=[wide, whole, whole],
        ),
        out_shape=(
            jax.ShapeDtypeStruct((rows, width), BF),
            jax.ShapeDtypeStruct((2 * rows, HD), F32),
            jax.ShapeDtypeStruct((2 * rows, HD), F32),
        ),
        compiler_params=pltpu.CompilerParams(vmem_limit_bytes=40 << 20),
        cost_estimate=pl.CostEstimate(
            flops=18_000_000_000, transcendentals=4_000_000, bytes_accessed=8_000_000
        ),
        name="attention_backward",
    )(chip, query, grad, mixed, lse, keys, keys_t, values)


def assemble_kernel(count, place_ref, *refs):
    pieces, whole = refs[:count], refs[count]
    depth = pieces[0].shape[0]
    for i in range(count):
        whole[pl.ds(pl.multiple_of(place_ref[i] * depth, depth), depth), :] = pieces[i][...]


def assemble(places, pieces):
    count = len(pieces)
    depth, width = pieces[0].shape
    piece = pl.BlockSpec((depth, width), lambda i, s: (0, 0), pipeline_mode=pl.Buffered(1))
    return pl.pallas_call(
        functools.partial(assemble_kernel, count),
        grid_spec=pltpu.PrefetchScalarGridSpec(
            num_scalar_prefetch=1,
            grid=(1,),
            in_specs=[piece] * count,
            out_specs=pl.BlockSpec((count * depth, width), lambda i, s: (0, 0)),
        ),
        out_shape=jax.ShapeDtypeStruct((count * depth, width), pieces[0].dtype),
        compiler_params=pltpu.CompilerParams(vmem_limit_bytes=24 << 20),
        cost_estimate=pl.CostEstimate(
            flops=0, transcendentals=0, bytes_accessed=4 * count * depth * width
        ),
        name="assemble_pieces",
    )(places, *pieces)


def split_kernel(count, place_ref, whole, *pieces):
    depth = pieces[0].shape[0]
    for i in range(count):
        pieces[i][...] = whole[pl.ds(pl.multiple_of(place_ref[i] * depth, depth), depth), :]


def split(places, whole, count):
    depth, width = whole.shape[0] // count, whole.shape[1]
    piece = pl.BlockSpec((depth, width), lambda i, s: (0, 0), pipeline_mode=pl.Buffered(1))
    return pl.pallas_call(
        functools.partial(split_kernel, count),
        grid_spec=pltpu.PrefetchScalarGridSpec(
            num_scalar_prefetch=1,
            grid=(1,),
            in_specs=[pl.BlockSpec(whole.shape, lambda i, s: (0, 0))],
            out_specs=[piece] * count,
        ),
        out_shape=(jax.ShapeDtypeStruct((depth, width), whole.dtype),) * count,
        compiler_params=pltpu.CompilerParams(vmem_limit_bytes=24 << 20),
        cost_estimate=pl.CostEstimate(
            flops=0, transcendentals=0, bytes_accessed=4 * count * depth * width
        ),
        name="split_pieces",
    )(places, whole)


class Shards:
    def __init__(self, count):
        self.count = count
        self.half = count // 2
        index = lax.axis_index("shard").astype(jnp.int32)
        hi, lo = index // 2, index % 2
        mine = [(hi ^ k) * 2 + lo for k in range(self.half)]
        partner = [(hi ^ k) * 2 + (1 - lo) for k in range(self.half)]
        self.places = jnp.stack(mine + partner)

    def far(self, value, k):
        return lax.ppermute(
            value, "shard", [(i, ((i // 2) ^ k) * 2 + i % 2) for i in range(self.count)]
        )

    def near(self, value):
        return lax.ppermute(value, "shard", [(i, i ^ 1) for i in range(self.count)])

    def gather_far(self, piece):
        return [piece] + [self.far(piece, k) for k in range(1, self.half)]

    def gather_near(self, pieces):
        return pieces + [self.near(piece) for piece in pieces]

    def whole(self, pieces):
        return assemble(self.places, pieces)

    def scatter(self, value):
        pieces = split(self.places, value, self.count)
        kept, sent = pieces[: self.half], pieces[self.half :]
        sums = [
            (a.astype(F32) + self.near(b).astype(F32)).astype(BF) for a, b in zip(kept, sent)
        ]
        total = sums[0].astype(F32)
        for k in range(1, self.half):
            total = total + self.far(sums[k], k).astype(F32)
        return total


def tp_swap(value, mask):
    return lax.ppermute(value, "tp", [(i, i ^ mask) for i in range(4)])


def gelu_parts(gate):
    inner = 0.7978845608028654 * (gate + 0.044715 * gate * gate * gate)
    t = jnp.tanh(inner)
    value = 0.5 * gate * (1.0 + t)
    slope = 0.5 * (1.0 + t) + 0.5 * gate * (1.0 - t * t) * 0.7978845608028654 * (
        1.0 + 3.0 * 0.044715 * gate * gate
    )
    return value, slope


def local(count, tokens, w_query, w_keyval, w_out, w_gate, w_up, w_down, gain_attn, gain_mlp, cotangent):
    rows, width = tokens.shape[0], tokens.shape[2]
    tp = lax.axis_index("tp").astype(jnp.int32)
    core, chip = tp % 2, tp // 2
    first_core = core == 0
    chip_table = jnp.reshape(chip, (1,))
    shards = Shards(count)

    def in_order(own, other):
        return jnp.where(
            first_core, jnp.concatenate([own, other], 0), jnp.concatenate([other, own], 0)
        )

    gain_one = gain_attn.astype(BF).astype(F32)[:, None]
    gain_two = gain_mlp.astype(BF).astype(F32)[:, None]
    own_query = w_query.astype(BF).astype(F32)
    own_keyval = w_keyval.astype(BF).astype(F32)
    own_gate = w_gate.astype(BF).astype(F32)
    own_up = w_up.astype(BF).astype(F32)
    keyval_half = jnp.where(first_core, own_keyval[:, :HD], own_keyval[:, HD:])
    send_in = (jnp.concatenate([own_query, keyval_half], 1) * gain_one).astype(BF)
    send_out = jnp.transpose(w_out).astype(BF)
    send_gate = (own_gate * gain_two).astype(BF)
    send_up = (own_up * gain_two).astype(BF)
    send_down = jnp.transpose(w_down).astype(BF)

    far_in = shards.gather_far(send_in)
    far_out = shards.gather_far(after(send_out, *far_in[1:]))
    far_gate = shards.gather_far(after(send_gate, *far_out[1:]))
    far_up = shards.gather_far(after(send_up, *far_gate[1:]))
    far_down = shards.gather_far(after(send_down, *far_up[1:]))

    inputs = tokens.reshape(rows, width).astype(F32)
    scale_one = lax.rsqrt(jnp.mean(inputs * inputs, axis=-1, keepdims=True) + EPS)
    unit_own = (inputs * scale_one).astype(BF)
    unit = in_order(unit_own, tp_swap(unit_own, 1))
    cot = cotangent.reshape(4, rows, width)
    cots = [lax.dynamic_index_in_dim(cot, tp ^ k, 0, keepdims=False) for k in range(4)]
    cot_near = jnp.concatenate(cots[:2], 0)
    cot_far = jnp.concatenate(cots[2:], 0)

    in_full = shards.whole(shards.gather_near(far_in))
    in_query = in_full[:, : GROUP * HD]
    in_key = in_full[:, GROUP * HD :]
    in_query_b = tp_swap(in_query, 2)
    out_full = shards.whole(shards.gather_near(far_out))
    out_full_b = tp_swap(after(out_full, in_query_b), 2)

    half = dot(unit, in_key).astype(BF)
    half_other = tp_swap(half, 1)
    before = lax.ppermute(half, "tp", [(0, 2), (1, 3)])
    before_other = tp_swap(before, 1)
    own_pair = jnp.concatenate([before, half], 0)
    other_pair = jnp.concatenate([before_other, half_other], 0)
    keys = jnp.where(first_core, own_pair, other_pair)
    values = jnp.where(first_core, other_pair, own_pair)
    keys_t = jnp.transpose(keys)
    values_t = jnp.transpose(values)

    scale = HD ** (-0.5)
    query_a = (dot(unit, in_query) * (scale * LOG2E)).astype(BF)
    mixed_a, lse_a = forward_attention(chip_table, query_a, keys, values_t)
    query_b = (dot(unit, in_query_b) * (scale * LOG2E)).astype(BF)
    mixed_b, lse_b = forward_attention(chip_table, query_b, keys, values_t)

    branch = dot(mixed_a, out_full, NT) + dot(mixed_b, out_full_b, NT)
    branch_own = lax.dynamic_slice_in_dim(branch, core * rows, rows, 0)
    branch_other = lax.dynamic_slice_in_dim(branch, (1 - core) * rows, rows, 0).astype(BF)
    hidden = inputs + (branch_own + tp_swap(branch_other, 1).astype(F32))
    scale_two = lax.rsqrt(jnp.mean(hidden * hidden, axis=-1, keepdims=True) + EPS)
    norm_own = (hidden * scale_two).astype(BF)
    norm_x = tp_swap(norm_own, 2)
    norm_near = jnp.concatenate([norm_own, tp_swap(norm_own, 1)], 0)
    norm_far = jnp.concatenate([norm_x, tp_swap(norm_x, 1)], 0)

    gate_full = shards.whole(shards.gather_near(far_gate))
    up_full = shards.whole(shards.gather_near(far_up))
    down_full = shards.whole(shards.gather_near(far_down))

    def feed_forward(norm, cot_part):
        gate = dot(norm, gate_full)
        up = dot(norm, up_full)
        value, slope = gelu_parts(gate)
        product = (value * up).astype(BF)
        grad_product = dot(cot_part, down_full)
        grad_gate = (grad_product * up * slope).astype(BF)
        grad_up = (grad_product * value).astype(BF)
        return product, grad_gate, grad_up

    product_near, dgate_near, dup_near = feed_forward(norm_near, cot_near)
    product_far, dgate_far, dup_far = feed_forward(norm_far, cot_far)

    def reduce_rows(near, far):
        out_far = far[:rows] + tp_swap(far[rows:].astype(BF), 1).astype(F32)
        mine = near[:rows] + tp_swap(near[rows:].astype(BF), 1).astype(F32)
        return mine + tp_swap(out_far.astype(BF), 2).astype(F32)

    back_far = dot(dgate_far, gate_full, NT) + dot(dup_far, up_full, NT)
    back_near = dot(dgate_near, gate_full, NT) + dot(dup_near, up_full, NT)
    grad_norm = reduce_rows(back_near, back_far)

    down_far = dot(product_far, down_full, NT)
    down_near = dot(product_near, down_full, NT)
    output = (hidden + reduce_rows(down_near, down_far)).astype(BF)

    norm_all = jnp.concatenate([norm_near, norm_far], 0)
    g_down = dot(
        jnp.concatenate([cot_near, cot_far], 0), jnp.concatenate([product_near, product_far], 0), TN
    ).astype(BF)
    g_gate = dot(norm_all, jnp.concatenate([dgate_near, dgate_far], 0), TN).astype(BF)
    g_up = dot(norm_all, jnp.concatenate([dup_near, dup_far], 0), TN).astype(BF)
    grad_w_down = jnp.transpose(shards.scatter(g_down))
    sum_gate = shards.scatter(g_gate)
    sum_up = shards.scatter(g_up)
    grad_w_gate = sum_gate * gain_two
    grad_w_up = sum_up * gain_two
    gain_two_part = jnp.sum(own_gate * sum_gate + own_up * sum_up, axis=1)

    unit_two = hidden * scale_two
    grad_hidden = cots[0].astype(F32) + scale_two * (
        grad_norm - unit_two * jnp.mean(grad_norm * unit_two, axis=-1, keepdims=True)
    )
    grad_branch_own = grad_hidden.astype(BF)
    grad_branch = in_order(grad_branch_own, tp_swap(grad_branch_own, 1))

    grad_mixed_b = dot(grad_branch, out_full_b).astype(BF)
    dq_b, dk_b, dv_b = backward_attention(
        chip_table, query_b, grad_mixed_b, mixed_b, lse_b, keys, keys_t, values
    )
    g_query_b = dot(unit, dq_b, TN).astype(BF)
    g_out_b = dot(grad_branch, mixed_b, TN).astype(BF)
    grad_mixed_a = dot(grad_branch, out_full).astype(BF)
    dq_a, dk_a, dv_a = backward_attention(
        chip_table, query_a, grad_mixed_a, mixed_a, lse_a, keys, keys_t, values
    )
    g_out = dot(grad_branch, mixed_a, TN) + tp_swap(g_out_b, 2).astype(F32)
    grad_w_out = jnp.transpose(shards.scatter(g_out.astype(BF)))

    grad_keys = (dk_a + dk_b) * LN2
    grad_values = dv_a + dv_b
    mine = jnp.where(first_core, grad_keys, grad_values)
    theirs = jnp.where(first_core, grad_values, grad_keys).astype(BF)
    mine = mine + tp_swap(theirs, 1).astype(F32)
    chip_rows = mine.shape[0] // 2
    earlier = lax.ppermute(mine[:chip_rows].astype(BF), "tp", [(2, 0), (3, 1)])
    grad_half = (mine[chip_rows:] + earlier.astype(F32)).astype(BF)

    g_query = dot(unit, dq_a, TN) + tp_swap(g_query_b, 2).astype(F32)
    g_half = dot(unit, grad_half, TN)
    g_in = jnp.concatenate([g_query, g_half], 1).astype(BF)
    sum_in = shards.scatter(g_in)

    back = dot(dq_a, in_query, NT) + dot(dq_b, in_query_b, NT) + dot(grad_half, in_key, NT)
    back_own = lax.dynamic_slice_in_dim(back, core * rows, rows, 0)
    back_other = lax.dynamic_slice_in_dim(back, (1 - core) * rows, rows, 0).astype(BF)
    grad_unit = back_own + tp_swap(back_other, 1).astype(F32)
    unit_one = inputs * scale_one
    grad_tokens = grad_hidden + scale_one * (
        grad_unit - unit_one * jnp.mean(grad_unit * unit_one, axis=-1, keepdims=True)
    )

    sum_query = sum_in[:, : GROUP * HD]
    sum_half = sum_in[:, GROUP * HD :]
    gain_query_part = jnp.sum(own_query * sum_query, axis=1)
    gain_half_part = jnp.sum(keyval_half * sum_half, axis=1)
    gains = jnp.stack([gain_query_part + gain_half_part, gain_two_part], 0)
    gains = gains + tp_swap(gains, 1)
    gains = gains + tp_swap(gains, 2)
    sum_half = sum_half + tp_swap(sum_half, 2)
    half_swapped = tp_swap(sum_half, 1)
    grad_w_keyval = (
        jnp.where(
            first_core,
            jnp.concatenate([sum_half, half_swapped], 1),
            jnp.concatenate([half_swapped, sum_half], 1),
        )
        * gain_one
    )
    return (
        output.reshape(rows, 1, width),
        grad_tokens.reshape(rows, 1, width),
        sum_query * gain_one,
        grad_w_keyval,
        grad_w_out,
        grad_w_gate,
        grad_w_up,
        grad_w_down,
        gains[0],
        gains[1],
    )


def solution(mesh):
    in_specs = (
        P("tp", "shard", None),
        P("shard", "tp"),
        P("shard", None),
        P("tp", "shard"),
        P("shard", "tp"),
        P("shard", "tp"),
        P("tp", "shard"),
        P("shard"),
        P("shard"),
        P(None, "shard", None),
    )
    out_specs = (
        P("tp", "shard", None),
        P("tp", "shard", None),
        P("shard", "tp"),
        P("shard", None),
        P("tp", "shard"),
        P("shard", "tp"),
        P("shard", "tp"),
        P("tp", "shard"),
        P("shard"),
        P("shard"),
    )
    return jax.shard_map(
        functools.partial(local, mesh.shape["shard"]),
        mesh=mesh,
        in_specs=in_specs,
        out_specs=out_specs,
        check_vma=False,
    )
```

```python
import functools

import jax
import jax.numpy as jnp
from jax import lax
from jax.experimental import pallas as pl
from jax.experimental.pallas import tpu as pltpu
from jax.sharding import PartitionSpec as P

HD = 128
WINDOW = 1024
QB = 256
GROUP = 3
EPS = 1e-06
LOG2E = 1.4426950408889634
LN2 = 0.6931471805599453
NEG = -1e30
BF = jnp.bfloat16
F32 = jnp.float32
NT = (((1,), (1,)), ((), ()))
TN = (((0,), (0,)), ((), ()))
NN = (((1,), (0,)), ((), ()))


def dot(a, b, dims=NN):
    return lax.dot_general(a, b, dims, preferred_element_type=F32)


def after(value, *others):
    return lax.optimization_barrier((value, *others))[0]


def forward_attention_kernel(chip_ref, q_ref, k_ref, vt_ref, o_ref, lse_ref):
    block = pl.program_id(0)
    chunks = WINDOW // QB
    key_row = lax.broadcasted_iota(jnp.int32, (QB, QB), 0)
    query_col = lax.broadcasted_iota(jnp.int32, (QB, QB), 1)

    def rows_of(chunk):
        return pl.ds(pl.multiple_of((block + chunk) * QB, QB), QB)

    def finish(head, top, total, mixed):
        cols = slice(head * HD, (head + 1) * HD)
        o_ref[:, cols] = jnp.transpose(mixed / total).astype(BF)
        lse_ref[head : head + 1, :] = top + jnp.log(total) * LOG2E

    @pl.when(chip_ref[0] != 0)
    def _():
        for head in range(GROUP):
            query = q_ref[:, head * HD : (head + 1) * HD]
            scores = []
            for chunk in range(chunks + 1):
                part = dot(k_ref[rows_of(chunk), :], query, NT)
                if chunk == 0:
                    part = jnp.where(key_row > query_col, part, NEG)
                if chunk == chunks:
                    part = jnp.where(key_row <= query_col, part, NEG)
                scores.append(part)
            top = jnp.max(functools.reduce(jnp.maximum, scores), axis=0, keepdims=True)
            total = jnp.zeros((1, QB), F32)
            mixed = jnp.zeros((HD, QB), F32)
            for chunk in range(chunks + 1):
                probs = jnp.exp2(scores[chunk] - top)
                total = total + jnp.sum(probs, axis=0, keepdims=True)
                mixed = mixed + dot(vt_ref[:, rows_of(chunk)], probs.astype(BF))
            finish(head, top, total, mixed)

    @pl.when(chip_ref[0] == 0)
    def _():
        for head in range(GROUP):
            query = q_ref[:, head * HD : (head + 1) * HD]

            def step(chunk, carry):
                top, total, mixed = carry
                part = dot(k_ref[rows_of(chunk), :], query, NT)
                part = jnp.where((key_row <= query_col) | (chunk < chunks), part, NEG)
                new_top = jnp.maximum(top, jnp.max(part, axis=0, keepdims=True))
                shrink = jnp.exp2(top - new_top)
                probs = jnp.exp2(part - new_top)
                total = total * shrink + jnp.sum(probs, axis=0, keepdims=True)
                mixed = mixed * shrink + dot(vt_ref[:, rows_of(chunk)], probs.astype(BF))
                return (new_top, total, mixed)

            first = (jnp.full((1, QB), NEG, F32), jnp.zeros((1, QB), F32), jnp.zeros((HD, QB), F32))
            top, total, mixed = lax.fori_loop(chunks - block, chunks + 1, step, first)
            finish(head, top, total, mixed)


def forward_attention(chip, query, keys, values_t):
    rows = query.shape[0]
    width = GROUP * HD
    return pl.pallas_call(
        forward_attention_kernel,
        grid_spec=pltpu.PrefetchScalarGridSpec(
            num_scalar_prefetch=1,
            grid=(rows // QB,),
            in_specs=[
                pl.BlockSpec((QB, width), lambda b, s: (b, 0)),
                pl.BlockSpec((2 * rows, HD), lambda b, s: (0, 0)),
                pl.BlockSpec((HD, 2 * rows), lambda b, s: (0, 0)),
            ],
            out_specs=[
                pl.BlockSpec((QB, width), lambda b, s: (b, 0)),
                pl.BlockSpec((8, QB), lambda b, s: (0, b)),
            ],
        ),
        out_shape=(
            jax.ShapeDtypeStruct((rows, width), BF),
            jax.ShapeDtypeStruct((8, rows), F32),
        ),
        compiler_params=pltpu.CompilerParams(vmem_limit_bytes=40 << 20),
        cost_estimate=pl.CostEstimate(
            flops=9_000_000_000, transcendentals=4_000_000, bytes_accessed=4_000_000
        ),
        name="attention_forward",
    )(chip, query, keys, values_t)


def backward_attention_kernel(
    chip_ref, q_ref, g_ref, o_ref, lse_ref, k_ref, kt_ref, v_ref, dq_ref, dk_ref, dv_ref
):
    block = pl.program_id(0)
    chunks = WINDOW // QB
    key_row = lax.broadcasted_iota(jnp.int32, (QB, QB), 0)
    query_col = lax.broadcasted_iota(jnp.int32, (QB, QB), 1)

    @pl.when(block == 0)
    def _():
        dk_ref[...] = jnp.zeros_like(dk_ref)
        dv_ref[...] = jnp.zeros_like(dv_ref)

    def rows_of(chunk):
        return pl.ds(pl.multiple_of((block + chunk) * QB, QB), QB)

    deltas = []
    for head in range(GROUP):
        cols = slice(head * HD, (head + 1) * HD)
        both = g_ref[:, cols].astype(F32) * o_ref[:, cols].astype(F32)
        deltas.append(jnp.sum(jnp.transpose(both), axis=0, keepdims=True))

    def one_chunk(chunk, keep, totals):
        rows = rows_of(chunk)
        keys = k_ref[rows, :]
        values = v_ref[rows, :]
        keys_t = kt_ref[:, rows]
        grad_keys = jnp.zeros((QB, HD), F32)
        grad_values = jnp.zeros((QB, HD), F32)
        new = []
        for head in range(GROUP):
            cols = slice(head * HD, (head + 1) * HD)
            query = q_ref[:, cols]
            grad = g_ref[:, cols]
            probs = jnp.exp2(dot(keys, query, NT) - lse_ref[head : head + 1, :])
            if keep is not None:
                probs = jnp.where(keep, probs, 0.0)
            grad_scores = (probs * (dot(values, grad, NT) - deltas[head])).astype(BF)
            grad_values = grad_values + dot(probs.astype(BF), grad)
            grad_keys = grad_keys + dot(grad_scores, query)
            new.append(totals[head] + dot(keys_t, grad_scores))
        dk_ref[rows, :] += grad_keys
        dv_ref[rows, :] += grad_values
        return tuple(new)

    def finish(totals):
        for head in range(GROUP):
            cols = slice(head * HD, (head + 1) * HD)
            dq_ref[:, cols] = (jnp.transpose(totals[head]) * HD ** (-0.5)).astype(BF)

    zeros = tuple(jnp.zeros((HD, QB), F32) for _ in range(GROUP))

    @pl.when(chip_ref[0] != 0)
    def _():
        totals = zeros
        for chunk in range(chunks + 1):
            keep = None
            if chunk == 0:
                keep = key_row > query_col
            if chunk == chunks:
                keep = key_row <= query_col
            totals = one_chunk(chunk, keep, totals)
        finish(totals)

    @pl.when(chip_ref[0] == 0)
    def _():
        def step(chunk, totals):
            return one_chunk(chunk, (key_row <= query_col) | (chunk < chunks), totals)

        finish(lax.fori_loop(chunks - block, chunks + 1, step, zeros))


def backward_attention(chip, query, grad, mixed, lse, keys, keys_t, values):
    rows = query.shape[0]
    width = GROUP * HD
    wide = pl.BlockSpec((QB, width), lambda b, s: (b, 0))
    whole = pl.BlockSpec((2 * rows, HD), lambda b, s: (0, 0))
    return pl.pallas_call(
        backward_attention_kernel,
        grid_spec=pltpu.PrefetchScalarGridSpec(
            num_scalar_prefetch=1,
            grid=(rows // QB,),
            in_specs=[
                wide,
                wide,
                wide,
                pl.BlockSpec((8, QB), lambda b, s: (0, b)),
                whole,
                pl.BlockSpec((HD, 2 * rows), lambda b, s: (0, 0)),
                whole,
            ],
            out_specs=[wide, whole, whole],
        ),
        out_shape=(
            jax.ShapeDtypeStruct((rows, width), BF),
            jax.ShapeDtypeStruct((2 * rows, HD), F32),
            jax.ShapeDtypeStruct((2 * rows, HD), F32),
        ),
        compiler_params=pltpu.CompilerParams(vmem_limit_bytes=40 << 20),
        cost_estimate=pl.CostEstimate(
            flops=18_000_000_000, transcendentals=4_000_000, bytes_accessed=8_000_000
        ),
        name="attention_backward",
    )(chip, query, grad, mixed, lse, keys, keys_t, values)


def assemble_kernel(count, place_ref, *refs):
    pieces, whole = refs[:count], refs[count]
    depth = pieces[0].shape[0]
    for i in range(count):
        whole[pl.ds(pl.multiple_of(place_ref[i] * depth, depth), depth), :] = pieces[i][...]


def assemble(places, pieces):
    count = len(pieces)
    depth, width = pieces[0].shape
    piece = pl.BlockSpec((depth, width), lambda i, s: (0, 0), pipeline_mode=pl.Buffered(1))
    return pl.pallas_call(
        functools.partial(assemble_kernel, count),
        grid_spec=pltpu.PrefetchScalarGridSpec(
            num_scalar_prefetch=1,
            grid=(1,),
            in_specs=[piece] * count,
            out_specs=pl.BlockSpec((count * depth, width), lambda i, s: (0, 0)),
        ),
        out_shape=jax.ShapeDtypeStruct((count * depth, width), pieces[0].dtype),
        compiler_params=pltpu.CompilerParams(vmem_limit_bytes=24 << 20),
        cost_estimate=pl.CostEstimate(
            flops=0, transcendentals=0, bytes_accessed=4 * count * depth * width
        ),
        name="assemble_pieces",
    )(places, *pieces)


def pack_kernel(*refs):
    packed = refs[-1]
    depth, width = refs[0].shape[0], packed.shape[1]
    for i, piece in enumerate(refs[:-1]):
        packed[pl.ds(i * depth, depth), :] = piece[:, :width]


def pack(pieces, width):
    depth = pieces[0].shape[0]
    rows = depth * len(pieces)
    return pl.pallas_call(
        pack_kernel,
        grid=(1,),
        in_specs=[pl.BlockSpec(piece.shape, lambda i: (0, 0)) for piece in pieces],
        out_specs=pl.BlockSpec((rows, width), lambda i: (0, 0)),
        out_shape=jax.ShapeDtypeStruct((rows, width), BF),
        compiler_params=pltpu.CompilerParams(vmem_limit_bytes=16 << 20),
        cost_estimate=pl.CostEstimate(flops=0, transcendentals=0, bytes_accessed=4 * rows * width),
        name="pack_pieces",
    )(*pieces)


def unpack_kernel(half, place_ref, far, near, whole):
    depth = far.shape[0] // half
    for i in range(half):
        rows = pl.ds(i * depth, depth)
        whole[pl.ds(pl.multiple_of(place_ref[i] * depth, depth), depth), :] = far[rows, :]
        whole[pl.ds(pl.multiple_of(place_ref[half + i] * depth, depth), depth), :] = near[rows, :]


def unpack(places, far, near, half):
    rows, width = far.shape
    packed = pl.BlockSpec((rows, width), lambda i, s: (0, 0))
    return pl.pallas_call(
        functools.partial(unpack_kernel, half),
        grid_spec=pltpu.PrefetchScalarGridSpec(
            num_scalar_prefetch=1,
            grid=(1,),
            in_specs=[packed, packed],
            out_specs=pl.BlockSpec((2 * rows, width), lambda i, s: (0, 0)),
        ),
        out_shape=jax.ShapeDtypeStruct((2 * rows, width), BF),
        compiler_params=pltpu.CompilerParams(vmem_limit_bytes=16 << 20),
        cost_estimate=pl.CostEstimate(flops=0, transcendentals=0, bytes_accessed=8 * rows * width),
        name="unpack_pieces",
    )(places, far, near)


def split_kernel(groups, half, place_ref, whole, *refs):
    depth = refs[0].shape[0] // len(groups[0])
    for group, kept, sent in zip(groups, refs[: len(groups)], refs[len(groups) :]):
        for at, i in enumerate(group):
            rows = pl.ds(at * depth, depth)
            kept[rows, :] = whole[pl.ds(pl.multiple_of(place_ref[i] * depth, depth), depth), :]
            sent[rows, :] = whole[
                pl.ds(pl.multiple_of(place_ref[half + i] * depth, depth), depth), :
            ]


def split(places, whole, half, parts=1):
    size = half // parts
    groups = [range(half - (p + 1) * size, half - p * size) for p in range(parts)]
    rows, width = whole.shape[0] // (2 * parts), whole.shape[1]
    out = pl.BlockSpec((rows, width), lambda i, s: (0, 0))
    pieces = pl.pallas_call(
        functools.partial(split_kernel, groups, half),
        grid_spec=pltpu.PrefetchScalarGridSpec(
            num_scalar_prefetch=1,
            grid=(1,),
            in_specs=[pl.BlockSpec(whole.shape, lambda i, s: (0, 0))],
            out_specs=[out] * (2 * parts),
        ),
        out_shape=(jax.ShapeDtypeStruct((rows, width), whole.dtype),) * (2 * parts),
        compiler_params=pltpu.CompilerParams(vmem_limit_bytes=24 << 20),
        cost_estimate=pl.CostEstimate(
            flops=0, transcendentals=0, bytes_accessed=8 * parts * rows * width
        ),
        name="split_pieces",
    )(places, whole)
    return pieces[:parts], pieces[parts:]


def fold_kernel(kept, came, *pieces):
    depth = pieces[0].shape[0]
    for i, piece in enumerate(pieces):
        rows = pl.ds(i * depth, depth)
        piece[...] = (kept[rows, :].astype(F32) + came[rows, :].astype(F32)).astype(BF)


def fold(kept, came, half):
    rows, width = kept.shape
    depth = rows // half
    whole = pl.BlockSpec((rows, width), lambda i: (0, 0))
    return pl.pallas_call(
        fold_kernel,
        grid=(1,),
        in_specs=[whole, whole],
        out_specs=[pl.BlockSpec((depth, width), lambda i: (0, 0))] * half,
        out_shape=(jax.ShapeDtypeStruct((depth, width), BF),) * half,
        compiler_params=pltpu.CompilerParams(vmem_limit_bytes=24 << 20),
        cost_estimate=pl.CostEstimate(
            flops=0, transcendentals=0, bytes_accessed=6 * rows * width
        ),
        name="fold_pieces",
    )(kept, came)


def gelu_parts(gate):
    square = gate * gate
    t = jnp.tanh(gate * (0.7978845608028654 + 0.035677408136300125 * square))
    half = 0.5 + 0.5 * t
    value = gate * half
    slope = half + 0.5 * gate * (1.0 - t * t) * (0.7978845608028654 + 0.10703222440890037 * square)
    return value, slope


def bring(count, place_ref, pieces, whole, sems, out):
    depth, wide = pieces[0].shape
    copies = [
        pltpu.make_async_copy(
            piece,
            whole.at[
                pl.ds(pl.multiple_of(place_ref[i % count] * depth, depth), depth),
                pl.ds(i // count * wide, wide),
            ],
            sems.at[i],
        )
        for i, piece in enumerate(pieces)
    ]
    save = pltpu.make_async_copy(whole, out, sems.at[len(pieces)])

    @pl.when(pl.program_id(0) == 0)
    def _():
        for copy in copies:
            copy.start()
        for copy in copies:
            copy.wait()
        save.start()

    return save


def gate_up_block(norm_ref, whole, product_ref, to_gate_ref, to_up_ref):
    hidden = product_ref.shape[1]
    step = 384
    for start in range(0, hidden, step):
        cols = slice(start, start + step)
        gate = dot(norm_ref[...], whole[:, cols])
        up = dot(norm_ref[...], whole[:, hidden + start : hidden + start + step])
        value, slope = gelu_parts(gate)
        product_ref[:, cols] = (value * up).astype(BF)
        to_gate_ref[:, cols] = (up * slope).astype(BF)
        to_up_ref[:, cols] = value.astype(BF)


def gate_up_first_kernel(count, place_ref, norm_ref, *refs):
    pieces = refs[: 2 * count]
    product_ref, to_gate_ref, to_up_ref, out, whole, sems = refs[2 * count :]
    save = bring(count, place_ref, pieces, whole, sems, out)
    gate_up_block(norm_ref, whole, product_ref, to_gate_ref, to_up_ref)

    @pl.when(pl.program_id(0) == pl.num_programs(0) - 1)
    def _():
        save.wait()


def gate_up_first(norm, places, gate_pieces, up_pieces):
    rows, width = norm.shape
    count = len(gate_pieces)
    hidden = gate_pieces[0].shape[1]
    block = 256
    out = pl.BlockSpec((block, hidden), lambda i, s: (i, 0))
    anywhere = pl.BlockSpec(memory_space=pl.ANY)
    return pl.pallas_call(
        functools.partial(gate_up_first_kernel, count),
        grid_spec=pltpu.PrefetchScalarGridSpec(
            num_scalar_prefetch=1,
            grid=(rows // block,),
            in_specs=[pl.BlockSpec((block, width), lambda i, s: (i, 0))] + [anywhere] * (2 * count),
            out_specs=[out, out, out, anywhere],
            scratch_shapes=[
                pltpu.VMEM((width, 2 * hidden), BF),
                pltpu.SemaphoreType.DMA((2 * count + 1,)),
            ],
        ),
        out_shape=(jax.ShapeDtypeStruct((2 * rows, hidden), BF),) * 3
        + (jax.ShapeDtypeStruct((width, 2 * hidden), BF),),
        compiler_params=pltpu.CompilerParams(vmem_limit_bytes=36 << 20),
        cost_estimate=pl.CostEstimate(
            flops=4 * rows * width * hidden,
            transcendentals=rows * hidden,
            bytes_accessed=2 * rows * width + 6 * rows * hidden + 8 * width * hidden,
        ),
        name="gate_up_first",
    )(places, norm, *gate_pieces, *up_pieces)


def gate_up_rest_kernel(norm_ref, whole_ref, a, b, c, product_ref, to_gate_ref, to_up_ref):
    del a, b, c
    gate_up_block(norm_ref, whole_ref, product_ref, to_gate_ref, to_up_ref)


def gate_up_rest(norm, gate_up, *earlier):
    rows, width = norm.shape
    hidden = gate_up.shape[1] // 2
    block = 256
    steps = rows // block
    out = pl.BlockSpec((block, hidden), lambda i: (i + steps, 0))
    anywhere = pl.BlockSpec(memory_space=pl.ANY)
    return pl.pallas_call(
        gate_up_rest_kernel,
        grid=(steps,),
        in_specs=[
            pl.BlockSpec((block, width), lambda i: (i, 0)),
            pl.BlockSpec(gate_up.shape, lambda i: (0, 0), pipeline_mode=pl.Buffered(1)),
            anywhere,
            anywhere,
            anywhere,
        ],
        out_specs=[out, out, out],
        out_shape=(jax.ShapeDtypeStruct((2 * rows, hidden), BF),) * 3,
        input_output_aliases={2: 0, 3: 1, 4: 2},
        compiler_params=pltpu.CompilerParams(vmem_limit_bytes=36 << 20),
        cost_estimate=pl.CostEstimate(
            flops=4 * rows * width * hidden,
            transcendentals=rows * hidden,
            bytes_accessed=2 * rows * width + 6 * rows * hidden + 4 * width * hidden,
        ),
        name="gate_up_rest",
    )(norm, gate_up, *earlier)


def product_gradient_kernel(count, place_ref, cot_ref, to_gate_ref, to_up_ref, *refs):
    pieces = refs[:count]
    dgate_ref, dup_ref, out, whole, sems = refs[count:]
    save = bring(count, place_ref, pieces, whole, sems, out)
    step = 384
    for start in range(0, whole.shape[1], step):
        cols = slice(start, start + step)
        grad = dot(cot_ref[...], whole[:, cols])
        dgate_ref[:, cols] = (grad * to_gate_ref[:, cols].astype(F32)).astype(BF)
        dup_ref[:, cols] = (grad * to_up_ref[:, cols].astype(F32)).astype(BF)

    @pl.when(pl.program_id(0) == pl.num_programs(0) - 1)
    def _():
        save.wait()


def product_gradient(cot, to_gate, to_up, places, pieces):
    rows, width = cot.shape
    count = len(pieces)
    hidden = to_gate.shape[1]
    block = 256
    part = pl.BlockSpec((block, hidden), lambda i, s: (i, 0))
    anywhere = pl.BlockSpec(memory_space=pl.ANY)
    return pl.pallas_call(
        functools.partial(product_gradient_kernel, count),
        grid_spec=pltpu.PrefetchScalarGridSpec(
            num_scalar_prefetch=1,
            grid=(rows // block,),
            in_specs=[pl.BlockSpec((block, width), lambda i, s: (i, 0)), part, part]
            + [anywhere] * count,
            out_specs=[part, part, anywhere],
            scratch_shapes=[
                pltpu.VMEM((width, hidden), BF),
                pltpu.SemaphoreType.DMA((count + 1,)),
            ],
        ),
        out_shape=(jax.ShapeDtypeStruct((rows, hidden), BF),) * 2
        + (jax.ShapeDtypeStruct((width, hidden), BF),),
        compiler_params=pltpu.CompilerParams(vmem_limit_bytes=32 << 20),
        cost_estimate=pl.CostEstimate(
            flops=2 * rows * width * hidden,
            transcendentals=0,
            bytes_accessed=2 * rows * width + 8 * rows * hidden + 4 * width * hidden,
        ),
        name="product_gradient",
    )(places, cot, to_gate, to_up, *pieces)


def feed_back_kernel(dgate_ref, dup_ref, gate_up_ref, kept_ref, sent_ref):
    hidden = dgate_ref.shape[1]
    total = dot(dgate_ref[...], gate_up_ref[:, :hidden], NT)
    total = (total + dot(dup_ref[...], gate_up_ref[:, hidden:], NT)).astype(BF)

    @pl.when(pl.program_id(0) < pl.num_programs(0) // 2)
    def _():
        kept_ref[...] = total

    @pl.when(pl.program_id(0) >= pl.num_programs(0) // 2)
    def _():
        sent_ref[...] = total


def feed_back(first, rows, dgate, dup, gate_up):
    width, hidden = gate_up.shape[0], dgate.shape[1]
    block = 256
    steps = rows // block
    skip = first // block
    part = pl.BlockSpec((block, hidden), lambda i: (i + skip, 0))
    return pl.pallas_call(
        feed_back_kernel,
        grid=(steps,),
        in_specs=[
            part,
            part,
            pl.BlockSpec(gate_up.shape, lambda i: (0, 0), pipeline_mode=pl.Buffered(1)),
        ],
        out_specs=[
            pl.BlockSpec((block, width), lambda i: (jnp.minimum(i, steps // 2 - 1), 0)),
            pl.BlockSpec((block, width), lambda i: (jnp.maximum(i - steps // 2, 0), 0)),
        ],
        out_shape=(jax.ShapeDtypeStruct((rows // 2, width), BF),) * 2,
        compiler_params=pltpu.CompilerParams(vmem_limit_bytes=36 << 20),
        cost_estimate=pl.CostEstimate(
            flops=4 * rows * width * hidden,
            transcendentals=0,
            bytes_accessed=2 * rows * width + 4 * rows * hidden + 4 * width * hidden,
        ),
        name="feed_back",
    )(dgate, dup, gate_up)


class Shards:
    def __init__(self, count):
        self.count = count
        self.half = count // 2
        index = lax.axis_index("shard").astype(jnp.int32)
        hi, lo = index // 2, index % 2
        mine = [(hi ^ k) * 2 + lo for k in range(self.half)]
        partner = [(hi ^ k) * 2 + (1 - lo) for k in range(self.half)]
        self.places = jnp.stack(mine + partner)

    def far(self, value, k):
        return lax.ppermute(
            value, "shard", [(i, ((i // 2) ^ k) * 2 + i % 2) for i in range(self.count)]
        )

    def near(self, value):
        return lax.ppermute(value, "shard", [(i, i ^ 1) for i in range(self.count)])

    def whole(self, pieces):
        return assemble(self.places, pieces)


def tp_swap(value, mask):
    return lax.ppermute(value, "tp", [(i, i ^ mask) for i in range(4)])


def local(count, tokens, w_query, w_keyval, w_out, w_gate, w_up, w_down, gain_attn, gain_mlp, cotangent):
    rows, width = tokens.shape[0], tokens.shape[2]
    tp = lax.axis_index("tp").astype(jnp.int32)
    core, chip = tp % 2, tp // 2
    first_core = core == 0
    chip_table = jnp.reshape(chip, (1,))
    shards = Shards(count)

    def in_order(own, other):
        return jnp.where(
            first_core, jnp.concatenate([own, other], 0), jnp.concatenate([other, own], 0)
        )

    gain_one = gain_attn.astype(BF).astype(F32)[:, None]
    gain_two = gain_mlp.astype(BF).astype(F32)[:, None]
    own_query = w_query.astype(BF).astype(F32)
    own_keyval = w_keyval.astype(BF).astype(F32)
    own_gate = w_gate.astype(BF).astype(F32)
    own_up = w_up.astype(BF).astype(F32)
    keyval_half = jnp.where(first_core, own_keyval[:, :HD], own_keyval[:, HD:])
    send_in = (jnp.concatenate([own_query, keyval_half], 1) * gain_one).astype(BF)
    send_out = jnp.transpose(w_out).astype(BF)
    send_gate = (own_gate * gain_two).astype(BF)
    send_up = (own_up * gain_two).astype(BF)
    send_down = jnp.transpose(w_down).astype(BF)

    heads = GROUP * HD
    half_count = shards.half
    places = shards.places
    most, part = range(1, half_count - 1), half_count // 2
    token = places

    def sync(*values):
        nonlocal token
        token, *values = lax.optimization_barrier((token, *values))
        return values

    def far_most(piece):
        return [shards.far(piece, k) for k in most]

    def far_last(piece):
        return [shards.far(piece, half_count - 1)]

    def near(pieces):
        return [shards.near(piece) for piece in pieces]

    def rows_of(value, other):
        return lax.dynamic_slice_in_dim(value, (core ^ other) * rows, rows, 0)

    inputs = tokens.reshape(rows, width).astype(F32)
    scale_one = lax.rsqrt(jnp.mean(inputs * inputs, axis=-1, keepdims=True) + EPS)
    unit_own = (inputs * scale_one).astype(BF)
    far_in = far_most(send_in) + far_last(send_in)
    unit_other = tp_swap(unit_own, 1)
    cot = cotangent.reshape(4, rows, width)
    cots = [lax.dynamic_index_in_dim(cot, tp ^ k, 0, keepdims=False) for k in range(4)]
    cot_all = jnp.concatenate(cots, 0)
    send_in, cot_all, send_out, unit_other, *far_in = sync(
        send_in, cot_all, send_out, unit_other, *far_in
    )

    far_in = [send_in] + far_in
    near_in = near(far_in)
    far_out = far_most(send_out) + far_last(send_out)
    query_far_b = tp_swap(pack(far_in, heads), 2)
    unit = in_order(unit_own, unit_other)
    unit, query_far_b, send_gate, send_up, *pieces = sync(
        unit, query_far_b, send_gate, send_up, *far_in, *near_in, *far_out
    )
    far_in, near_in, far_out = (
        pieces[:half_count],
        pieces[half_count : 2 * half_count],
        [send_out] + pieces[2 * half_count :],
    )

    in_full = shards.whole(far_in + near_in)
    in_query = in_full[:, :heads]
    scale = HD ** (-0.5)
    column = lax.broadcasted_iota(jnp.int32, (1, in_full.shape[1]), 1)
    query_half = (
        dot(unit, in_full) * jnp.where(column < heads, scale * LOG2E, 1.0)
    ).astype(BF)
    half = query_half[:, heads:]
    half_other = tp_swap(half, 1)
    before = lax.ppermute(half, "tp", [(0, 2), (1, 3)])
    before_other = tp_swap(before, 1)
    query_near_b = tp_swap(after(pack(near_in, heads), half), 2)
    near_out = near(far_out)
    far_gate = far_most(send_gate)
    own_pair = jnp.concatenate([before, half], 0)
    other_pair = jnp.concatenate([before_other, half_other], 0)
    keys = jnp.where(first_core, own_pair, other_pair)
    values = jnp.where(first_core, other_pair, own_pair)
    query_half, keys, values, query_near_b, send_gate, *pieces = sync(
        query_half, keys, values, query_near_b, send_gate, *near_out, *far_gate
    )
    near_out, far_gate = pieces[:half_count], [send_gate] + pieces[half_count:]

    keys_t = jnp.transpose(keys)
    values_t = jnp.transpose(values)
    far_gate += far_last(send_gate)
    near_gate = near(far_gate[:part])
    out_far_b = tp_swap(pack(far_out, heads), 2)
    mixed_a, lse_a = forward_attention(chip_table, query_half, keys, values_t)
    in_query_b = unpack(places, query_far_b, query_near_b, half_count)
    query_b = (dot(unit, in_query_b) * (scale * LOG2E)).astype(BF)
    out_full = shards.whole(far_out + near_out)
    mixed_a, query_b, out_far_b, send_up, *pieces = sync(
        mixed_a, query_b, out_far_b, send_up, *far_gate[1:], *near_gate
    )
    far_gate, near_gate = [send_gate] + pieces[: half_count - 1], pieces[half_count - 1 :]

    far_up = far_most(send_up)
    near_gate += near(far_gate[part:])
    out_near_b = tp_swap(pack(near_out, heads), 2)
    mixed_b, lse_b = forward_attention(chip_table, query_b, keys, values_t)
    branch_other = dot(rows_of(mixed_a, 1), out_full, NT)
    branch_own = dot(rows_of(mixed_a, 0), out_full, NT)
    mixed_b, out_near_b, branch_other, branch_own, send_up, *pieces = sync(
        mixed_b, out_near_b, branch_other, branch_own, send_up, *far_up, *near_gate
    )
    far_up, near_gate = [send_up] + pieces[: len(most)], pieces[len(most) :]

    far_up += far_last(send_up)
    near_up = near(far_up[:part])
    out_full_b = unpack(places, out_far_b, out_near_b, half_count)
    branch_other = (branch_other + dot(rows_of(mixed_b, 1), out_full_b, NT)).astype(BF)
    branch_came = tp_swap(branch_other, 1)
    branch_own = branch_own + dot(rows_of(mixed_b, 0), out_full_b, NT)
    hidden = inputs + (branch_own + branch_came.astype(F32))
    scale_two = lax.rsqrt(jnp.mean(hidden * hidden, axis=-1, keepdims=True) + EPS)
    norm_own = (hidden * scale_two).astype(BF)
    norm_own, send_down, *pieces = sync(norm_own, send_down, *far_up[1:], *near_up)
    far_up, near_up = [send_up] + pieces[: half_count - 1], pieces[half_count - 1 :]

    cut = rows // 16 * 9
    far_down = far_most(send_down)
    near_up += near(far_up[part:])
    norm_core = tp_swap(norm_own, 1)
    norm_x1 = tp_swap(norm_own[:cut], 2)
    norm_near = jnp.concatenate([norm_own, norm_core], 0)
    norm_near, norm_x1, send_down, *pieces = sync(
        norm_near, norm_x1, send_down, *far_down, *near_up
    )
    far_down, near_up = [send_down] + pieces[: len(most)], pieces[len(most) :]

    far_down += far_last(send_down)
    near_down = near(far_down[:part])
    norm_x2 = tp_swap(norm_own[cut:], 2)
    norm_d1 = tp_swap(norm_x1, 1)
    product, to_gate, to_up, gate_up_full = gate_up_first(
        norm_near, places, far_gate + near_gate, far_up + near_up
    )
    norm_x2, norm_d1, product, to_gate, to_up, *pieces = sync(
        norm_x2, norm_d1, product, to_gate, to_up, *far_down[1:], *near_down
    )
    far_down, near_down = [send_down] + pieces[: half_count - 1], pieces[half_count - 1 :]

    near_down += near(far_down[part:])
    norm_d2 = tp_swap(norm_x2, 1)
    norm_far = jnp.concatenate([norm_x1, norm_x2, norm_d1, norm_d2], 0)
    product, to_gate, to_up = gate_up_rest(norm_far, gate_up_full, product, to_gate, to_up)
    norm_all = jnp.concatenate([norm_near, norm_far], 0)
    g_down = dot(cot_all, product, TN).astype(BF)
    kept_down, sent_down = split(places, g_down, half_count, 2)
    cot_all, sent, *near_down = sync(cot_all, sent_down[0], *near_down)

    came = shards.near(sent)
    dgate, dup, down_full = product_gradient(
        cot_all, to_gate, to_up, places, far_down + near_down
    )
    came_down = [came]
    dgate, sent, *came_down = sync(dgate, sent_down[1], *came_down)

    came_down.append(shards.near(sent))
    back_x, back_diagonal = feed_back(2 * rows, 2 * rows, dgate, dup, gate_up_full)
    sums_down = list(fold(kept_down[0], came_down[0], part))
    back_diagonal = tp_swap(back_diagonal, 1)
    back_far = [
        (a.astype(F32) + b.astype(F32)).astype(BF)
        for a, b in (
            (back_x[:cut], back_diagonal[:cut]),
            (back_x[cut:], back_diagonal[cut:]),
        )
    ]
    dgate, *pieces = sync(dgate, *back_far, came_down[1], *sums_down)
    back_far, came_down[1], sums_down = pieces[:2], pieces[2], pieces[3:]

    back_came = [tp_swap(back_far[0], 2)]
    far_sums = [shards.far(sums_down[0], part)]
    sums_down = list(fold(kept_down[1], came_down[1], part)) + sums_down
    g_gate = dot(norm_all, dgate, TN).astype(BF)
    kept_gate, sent_gate = split(places, g_gate, half_count, 2)
    product_down = product
    down_x = dot(product_down[2 * rows : 3 * rows], down_full, NT).astype(BF)
    down_diagonal = dot(product_down[3 * rows :], down_full, NT).astype(BF)
    dup, back_far[1], sent, down_diagonal, *pieces = sync(
        dup, back_far[1], sent_gate[0], down_diagonal, *back_came, *far_sums, *sums_down
    )
    back_came, far_sums, sums_down = [pieces[0]], [pieces[1]], pieces[2:]

    back_came.append(tp_swap(back_far[1], 2))
    came_gate = [shards.near(sent)]
    others = [k for k in range(1, half_count) if k != part]
    far_sums += [shards.far(sums_down[k], k) for k in others]
    down_diagonal = tp_swap(down_diagonal, 1)
    g_up = dot(norm_all, dup, TN).astype(BF)
    kept_up, sent_up = split(places, g_up, half_count, 2)
    down_far = (down_x.astype(F32) + down_diagonal.astype(F32)).astype(BF)
    dgate, sent, down_far, *pieces = sync(
        dgate, sent_gate[1], down_far, *back_came, *came_gate, *far_sums
    )
    back_came, came_gate, far_sums_down = pieces[:2], [pieces[2]], pieces[3:]

    came_gate.append(shards.near(sent))
    down_came = [tp_swap(down_far[:cut], 2)]
    back_own, back_core = feed_back(0, 2 * rows, dgate, dup, gate_up_full)
    back_core = tp_swap(back_core, 1)
    sums_gate = list(fold(kept_gate[0], came_gate[0], part))
    back_own, back_core, sent, *pieces = sync(
        back_own, back_core, sent_up[0], *down_came, came_gate[1], *sums_gate
    )
    down_came, came_gate[1], sums_gate = [pieces[0]], pieces[1], pieces[2:]

    came_up = [shards.near(sent)]
    far_sums = [shards.far(sums_gate[0], part)]
    sums_gate = list(fold(kept_gate[1], came_gate[1], part)) + sums_gate
    grad_norm = (
        back_own.astype(F32)
        + back_core.astype(F32)
        + jnp.concatenate(back_came, 0).astype(F32)
    )
    unit_two = hidden * scale_two
    grad_hidden = cots[0].astype(F32) + scale_two * (
        grad_norm - unit_two * jnp.mean(grad_norm * unit_two, axis=-1, keepdims=True)
    )
    branch_own = grad_hidden.astype(BF)
    branch_other = tp_swap(branch_own, 1)
    g_out_b = dot(branch_own, rows_of(mixed_b, 0), TN)
    grad_own = dot(branch_own, out_full_b).astype(BF)
    branch_other = after(branch_other, g_out_b, grad_own)
    g_out_b = (g_out_b + dot(branch_other, rows_of(mixed_b, 1), TN)).astype(BF)
    g_out_came = tp_swap(g_out_b, 2)
    grad_mixed_b = in_order(grad_own, dot(branch_other, out_full_b).astype(BF))
    grad_mixed_b, sent, *pieces = sync(
        grad_mixed_b, sent_up[1], *came_up, *far_sums, *sums_gate
    )
    came_up, far_sums, sums_gate = [pieces[0]], [pieces[1]], pieces[2:]

    came_up.append(shards.near(sent))
    far_sums += [shards.far(sums_gate[k], k) for k in others]
    sums_up = list(fold(kept_up[0], came_up[0], part))
    dq_b, dk_b, dv_b = backward_attention(
        chip_table, query_b, grad_mixed_b, mixed_b, lse_b, keys, keys_t, values
    )
    g_query_b = dot(unit, dq_b, TN).astype(BF)
    dq_b, g_query_b, g_out_came, *pieces = sync(
        dq_b, g_query_b, g_out_came, came_up[1], *far_sums, *sums_up
    )
    came_up[1], far_sums_gate, sums_up = (
        pieces[0],
        pieces[1:half_count],
        pieces[half_count:],
    )

    g_query_came = tp_swap(g_query_b, 2)
    far_sums = [shards.far(sums_up[0], part)]
    sums_up = list(fold(kept_up[1], came_up[1], part)) + sums_up
    g_out = (
        dot(branch_own, rows_of(mixed_a, 0), TN)
        + dot(branch_other, rows_of(mixed_a, 1), TN)
        + g_out_came.astype(F32)
    )
    (kept_out,), (sent_out,) = split(places, g_out.astype(BF), half_count)
    came_out = shards.near(sent_out)
    grad_mixed_a = in_order(
        dot(branch_own, out_full).astype(BF), dot(branch_other, out_full).astype(BF)
    )
    dq_a, dk_a, dv_a = backward_attention(
        chip_table, query_half, after(grad_mixed_a, sent_out), mixed_a, lse_a, keys, keys_t, values
    )
    dq_a, came_out, *pieces = sync(dq_a, came_out, *far_sums, *sums_up)
    far_sums, sums_up = [pieces[0]], pieces[1:]

    grad_keys = (dk_a + dk_b) * LN2
    grad_values = dv_a + dv_b
    mine = jnp.where(first_core, grad_keys, grad_values)
    theirs = jnp.where(first_core, grad_values, grad_keys).astype(BF)
    mine = mine + tp_swap(theirs, 1).astype(F32)
    chip_rows = mine.shape[0] // 2
    g_query = (dot(unit, dq_a, TN) + g_query_came.astype(F32)).astype(BF)
    (kept_query,), (sent_query,) = split(places, g_query, half_count)
    earlier = lax.ppermute(mine[:chip_rows].astype(BF), "tp", [(2, 0), (3, 1)])
    grad_half = (mine[chip_rows:] + earlier.astype(F32)).astype(BF)
    came_query = shards.near(sent_query)
    far_sums += [shards.far(sums_up[k], k) for k in others]
    sums_out = fold(kept_out, came_out, half_count)
    dq_a1, dq_b1 = after(dq_a, sent_query), after(dq_b, sent_query)
    back_other = dot(rows_of(dq_a1, 1), in_query, NT) + dot(rows_of(dq_b1, 1), in_query_b, NT)
    back_own = dot(rows_of(dq_a1, 0), in_query, NT) + dot(rows_of(dq_b1, 0), in_query_b, NT)
    g_half = dot(unit, after(grad_half, back_own), TN).astype(BF)
    (kept_half,), (sent_half,) = split(places, g_half, half_count)
    back_other, back_own, grad_half, sent_half, came_query, *pieces = sync(
        back_other, back_own, grad_half, sent_half, came_query, *far_sums, *sums_out
    )
    far_sums_up, sums_out = pieces[: half_count - 1], pieces[half_count - 1 :]

    came_half = shards.near(sent_half)
    sums_query = fold(kept_query, came_query, half_count)
    far_query = [shards.far(sums_query[k], k) for k in range(1, half_count)]
    far_out_sums = [shards.far(sums_out[k], k) for k in range(1, half_count)]
    in_half = in_full[:, heads:]
    back_other = (back_other + dot(rows_of(grad_half, 1), in_half, NT)).astype(BF)
    back_came = tp_swap(back_other, 1)
    back_own = back_own + dot(rows_of(grad_half, 0), in_half, NT)
    down_came.append(tp_swap(down_far[cut:], 2))
    down_own = dot(after(product, back_own)[:rows], down_full, NT).astype(BF)
    down_core = dot(after(product, back_own)[rows : 2 * rows], down_full, NT).astype(BF)
    sums_half = fold(kept_half, after(came_half, back_own, *sums_query), half_count)
    far_half = [shards.far(sums_half[k], k) for k in range(1, half_count)]

    grad_unit = back_own + back_came.astype(F32)
    unit_one = inputs * scale_one
    grad_tokens = grad_hidden + scale_one * (
        grad_unit - unit_one * jnp.mean(grad_unit * unit_one, axis=-1, keepdims=True)
    )
    output = (
        hidden
        + down_own.astype(F32)
        + tp_swap(down_core, 1).astype(F32)
        + jnp.concatenate(down_came, 0).astype(F32)
    ).astype(BF)

    def total(own, others):
        return functools.reduce(lambda t, o: t + o.astype(F32), others, own.astype(F32))

    sum_gate = total(sums_gate[0], far_sums_gate)
    sum_up = total(sums_up[0], far_sums_up)
    grad_w_gate = sum_gate * gain_two
    grad_w_up = sum_up * gain_two
    gain_two_part = jnp.sum(own_gate * sum_gate + own_up * sum_up, axis=1)
    grad_w_down = jnp.transpose(total(sums_down[0], far_sums_down))
    grad_w_out = jnp.transpose(total(sums_out[0], far_out_sums))
    sum_query = total(sums_query[0], far_query)
    sum_half = total(sums_half[0], far_half)

    gain_one_part = jnp.sum(own_query * sum_query, axis=1) + jnp.sum(keyval_half * sum_half, axis=1)
    small = jnp.concatenate(
        [jnp.transpose(sum_half), gain_one_part[None], gain_two_part[None], jnp.zeros((6, sum_half.shape[0]), F32)], 0
    )
    small = small + tp_swap(small, 2)
    other = tp_swap(small, 1)
    gains = small[HD : HD + 2] + other[HD : HD + 2]
    sum_half = jnp.transpose(small[:HD])
    half_swapped = jnp.transpose(other[:HD])
    grad_w_keyval = (
        jnp.where(
            first_core,
            jnp.concatenate([sum_half, half_swapped], 1),
            jnp.concatenate([half_swapped, sum_half], 1),
        )
        * gain_one
    )
    return (
        output.reshape(rows, 1, width),
        grad_tokens.reshape(rows, 1, width),
        sum_query * gain_one,
        grad_w_keyval,
        grad_w_out,
        grad_w_gate,
        grad_w_up,
        grad_w_down,
        gains[0],
        gains[1],
    )


def solution(mesh):
    in_specs = (
        P("tp", "shard", None),
        P("shard", "tp"),
        P("shard", None),
        P("tp", "shard"),
        P("shard", "tp"),
        P("shard", "tp"),
        P("tp", "shard"),
        P("shard"),
        P("shard"),
        P(None, "shard", None),
    )
    out_specs = (
        P("tp", "shard", None),
        P("tp", "shard", None),
        P("shard", "tp"),
        P("shard", None),
        P("tp", "shard"),
        P("shard", "tp"),
        P("shard", "tp"),
        P("tp", "shard"),
        P("shard"),
        P("shard"),
    )
    return jax.shard_map(
        functools.partial(local, mesh.shape["shard"]),
        mesh=mesh,
        in_specs=in_specs,
        out_specs=out_specs,
        check_vma=False,
    )
```

```python
import functools

import jax
import jax.numpy as jnp
from jax import lax
from jax.experimental import pallas as pl
from jax.experimental.pallas import tpu as pltpu
from jax.sharding import PartitionSpec as P

HD = 128
WINDOW = 1024
QB = 256
GROUP = 3
EPS = 1e-06
LOG2E = 1.4426950408889634
LN2 = 0.6931471805599453
NEG = -1e30
LARGE = 1 << 20
SMALL = pl.CostEstimate(flops=0, transcendentals=0, bytes_accessed=0)
BF = jnp.bfloat16
F32 = jnp.float32
NT = (((1,), (1,)), ((), ()))
TN = (((0,), (0,)), ((), ()))
NN = (((1,), (0,)), ((), ()))


def dot(a, b, dims=NN):
    return lax.dot_general(a, b, dims, preferred_element_type=F32)


def after(value, *others):
    return lax.optimization_barrier((value, *others))[0]


def kernel_call(*args, **kwargs):
    call = pl.pallas_call(*args, **kwargs)

    def run(*operands):
        return call(
            *(
                pltpu.with_memory_space_constraint(x, pltpu.HBM) if x.size > LARGE else x
                for x in operands
            )
        )

    return run


def forward_attention_kernel(chip_ref, q_ref, k_ref, vt_ref, o_ref, lse_ref):
    block = pl.program_id(0)
    chunks = WINDOW // QB
    key_row = lax.broadcasted_iota(jnp.int32, (QB, QB), 0)
    query_col = lax.broadcasted_iota(jnp.int32, (QB, QB), 1)

    def rows_of(chunk):
        return pl.ds(pl.multiple_of((block + chunk) * QB, QB), QB)

    def finish(head, top, total, mixed):
        cols = slice(head * HD, (head + 1) * HD)
        o_ref[:, cols] = jnp.transpose(mixed / total).astype(BF)
        lse_ref[head : head + 1, :] = top + jnp.log(total) * LOG2E

    def attend(first):
        for head in range(GROUP):
            query = q_ref[:, head * HD : (head + 1) * HD]
            scores = {}
            for chunk in range(first, chunks + 1):
                scores[chunk] = dot(k_ref[rows_of(chunk), :], query, NT)
                if chunk == 0:
                    scores[chunk] = jnp.where(key_row > query_col, scores[chunk], NEG)
                if chunk == chunks:
                    scores[chunk] = jnp.where(key_row <= query_col, scores[chunk], NEG)
            top = functools.reduce(jnp.maximum, scores.values())
            top = jnp.max(top, axis=0, keepdims=True)
            total = jnp.zeros((1, QB), F32)
            mixed = jnp.zeros((HD, QB), F32)
            for chunk, part in scores.items():
                probs = jnp.exp2(part - top)
                total = total + jnp.sum(probs, axis=0, keepdims=True)
                mixed = mixed + dot(vt_ref[:, rows_of(chunk)], probs.astype(BF))
            finish(head, top, total, mixed)

    pl.when(chip_ref[0] != 0)(functools.partial(attend, 0))
    for at in range(chunks):
        pl.when((chip_ref[0] == 0) & (block == at))(functools.partial(attend, chunks - at))


def forward_attention(chip, query, keys, values_t):
    rows = query.shape[0]
    width = GROUP * HD
    return kernel_call(
        forward_attention_kernel,
        grid_spec=pltpu.PrefetchScalarGridSpec(
            num_scalar_prefetch=1,
            grid=(rows // QB,),
            in_specs=[
                pl.BlockSpec((QB, width), lambda b, s: (b, 0)),
                pl.BlockSpec((2 * rows, HD), lambda b, s: (0, 0)),
                pl.BlockSpec((HD, 2 * rows), lambda b, s: (0, 0)),
            ],
            out_specs=[
                pl.BlockSpec((QB, width), lambda b, s: (b, 0)),
                pl.BlockSpec((8, QB), lambda b, s: (0, b)),
            ],
        ),
        out_shape=(
            jax.ShapeDtypeStruct((rows, width), BF),
            jax.ShapeDtypeStruct((8, rows), F32),
        ),
        compiler_params=pltpu.CompilerParams(vmem_limit_bytes=40 << 20),
        cost_estimate=SMALL,
        name="attention_forward",
    )(chip, query, keys, values_t)


def backward_attention_kernel(
    chip_ref, q_ref, g_ref, o_ref, lse_ref, k_ref, kt_ref, v_ref, dq_ref, dk_ref, dv_ref
):
    block = pl.program_id(0)
    chunks = WINDOW // QB
    key_row = lax.broadcasted_iota(jnp.int32, (QB, QB), 0)
    query_col = lax.broadcasted_iota(jnp.int32, (QB, QB), 1)

    @pl.when(block == 0)
    def _():
        dk_ref[...] = jnp.zeros_like(dk_ref)
        dv_ref[...] = jnp.zeros_like(dv_ref)

    def rows_of(chunk):
        return pl.ds(pl.multiple_of((block + chunk) * QB, QB), QB)

    deltas = []
    for head in range(GROUP):
        cols = slice(head * HD, (head + 1) * HD)
        both = g_ref[:, cols].astype(F32) * o_ref[:, cols].astype(F32)
        deltas.append(jnp.sum(jnp.transpose(both), axis=0, keepdims=True))

    def one_chunk(chunk, keep, totals):
        rows = rows_of(chunk)
        keys = k_ref[rows, :]
        values = v_ref[rows, :]
        keys_t = kt_ref[:, rows]
        grad_keys = jnp.zeros((QB, HD), F32)
        grad_values = jnp.zeros((QB, HD), F32)
        new = []
        for head in range(GROUP):
            cols = slice(head * HD, (head + 1) * HD)
            query = q_ref[:, cols]
            grad = g_ref[:, cols]
            probs = jnp.exp2(dot(keys, query, NT) - lse_ref[head : head + 1, :])
            if keep is not None:
                probs = jnp.where(keep, probs, 0.0)
            grad_scores = (probs * (dot(values, grad, NT) - deltas[head])).astype(BF)
            grad_values = grad_values + dot(probs.astype(BF), grad)
            grad_keys = grad_keys + dot(grad_scores, query)
            new.append(totals[head] + dot(keys_t, grad_scores))
        dk_ref[rows, :] += grad_keys
        dv_ref[rows, :] += grad_values
        return tuple(new)

    def finish(totals):
        for head in range(GROUP):
            cols = slice(head * HD, (head + 1) * HD)
            dq_ref[:, cols] = (jnp.transpose(totals[head]) * HD ** (-0.5)).astype(BF)

    zeros = tuple(jnp.zeros((HD, QB), F32) for _ in range(GROUP))

    @pl.when(chip_ref[0] != 0)
    def _():
        totals = zeros
        for chunk in range(chunks + 1):
            keep = None
            if chunk == 0:
                keep = key_row > query_col
            if chunk == chunks:
                keep = key_row <= query_col
            totals = one_chunk(chunk, keep, totals)
        finish(totals)

    @pl.when(chip_ref[0] == 0)
    def _():
        def step(chunk, totals):
            return one_chunk(chunk, (key_row <= query_col) | (chunk < chunks), totals)

        finish(lax.fori_loop(chunks - block, chunks + 1, step, zeros))


def backward_attention(chip, query, grad, mixed, lse, keys, keys_t, values):
    rows = query.shape[0]
    width = GROUP * HD
    wide = pl.BlockSpec((QB, width), lambda b, s: (b, 0))
    whole = pl.BlockSpec((2 * rows, HD), lambda b, s: (0, 0))
    return kernel_call(
        backward_attention_kernel,
        grid_spec=pltpu.PrefetchScalarGridSpec(
            num_scalar_prefetch=1,
            grid=(rows // QB,),
            in_specs=[
                wide,
                wide,
                wide,
                pl.BlockSpec((8, QB), lambda b, s: (0, b)),
                whole,
                pl.BlockSpec((HD, 2 * rows), lambda b, s: (0, 0)),
                whole,
            ],
            out_specs=[wide, whole, whole],
        ),
        out_shape=(
            jax.ShapeDtypeStruct((rows, width), BF),
            jax.ShapeDtypeStruct((2 * rows, HD), F32),
            jax.ShapeDtypeStruct((2 * rows, HD), F32),
        ),
        compiler_params=pltpu.CompilerParams(vmem_limit_bytes=40 << 20),
        cost_estimate=SMALL,
        name="attention_backward",
    )(chip, query, grad, mixed, lse, keys, keys_t, values)


def pack_kernel(*refs):
    packed = refs[-1]
    depth, width = refs[0].shape[0], packed.shape[1]
    for i, piece in enumerate(refs[:-1]):
        packed[pl.ds(i * depth, depth), :] = piece[:, :width]


def pack(pieces, width):
    depth = pieces[0].shape[0]
    rows = depth * len(pieces)
    return kernel_call(
        pack_kernel,
        grid=(1,),
        in_specs=[pl.BlockSpec(piece.shape, lambda i: (0, 0)) for piece in pieces],
        out_specs=pl.BlockSpec((rows, width), lambda i: (0, 0)),
        out_shape=jax.ShapeDtypeStruct((rows, width), BF),
        compiler_params=pltpu.CompilerParams(vmem_limit_bytes=16 << 20),
        cost_estimate=SMALL,
        name="pack_pieces",
    )(*pieces)


def unpack_kernel(half, place_ref, far, near, whole):
    depth = far.shape[0] // half
    for i in range(half):
        rows = pl.ds(i * depth, depth)
        whole[pl.ds(pl.multiple_of(place_ref[i] * depth, depth), depth), :] = far[rows, :]
        whole[pl.ds(pl.multiple_of(place_ref[half + i] * depth, depth), depth), :] = near[rows, :]


def unpack(places, far, near, half):
    rows, width = far.shape
    packed = pl.BlockSpec((rows, width), lambda i, s: (0, 0))
    return kernel_call(
        functools.partial(unpack_kernel, half),
        grid_spec=pltpu.PrefetchScalarGridSpec(
            num_scalar_prefetch=1,
            grid=(1,),
            in_specs=[packed, packed],
            out_specs=pl.BlockSpec((2 * rows, width), lambda i, s: (0, 0)),
        ),
        out_shape=jax.ShapeDtypeStruct((2 * rows, width), BF),
        compiler_params=pltpu.CompilerParams(vmem_limit_bytes=16 << 20),
        cost_estimate=SMALL,
        name="unpack_pieces",
    )(places, far, near)


def split_kernel(groups, half, place_ref, whole, *refs):
    depth = refs[0].shape[0] // len(groups[0])
    for group, kept, sent in zip(groups, refs[: len(groups)], refs[len(groups) :]):
        for at, i in enumerate(group):
            rows = pl.ds(at * depth, depth)
            kept[rows, :] = whole[pl.ds(pl.multiple_of(place_ref[i] * depth, depth), depth), :]
            sent[rows, :] = whole[
                pl.ds(pl.multiple_of(place_ref[half + i] * depth, depth), depth), :
            ]


def split(places, whole, half, parts=1):
    size = half // parts
    groups = [range(half - (p + 1) * size, half - p * size) for p in range(parts)]
    rows, width = whole.shape[0] // (2 * parts), whole.shape[1]
    out = pl.BlockSpec((rows, width), lambda i, s: (0, 0))
    pieces = kernel_call(
        functools.partial(split_kernel, groups, half),
        grid_spec=pltpu.PrefetchScalarGridSpec(
            num_scalar_prefetch=1,
            grid=(1,),
            in_specs=[pl.BlockSpec(whole.shape, lambda i, s: (0, 0))],
            out_specs=[out] * (2 * parts),
        ),
        out_shape=(jax.ShapeDtypeStruct((rows, width), whole.dtype),) * (2 * parts),
        compiler_params=pltpu.CompilerParams(vmem_limit_bytes=24 << 20),
        cost_estimate=SMALL,
        name="split_pieces",
    )(places, whole)
    return pieces[:parts], pieces[parts:]


def fold_kernel(kept, came, *pieces):
    depth = pieces[0].shape[0]
    for i, piece in enumerate(pieces):
        rows = pl.ds(i * depth, depth)
        piece[...] = (kept[rows, :].astype(F32) + came[rows, :].astype(F32)).astype(BF)


def fold(kept, came, half):
    rows, width = kept.shape
    depth = rows // half
    whole = pl.BlockSpec((rows, width), lambda i: (0, 0))
    return kernel_call(
        fold_kernel,
        grid=(1,),
        in_specs=[whole, whole],
        out_specs=[pl.BlockSpec((depth, width), lambda i: (0, 0))] * half,
        out_shape=(jax.ShapeDtypeStruct((depth, width), BF),) * half,
        compiler_params=pltpu.CompilerParams(vmem_limit_bytes=24 << 20),
        cost_estimate=SMALL,
        name="fold_pieces",
    )(kept, came)


def weight_gradient_kernel(half, slot_ref, near_ref, far_ref, grad_ref, *refs):
    part = half // 2
    rows = near_ref.shape[0]
    depth = refs[0].shape[0] // part
    total = dot(near_ref[...], grad_ref[:rows, :], TN) + dot(far_ref[...], grad_ref[rows:, :], TN)
    total = total.astype(BF)
    count = total.shape[0] // depth
    for at in range(count):
        slot = slot_ref[pl.program_id(0) * count + at]
        k = lax.rem(slot, half)
        target = 2 * (slot // half) + 1 - k // part
        place = pl.ds(pl.multiple_of(lax.rem(k, part) * depth, depth), depth)
        for i, ref in enumerate(refs):

            @pl.when(target == i)
            def _(ref=ref, place=place, at=at):
                ref[place, :] = total[at * depth : (at + 1) * depth, :]


def weight_gradient(slots, near, far, grad):
    half = slots.shape[0] // 2
    rows, width = near.shape
    hidden = grad.shape[1]
    block = 384
    tall = pl.BlockSpec((rows, block), lambda i, s: (0, i))
    out = pl.BlockSpec((width // 4, hidden), lambda i, s: (0, 0))
    pieces = kernel_call(
        functools.partial(weight_gradient_kernel, half),
        grid_spec=pltpu.PrefetchScalarGridSpec(
            num_scalar_prefetch=1,
            grid=(width // block,),
            in_specs=[
                tall,
                tall,
                pl.BlockSpec(grad.shape, lambda i, s: (0, 0), pipeline_mode=pl.Buffered(1)),
            ],
            out_specs=[out] * 4,
        ),
        out_shape=(jax.ShapeDtypeStruct((width // 4, hidden), BF),) * 4,
        compiler_params=pltpu.CompilerParams(vmem_limit_bytes=40 << 20),
        cost_estimate=SMALL,
        name="weight_gradient",
    )(slots, near, far, grad)
    return pieces[:2], pieces[2:]


def gelu_parts(gate):
    square = gate * gate
    t = jnp.tanh(gate * (0.7978845608028654 + 0.035677408136300125 * square))
    half = 0.5 + 0.5 * t
    value = gate * half
    slope = half + 0.5 * gate * (1.0 - t * t) * (0.7978845608028654 + 0.10703222440890037 * square)
    return value, slope


def gate_up_block(norm_ref, whole, product_ref, to_gate_ref, to_up_ref):
    hidden = product_ref.shape[1]
    step = 384
    for start in range(0, hidden, step):
        cols = slice(start, start + step)
        gate = dot(norm_ref[...], whole[:, cols])
        up = dot(norm_ref[...], whole[:, hidden + start : hidden + start + step])
        value, slope = gelu_parts(gate)
        product_ref[:, cols] = (value * up).astype(BF)
        to_gate_ref[:, cols] = (up * slope).astype(BF)
        to_up_ref[:, cols] = value.astype(BF)


def gate_up_kernel(norm_ref, whole_ref, *refs):
    gate_up_block(norm_ref, whole_ref, *refs[-3:])


def apply_gate_up(norm, gate_up, *earlier):
    rows, width = norm.shape
    hidden = gate_up.shape[1] // 2
    block = 256
    steps = rows // block
    skip = steps if earlier else 0
    out = pl.BlockSpec((block, hidden), lambda i: (i + skip, 0))
    return kernel_call(
        gate_up_kernel,
        grid=(steps,),
        in_specs=[
            pl.BlockSpec((block, width), lambda i: (i, 0)),
            pl.BlockSpec(gate_up.shape, lambda i: (0, 0), pipeline_mode=pl.Buffered(1)),
        ]
        + [pl.BlockSpec(memory_space=pl.ANY)] * len(earlier),
        out_specs=[out, out, out],
        out_shape=(jax.ShapeDtypeStruct((2 * rows, hidden), BF),) * 3,
        input_output_aliases={2 + i: i for i in range(len(earlier))},
        compiler_params=pltpu.CompilerParams(vmem_limit_bytes=36 << 20),
        cost_estimate=SMALL,
        name="gate_up_rest" if earlier else "gate_up_first",
    )(norm, gate_up, *earlier)


def product_gradient_kernel(near_ref, far_ref, to_gate_ref, to_up_ref, down_ref, dgate_ref, dup_ref):
    step = 384

    def block(cot_ref):
        for start in range(0, down_ref.shape[1], step):
            cols = slice(start, start + step)
            grad = dot(cot_ref[...], down_ref[:, cols])
            dgate_ref[:, cols] = (grad * to_gate_ref[:, cols].astype(F32)).astype(BF)
            dup_ref[:, cols] = (grad * to_up_ref[:, cols].astype(F32)).astype(BF)

    first = pl.program_id(0) < pl.num_programs(0) // 2
    pl.when(first)(functools.partial(block, near_ref))
    pl.when(jnp.logical_not(first))(functools.partial(block, far_ref))


def product_gradient(near, far, to_gate, to_up, down):
    rows, width = near.shape
    hidden = to_gate.shape[1]
    block = 256
    steps = rows // block
    part = pl.BlockSpec((block, hidden), lambda i: (i, 0))
    return kernel_call(
        product_gradient_kernel,
        grid=(2 * steps,),
        in_specs=[
            pl.BlockSpec((block, width), lambda i: (jnp.minimum(i, steps - 1), 0)),
            pl.BlockSpec((block, width), lambda i: (jnp.maximum(i - steps, 0), 0)),
            part,
            part,
            pl.BlockSpec(down.shape, lambda i: (0, 0), pipeline_mode=pl.Buffered(1)),
        ],
        out_specs=[part, part],
        out_shape=(jax.ShapeDtypeStruct((2 * rows, hidden), BF),) * 2,
        compiler_params=pltpu.CompilerParams(vmem_limit_bytes=32 << 20),
        cost_estimate=SMALL,
        name="product_gradient",
    )(near, far, to_gate, to_up, down)


def down_project_kernel(product_ref, down_ref, *outs):
    for i, out in enumerate(outs):

        @pl.when(pl.program_id(0) // 2 == i)
        def _(out=out):
            out[...] = dot(product_ref[...], down_ref[...], NT).astype(BF)


def down_project(product, down):
    rows, hidden = product.shape
    width = down.shape[0]
    block = rows // 8

    def spec(i):
        return pl.BlockSpec((block, width), lambda at: (jnp.clip(at - 2 * i, 0, 1), 0))

    return kernel_call(
        down_project_kernel,
        grid=(8,),
        in_specs=[
            pl.BlockSpec((block, hidden), lambda at: (at, 0)),
            pl.BlockSpec(down.shape, lambda at: (0, 0), pipeline_mode=pl.Buffered(1)),
        ],
        out_specs=[spec(i) for i in range(4)],
        out_shape=(jax.ShapeDtypeStruct((rows // 4, width), BF),) * 4,
        compiler_params=pltpu.CompilerParams(vmem_limit_bytes=24 << 20),
        cost_estimate=SMALL,
        name="down_project",
    )(product, down)


def feed_back_kernel(dgate_ref, dup_ref, gate_up_ref, kept_ref, sent_ref):
    hidden = dgate_ref.shape[1]
    total = dot(dgate_ref[...], gate_up_ref[:, :hidden], NT)
    total = (total + dot(dup_ref[...], gate_up_ref[:, hidden:], NT)).astype(BF)

    @pl.when(pl.program_id(0) < pl.num_programs(0) // 2)
    def _():
        kept_ref[...] = total

    @pl.when(pl.program_id(0) >= pl.num_programs(0) // 2)
    def _():
        sent_ref[...] = total


def feed_back(first, rows, dgate, dup, gate_up):
    width, hidden = gate_up.shape[0], dgate.shape[1]
    block = 256
    steps = rows // block
    skip = first // block
    part = pl.BlockSpec((block, hidden), lambda i: (i + skip, 0))
    return kernel_call(
        feed_back_kernel,
        grid=(steps,),
        in_specs=[
            part,
            part,
            pl.BlockSpec(gate_up.shape, lambda i: (0, 0), pipeline_mode=pl.Buffered(1)),
        ],
        out_specs=[
            pl.BlockSpec((block, width), lambda i: (jnp.minimum(i, steps // 2 - 1), 0)),
            pl.BlockSpec((block, width), lambda i: (jnp.maximum(i - steps // 2, 0), 0)),
        ],
        out_shape=(jax.ShapeDtypeStruct((rows // 2, width), BF),) * 2,
        compiler_params=pltpu.CompilerParams(vmem_limit_bytes=36 << 20),
        cost_estimate=SMALL,
        name="feed_back",
    )(dgate, dup, gate_up)


class Shards:
    def __init__(self, count):
        self.count = count
        self.half = count // 2
        index = lax.axis_index("shard").astype(jnp.int32)
        hi, lo = index // 2, index % 2
        mine = [(hi ^ k) * 2 + lo for k in range(self.half)]
        partner = [(hi ^ k) * 2 + (1 - lo) for k in range(self.half)]
        self.places = jnp.stack(mine + partner)
        owner = jnp.arange(count, dtype=jnp.int32)
        self.slots = (owner // 2 ^ hi) + self.half * (owner % 2 ^ lo)

    def far(self, value, k):
        return lax.ppermute(
            value, "shard", [(i, ((i // 2) ^ k) * 2 + i % 2) for i in range(self.count)]
        )

    def near(self, value):
        return lax.ppermute(value, "shard", [(i, i ^ 1) for i in range(self.count)])


def tp_swap(value, mask):
    return lax.ppermute(value, "tp", [(i, i ^ mask) for i in range(4)])


def local(count, tokens, w_query, w_keyval, w_out, w_gate, w_up, w_down, gain_attn, gain_mlp, cotangent):
    rows, width = tokens.shape[0], tokens.shape[2]
    tp = lax.axis_index("tp").astype(jnp.int32)
    core, chip = tp % 2, tp // 2
    first_core = core == 0
    chip_table = jnp.reshape(chip, (1,))
    shards = Shards(count)

    def in_order(own, other):
        return jnp.where(
            first_core, jnp.concatenate([own, other], 0), jnp.concatenate([other, own], 0)
        )

    gain_one = gain_attn.astype(BF).astype(F32)[:, None]
    gain_two = gain_mlp.astype(BF).astype(F32)[:, None]
    own_query = w_query.astype(BF).astype(F32)
    own_keyval = w_keyval.astype(BF).astype(F32)
    own_gate = w_gate.astype(BF).astype(F32)
    own_up = w_up.astype(BF).astype(F32)
    keyval_half = jnp.where(first_core, own_keyval[:, :HD], own_keyval[:, HD:])
    send_in = (jnp.concatenate([own_query, keyval_half], 1) * gain_one).astype(BF)
    send_out = jnp.transpose(w_out).astype(BF)
    send_gate_up = (jnp.concatenate([own_gate, own_up], 1) * gain_two).astype(BF)
    send_down = jnp.transpose(w_down).astype(BF)

    heads = GROUP * HD
    half_count = shards.half
    places = shards.places
    part = half_count // 2
    token = places

    def sync(*values):
        nonlocal token
        token, *values = lax.optimization_barrier((token, *values))
        return values

    def far_all(piece):
        return [shards.far(piece, k) for k in range(1, half_count)]

    def rows_of(value, other):
        return lax.dynamic_slice_in_dim(value, (core ^ other) * rows, rows, 0)

    inputs = tokens.reshape(rows, width).astype(F32)
    scale_one = lax.rsqrt(jnp.mean(inputs * inputs, axis=-1, keepdims=True) + EPS)
    unit_own = (inputs * scale_one).astype(BF)
    far_in = far_all(send_in)
    unit_other = tp_swap(unit_own, 1)
    cot = cotangent.reshape(4, rows, width)
    cots = [lax.dynamic_index_in_dim(cot, tp ^ k, 0, keepdims=False) for k in range(4)]
    cot_near, cot_far = jnp.concatenate(cots[:2], 0), jnp.concatenate(cots[2:], 0)
    send_in, cot_near, cot_far, send_out, send_gate_up, send_down, unit_other, *far_in = sync(
        send_in, cot_near, cot_far, send_out, send_gate_up, send_down, unit_other, *far_in
    )

    gate_up_full = lax.all_gather(send_gate_up, "shard", axis=0, tiled=True)
    far_out = far_all(send_out)
    far_in = pack([send_in] + far_in, send_in.shape[1])
    near_in = shards.near(far_in)
    query_far_b = tp_swap(far_in[:, :heads], 2)
    unit = in_order(unit_own, unit_other)
    unit, query_far_b, near_in, far_in, *far_out = sync(
        unit, query_far_b, near_in, far_in, *far_out
    )

    in_full = unpack(places, far_in, near_in, half_count)
    in_query = in_full[:, :heads]
    scale = HD ** (-0.5)
    column = lax.broadcasted_iota(jnp.int32, (1, in_full.shape[1]), 1)
    query_half = (
        dot(unit, in_full) * jnp.where(column < heads, scale * LOG2E, 1.0)
    ).astype(BF)
    half, query_half, in_query, query_near, *far_out = sync(
        query_half[:, heads:], query_half, in_query, near_in[:, :heads], *far_out
    )

    half_other = tp_swap(half, 1)
    before = lax.ppermute(half, "tp", [(0, 2), (1, 3)])
    far_out = pack([send_out] + far_out, heads)
    near_out = shards.near(far_out)
    half, half_other, before, far_out, query_near = sync(
        half, half_other, before, far_out, query_near
    )

    query_near_b = tp_swap(query_near, 2)
    before_other = tp_swap(before, 1)
    own_pair = jnp.concatenate([before, half], 0)
    other_pair = jnp.concatenate([before_other, half_other], 0)
    keys = jnp.where(first_core, own_pair, other_pair)
    values = jnp.where(first_core, other_pair, own_pair)
    keys_t = jnp.transpose(keys)
    values_t = jnp.transpose(values)
    mixed_a, lse_a = forward_attention(chip_table, query_half, keys, values_t)
    mixed_a, query_near_b, far_out, near_out, send_down = sync(
        mixed_a, query_near_b, far_out, near_out, send_down
    )

    down_full = lax.all_gather(send_down, "shard", axis=0, tiled=True)
    out_far_b = tp_swap(far_out, 2)
    in_query_b = unpack(places, query_far_b, query_near_b, half_count)
    query_b = (dot(unit, in_query_b) * (scale * LOG2E)).astype(BF)
    mixed_b, lse_b = forward_attention(chip_table, query_b, keys, values_t)
    mixed_a, mixed_b, out_far_b, near_out = sync(mixed_a, mixed_b, out_far_b, near_out)

    out_near_b = tp_swap(near_out, 2)
    out_full = unpack(places, far_out, near_out, half_count)
    branch_other = dot(rows_of(mixed_a, 1), out_full, NT)
    branch_own = dot(rows_of(mixed_a, 0), out_full, NT)
    branch_other, branch_own, mixed_b, out_near_b = sync(
        branch_other, branch_own, mixed_b, out_near_b
    )

    out_full_b = unpack(places, out_far_b, out_near_b, half_count)
    branch_other = (branch_other + dot(rows_of(mixed_b, 1), out_full_b, NT)).astype(BF)
    branch_came = tp_swap(branch_other, 1)
    branch_own = branch_own + dot(rows_of(mixed_b, 0), out_full_b, NT)
    hidden = inputs + (branch_own + branch_came.astype(F32))
    scale_two = lax.rsqrt(jnp.mean(hidden * hidden, axis=-1, keepdims=True) + EPS)
    norm_own = (hidden * scale_two).astype(BF)
    (norm_own,) = sync(norm_own)

    cut = rows // 2
    norm_core = tp_swap(norm_own, 1)
    norm_x1 = tp_swap(norm_own[:cut], 2)
    norm_near = jnp.concatenate([norm_own, norm_core], 0)
    norm_own, norm_near, norm_x1 = sync(norm_own, norm_near, norm_x1)

    norm_x2 = tp_swap(norm_own[cut:], 2)
    norm_d1 = tp_swap(norm_x1, 1)
    product, to_gate, to_up = apply_gate_up(norm_near, gate_up_full)
    norm_x2, norm_d1, product, to_gate, to_up = sync(norm_x2, norm_d1, product, to_gate, to_up)

    norm_d2 = tp_swap(norm_x2, 1)
    norm_far = jnp.concatenate([norm_x1, norm_x2, norm_d1, norm_d2], 0)
    product, to_gate, to_up = apply_gate_up(norm_far, gate_up_full, product, to_gate, to_up)
    product, to_gate, to_up, norm_far = sync(product, to_gate, to_up, norm_far)
    kept_down, sent_down = weight_gradient(shards.slots, cot_near, cot_far, product)
    cot_near, cot_far, sent, product, norm_far = sync(
        cot_near, cot_far, sent_down[0], product, norm_far
    )

    came_down = [shards.near(sent)]
    dgate, dup = product_gradient(cot_near, cot_far, to_gate, to_up, down_full)
    dgate, dup, sent, product, *came_down = sync(dgate, dup, sent_down[1], product, *came_down)

    came_down.append(shards.near(sent))
    sums_down = list(fold(kept_down[0], came_down[0], part))
    kept_gate, sent_gate = weight_gradient(shards.slots, norm_near, norm_far, dgate)
    dgate, dup, sent, product, came_down[1], *sums_down = sync(
        dgate, dup, sent_gate[0], product, came_down[1], *sums_down
    )

    came_gate = [shards.near(sent)]
    far_sums = [shards.far(sums_down[0], part)]
    sums_down = list(fold(kept_down[1], came_down[1], part)) + sums_down
    back_x, back_diagonal = feed_back(2 * rows, 2 * rows, dgate, dup, gate_up_full)
    back_x, back_diagonal, dup, dgate, sent, *pieces = sync(
        back_x, back_diagonal, dup, dgate, sent_gate[1], *came_gate, *far_sums, *sums_down
    )
    came_gate, far_sums, sums_down = pieces[:1], pieces[1:2], pieces[2:]

    others = [k for k in range(1, half_count) if k != part]
    came_gate.append(shards.near(sent))
    far_sums += [shards.far(sums_down[k], k) for k in others]
    back_diagonal = tp_swap(back_diagonal, 1)
    sums_gate = list(fold(kept_gate[0], came_gate[0], part))
    back_far = [
        (a.astype(F32) + b.astype(F32)).astype(BF)
        for a, b in (
            (back_x[:cut], back_diagonal[:cut]),
            (back_x[cut:], back_diagonal[cut:]),
        )
    ]
    kept_up, sent_up = weight_gradient(shards.slots, norm_near, norm_far, after(dup, *back_far))
    dgate, dup, sent, *pieces = sync(
        dgate, dup, sent_up[0], *back_far, came_gate[1], *sums_gate, *far_sums
    )
    back_far, came_gate[1], sums_gate, far_sums_down = (
        pieces[:2],
        pieces[2],
        pieces[3 : 3 + part],
        pieces[3 + part :],
    )

    back_came = [tp_swap(back_far[0], 2)]
    came_up = [shards.near(sent)]
    far_sums = [shards.far(sums_gate[0], part)]
    sums_gate = list(fold(kept_gate[1], came_gate[1], part)) + sums_gate
    back_own, back_core = feed_back(0, 2 * rows, dgate, dup, gate_up_full)
    back_own, back_core, product, sent, back_far[1], *pieces = sync(
        back_own, back_core, product, sent_up[1], back_far[1], *back_came, *came_up, *far_sums, *sums_gate
    )
    back_came, came_up, far_sums, sums_gate = pieces[:1], pieces[1:2], pieces[2:3], pieces[3:]

    back_came.append(tp_swap(back_far[1], 2))
    came_up.append(shards.near(sent))
    far_sums += [shards.far(sums_gate[k], k) for k in others]
    back_core = tp_swap(back_core, 1)
    sums_up = list(fold(kept_up[0], came_up[0], part))
    down_parts = down_project(product, down_full)
    back_own, back_core, *pieces = sync(
        back_own, back_core, *back_came, came_up[1], *sums_up, *far_sums, *down_parts
    )
    back_came, came_up[1], sums_up, far_sums_gate, down_parts = (
        pieces[:2],
        pieces[2],
        pieces[3 : 3 + part],
        pieces[3 + part : 2 + part + half_count],
        pieces[2 + part + half_count :],
    )

    sums_up = list(fold(kept_up[1], came_up[1], part)) + sums_up
    down_diagonal = tp_swap(down_parts[3], 1)
    grad_norm = (
        back_own.astype(F32)
        + back_core.astype(F32)
        + jnp.concatenate(back_came, 0).astype(F32)
    )
    unit_two = hidden * scale_two
    grad_hidden = cots[0].astype(F32) + scale_two * (
        grad_norm - unit_two * jnp.mean(grad_norm * unit_two, axis=-1, keepdims=True)
    )
    branch_own = grad_hidden.astype(BF)
    branch_other = tp_swap(branch_own, 1)
    g_out_b = dot(branch_own, rows_of(mixed_b, 0), TN)
    grad_own = dot(branch_own, out_full_b).astype(BF)
    down_far = (down_parts[2].astype(F32) + down_diagonal.astype(F32)).astype(BF)
    branch_other = after(branch_other, g_out_b, grad_own, down_far)
    g_out_b = (g_out_b + dot(branch_other, rows_of(mixed_b, 1), TN)).astype(BF)
    grad_mixed_b = in_order(grad_own, dot(branch_other, out_full_b).astype(BF))
    grad_mixed_b, g_out_b, down_far, branch_own, branch_other, *sums_up = sync(
        grad_mixed_b, g_out_b, down_far, branch_own, branch_other, *sums_up
    )

    g_out_came = tp_swap(g_out_b, 2)
    far_sums = [shards.far(sums_up[part], part)]
    dq_b, dk_b, dv_b = backward_attention(
        chip_table, query_b, grad_mixed_b, mixed_b, lse_b, keys, keys_t, values
    )
    dq_b, dk_b, dv_b, g_out_came, branch_own, branch_other, *pieces = sync(
        dq_b, dk_b, dv_b, g_out_came, branch_own, branch_other, *far_sums, *sums_up
    )
    far_sums, sums_up = pieces[:1], pieces[1:]

    g_query_b = dot(unit, dq_b, TN).astype(BF)
    g_out = (
        dot(branch_own, rows_of(mixed_a, 0), TN)
        + dot(branch_other, rows_of(mixed_a, 1), TN)
        + g_out_came.astype(F32)
    )
    (kept_out,), (sent_out,) = split(places, g_out.astype(BF), half_count)
    grad_mixed_a = in_order(
        dot(branch_own, out_full).astype(BF), dot(branch_other, out_full).astype(BF)
    )
    g_query_b, sent_out, grad_mixed_a, kept_out, *sums_up = sync(
        g_query_b, sent_out, grad_mixed_a, kept_out, *sums_up
    )

    g_query_came = tp_swap(g_query_b, 2)
    far_sums += [shards.far(sums_up[k], k) for k in others]
    came_out = shards.near(sent_out)
    dq_a, dk_a, dv_a = backward_attention(
        chip_table, query_half, grad_mixed_a, mixed_a, lse_a, keys, keys_t, values
    )
    dq_a, dk_a, dv_a, g_query_came, came_out, *far_sums_up = sync(
        dq_a, dk_a, dv_a, g_query_came, came_out, *far_sums
    )

    grad_keys = (dk_a + dk_b) * LN2
    grad_values = dv_a + dv_b
    mine = jnp.where(first_core, grad_keys, grad_values)
    theirs = jnp.where(first_core, grad_values, grad_keys).astype(BF)
    theirs = tp_swap(theirs, 1)
    cuts = [0, rows // 16 * 5, rows // 32 * 21, rows]
    down_far = [down_far[a:b] for a, b in zip(cuts[:-1], cuts[1:])]
    down_came = [tp_swap(down_far[0], 2)]
    g_query = (dot(unit, dq_a, TN) + g_query_came.astype(F32)).astype(BF)
    (kept_query,), (sent_query,) = split(places, g_query, half_count)
    sums_out = fold(kept_out, came_out, half_count)
    mine = mine + theirs.astype(F32)
    chip_rows = mine.shape[0] // 2
    mine, own = mine[chip_rows:], mine[:chip_rows].astype(BF)
    mine, own, sent_query, dq_a, dq_b, down_came[0], down_far[1], down_far[2], *sums_out = sync(
        mine, own, sent_query, dq_a, dq_b, down_came[0], down_far[1], down_far[2], *sums_out
    )

    earlier = lax.ppermute(own, "tp", [(2, 0), (3, 1)])
    came_query = shards.near(sent_query)
    far_out_sums = [shards.far(sums_out[k], k) for k in range(1, half_count)]
    back_other = dot(rows_of(dq_a, 1), in_query, NT) + dot(rows_of(dq_b, 1), in_query_b, NT)
    back_own = dot(rows_of(dq_a, 0), in_query, NT) + dot(rows_of(dq_b, 0), in_query_b, NT)
    back_own, back_other, earlier, came_query, down_far[1], *far_out_sums = sync(
        back_own, back_other, earlier, came_query, down_far[1], *far_out_sums
    )

    down_came.append(tp_swap(down_far[1], 2))
    grad_half = (mine + earlier.astype(F32)).astype(BF)
    g_half = dot(unit, grad_half, TN).astype(BF)
    (kept_half,), (sent_half,) = split(places, g_half, half_count)
    sums_query = fold(kept_query, came_query, half_count)
    in_half = in_full[:, heads:]
    back_other = (back_other + dot(rows_of(grad_half, 1), in_half, NT)).astype(BF)
    back_own = back_own + dot(rows_of(grad_half, 0), in_half, NT)
    back_other, back_own, kept_half, sent_half, down_came[1], down_far[2], *sums_query = sync(
        back_other, back_own, kept_half, sent_half, down_came[1], down_far[2], *sums_query
    )

    came_half = shards.near(sent_half)
    back_came = tp_swap(back_other, 1)
    far_query = [shards.far(sums_query[k], k) for k in range(1, half_count)]
    down_came.append(tp_swap(down_far[2], 2))
    down_core = tp_swap(down_parts[1], 1)
    grad_unit = back_own + back_came.astype(F32)
    unit_one = inputs * scale_one
    grad_tokens = grad_hidden + scale_one * (
        grad_unit - unit_one * jnp.mean(grad_unit * unit_one, axis=-1, keepdims=True)
    )
    came_half, grad_tokens, down_core, *pieces = sync(
        came_half, grad_tokens, down_core, *down_came, *far_query
    )
    down_came, far_query = pieces[:3], pieces[3:]

    sums_half = fold(kept_half, came_half, half_count)
    far_half = [shards.far(sums_half[k], k) for k in range(1, half_count)]
    output = (
        hidden
        + down_parts[0].astype(F32)
        + down_core.astype(F32)
        + jnp.concatenate(down_came, 0).astype(F32)
    ).astype(BF)

    def total(own, others):
        return functools.reduce(lambda t, o: t + o.astype(F32), others, own.astype(F32))

    sum_gate = total(sums_gate[0], far_sums_gate)
    sum_up = total(sums_up[0], far_sums_up)
    grad_w_gate = sum_gate * gain_two
    grad_w_up = sum_up * gain_two
    gain_two_part = jnp.sum(own_gate * sum_gate + own_up * sum_up, axis=1)
    grad_w_down = jnp.transpose(total(sums_down[0], far_sums_down))
    grad_w_out = jnp.transpose(total(sums_out[0], far_out_sums))
    sum_query = total(sums_query[0], far_query)
    sum_half = total(sums_half[0], far_half)

    gain_one_part = jnp.sum(own_query * sum_query, axis=1) + jnp.sum(keyval_half * sum_half, axis=1)
    small = jnp.concatenate(
        [jnp.transpose(sum_half), gain_one_part[None], gain_two_part[None], jnp.zeros((6, sum_half.shape[0]), F32)], 0
    )
    small = small + tp_swap(small, 2)
    other = tp_swap(small, 1)
    gains = small[HD : HD + 2] + other[HD : HD + 2]
    sum_half = jnp.transpose(small[:HD])
    half_swapped = jnp.transpose(other[:HD])
    grad_w_keyval = (
        jnp.where(
            first_core,
            jnp.concatenate([sum_half, half_swapped], 1),
            jnp.concatenate([half_swapped, sum_half], 1),
        )
        * gain_one
    )
    return (
        output.reshape(rows, 1, width),
        grad_tokens.reshape(rows, 1, width),
        sum_query * gain_one,
        grad_w_keyval,
        grad_w_out,
        grad_w_gate,
        grad_w_up,
        grad_w_down,
        gains[0],
        gains[1],
    )


def solution(mesh):
    in_specs = (
        P("tp", "shard", None),
        P("shard", "tp"),
        P("shard", None),
        P("tp", "shard"),
        P("shard", "tp"),
        P("shard", "tp"),
        P("tp", "shard"),
        P("shard"),
        P("shard"),
        P(None, "shard", None),
    )
    out_specs = (
        P("tp", "shard", None),
        P("tp", "shard", None),
        P("shard", "tp"),
        P("shard", None),
        P("tp", "shard"),
        P("shard", "tp"),
        P("shard", "tp"),
        P("tp", "shard"),
        P("shard"),
        P("shard"),
    )
    return jax.shard_map(
        functools.partial(local, mesh.shape["shard"]),
        mesh=mesh,
        in_specs=in_specs,
        out_specs=out_specs,
        check_vma=False,
    )
```

```python
import functools

import jax
import jax.numpy as jnp
from jax import lax
from jax.experimental import pallas as pl
from jax.experimental.pallas import tpu as pltpu
from jax.sharding import PartitionSpec as P

HD = 128
WINDOW = 1024
QB = 256
GROUP = 3
EPS = 1e-06
LOG2E = 1.4426950408889634
LN2 = 0.6931471805599453
NEG = -1e30
LARGE = 1 << 20
OUT = pltpu.HBM
SMALL = pl.CostEstimate(flops=0, transcendentals=0, bytes_accessed=0)
BF = jnp.bfloat16
F32 = jnp.float32
NT = (((1,), (1,)), ((), ()))
TN = (((0,), (0,)), ((), ()))
NN = (((1,), (0,)), ((), ()))


def dot(a, b, dims=NN):
    return lax.dot_general(a, b, dims, preferred_element_type=F32)


def after(value, *others):
    return lax.optimization_barrier((value, *others))[0]


def kernel_call(*args, **kwargs):
    call = pl.pallas_call(*args, **kwargs)

    def run(*operands):
        return call(
            *(
                pltpu.with_memory_space_constraint(x, pltpu.HBM) if x.size > LARGE else x
                for x in operands
            )
        )

    return run


def forward_attention_kernel(chip_ref, q_ref, k_ref, vt_ref, o_ref, lse_ref):
    block = pl.program_id(0)
    chunks = WINDOW // QB
    key_row = lax.broadcasted_iota(jnp.int32, (QB, QB), 0)
    query_col = lax.broadcasted_iota(jnp.int32, (QB, QB), 1)

    def rows_of(chunk):
        return pl.ds(pl.multiple_of((block + chunk) * QB, QB), QB)

    def finish(head, top, total, mixed):
        cols = slice(head * HD, (head + 1) * HD)
        o_ref[:, cols] = jnp.transpose(mixed / total).astype(BF)
        lse_ref[head : head + 1, :] = top + jnp.log(total) * LOG2E

    def attend(first):
        for head in range(GROUP):
            query = q_ref[:, head * HD : (head + 1) * HD]
            scores = {}
            for chunk in range(first, chunks + 1):
                scores[chunk] = dot(k_ref[rows_of(chunk), :], query, NT)
                if chunk == 0:
                    scores[chunk] = jnp.where(key_row > query_col, scores[chunk], NEG)
                if chunk == chunks:
                    scores[chunk] = jnp.where(key_row <= query_col, scores[chunk], NEG)
            top = functools.reduce(jnp.maximum, scores.values())
            top = jnp.max(top, axis=0, keepdims=True)
            total = jnp.zeros((1, QB), F32)
            mixed = jnp.zeros((HD, QB), F32)
            for chunk, part in scores.items():
                probs = jnp.exp2(part - top)
                total = total + jnp.sum(probs, axis=0, keepdims=True)
                mixed = mixed + dot(vt_ref[:, rows_of(chunk)], probs.astype(BF))
            finish(head, top, total, mixed)

    pl.when(chip_ref[0] != 0)(functools.partial(attend, 0))
    for at in range(chunks):
        pl.when((chip_ref[0] == 0) & (block == at))(functools.partial(attend, chunks - at))


def forward_attention(chip, query, keys, values_t):
    rows = query.shape[0]
    width = GROUP * HD
    return kernel_call(
        forward_attention_kernel,
        grid_spec=pltpu.PrefetchScalarGridSpec(
            num_scalar_prefetch=1,
            grid=(rows // QB,),
            in_specs=[
                pl.BlockSpec((QB, width), lambda b, s: (b, 0)),
                pl.BlockSpec((2 * rows, HD), lambda b, s: (0, 0)),
                pl.BlockSpec((HD, 2 * rows), lambda b, s: (0, 0)),
            ],
            out_specs=[
                pl.BlockSpec((QB, width), lambda b, s: (b, 0)),
                pl.BlockSpec((8, QB), lambda b, s: (0, b)),
            ],
        ),
        out_shape=(
            jax.ShapeDtypeStruct((rows, width), BF),
            jax.ShapeDtypeStruct((8, rows), F32),
        ),
        compiler_params=pltpu.CompilerParams(vmem_limit_bytes=40 << 20),
        cost_estimate=SMALL,
        name="attention_forward",
    )(chip, query, keys, values_t)


def backward_attention_kernel(
    chip_ref, q_ref, g_ref, o_ref, lse_ref, k_ref, kt_ref, v_ref, dq_ref, dk_ref, dv_ref
):
    block = pl.program_id(0)
    chunks = WINDOW // QB
    key_row = lax.broadcasted_iota(jnp.int32, (QB, QB), 0)
    query_col = lax.broadcasted_iota(jnp.int32, (QB, QB), 1)

    @pl.when(block == 0)
    def _():
        dk_ref[...] = jnp.zeros_like(dk_ref)
        dv_ref[...] = jnp.zeros_like(dv_ref)

    def rows_of(chunk):
        return pl.ds(pl.multiple_of((block + chunk) * QB, QB), QB)

    deltas = []
    for head in range(GROUP):
        cols = slice(head * HD, (head + 1) * HD)
        both = g_ref[:, cols].astype(F32) * o_ref[:, cols].astype(F32)
        deltas.append(jnp.sum(jnp.transpose(both), axis=0, keepdims=True))

    def one_chunk(chunk, keep, totals):
        rows = rows_of(chunk)
        keys = k_ref[rows, :]
        values = v_ref[rows, :]
        keys_t = kt_ref[:, rows]
        grad_keys = jnp.zeros((QB, HD), F32)
        grad_values = jnp.zeros((QB, HD), F32)
        new = []
        for head in range(GROUP):
            cols = slice(head * HD, (head + 1) * HD)
            query = q_ref[:, cols]
            grad = g_ref[:, cols]
            probs = jnp.exp2(dot(keys, query, NT) - lse_ref[head : head + 1, :])
            if keep is not None:
                probs = jnp.where(keep, probs, 0.0)
            grad_scores = (probs * (dot(values, grad, NT) - deltas[head])).astype(BF)
            grad_values = grad_values + dot(probs.astype(BF), grad)
            grad_keys = grad_keys + dot(grad_scores, query)
            new.append(totals[head] + dot(keys_t, grad_scores))
        dk_ref[rows, :] += grad_keys
        dv_ref[rows, :] += grad_values
        return tuple(new)

    def finish(totals):
        for head in range(GROUP):
            cols = slice(head * HD, (head + 1) * HD)
            dq_ref[:, cols] = (jnp.transpose(totals[head]) * HD ** (-0.5)).astype(BF)

    zeros = tuple(jnp.zeros((HD, QB), F32) for _ in range(GROUP))

    @pl.when(chip_ref[0] != 0)
    def _():
        totals = zeros
        for chunk in range(chunks + 1):
            keep = None
            if chunk == 0:
                keep = key_row > query_col
            if chunk == chunks:
                keep = key_row <= query_col
            totals = one_chunk(chunk, keep, totals)
        finish(totals)

    @pl.when(chip_ref[0] == 0)
    def _():
        def step(chunk, totals):
            return one_chunk(chunk, (key_row <= query_col) | (chunk < chunks), totals)

        finish(lax.fori_loop(chunks - block, chunks + 1, step, zeros))


def backward_attention(chip, query, grad, mixed, lse, keys, keys_t, values):
    rows = query.shape[0]
    width = GROUP * HD
    wide = pl.BlockSpec((QB, width), lambda b, s: (b, 0))
    whole = pl.BlockSpec((2 * rows, HD), lambda b, s: (0, 0))
    return kernel_call(
        backward_attention_kernel,
        grid_spec=pltpu.PrefetchScalarGridSpec(
            num_scalar_prefetch=1,
            grid=(rows // QB,),
            in_specs=[
                wide,
                wide,
                wide,
                pl.BlockSpec((8, QB), lambda b, s: (0, b)),
                whole,
                pl.BlockSpec((HD, 2 * rows), lambda b, s: (0, 0)),
                whole,
            ],
            out_specs=[wide, whole, whole],
        ),
        out_shape=(
            jax.ShapeDtypeStruct((rows, width), BF),
            jax.ShapeDtypeStruct((2 * rows, HD), F32),
            jax.ShapeDtypeStruct((2 * rows, HD), F32),
        ),
        compiler_params=pltpu.CompilerParams(vmem_limit_bytes=40 << 20),
        cost_estimate=SMALL,
        name="attention_backward",
    )(chip, query, grad, mixed, lse, keys, keys_t, values)


def pack_kernel(*refs):
    packed = refs[-1]
    depth, width = refs[0].shape[0], packed.shape[1]
    for i, piece in enumerate(refs[:-1]):
        packed[pl.ds(i * depth, depth), :] = piece[:, :width]


def pack(pieces, width):
    depth = pieces[0].shape[0]
    rows = depth * len(pieces)
    return kernel_call(
        pack_kernel,
        grid=(1,),
        in_specs=[pl.BlockSpec(piece.shape, lambda i: (0, 0)) for piece in pieces],
        out_specs=pl.BlockSpec((rows, width), lambda i: (0, 0)),
        out_shape=jax.ShapeDtypeStruct((rows, width), BF),
        compiler_params=pltpu.CompilerParams(vmem_limit_bytes=16 << 20),
        cost_estimate=SMALL,
        name="pack_pieces",
    )(*pieces)


def unpack_kernel(half, place_ref, far, near, whole):
    depth = far.shape[0] // half
    for i in range(half):
        rows = pl.ds(i * depth, depth)
        whole[pl.ds(pl.multiple_of(place_ref[i] * depth, depth), depth), :] = far[rows, :]
        whole[pl.ds(pl.multiple_of(place_ref[half + i] * depth, depth), depth), :] = near[rows, :]


def unpack(places, far, near, half):
    rows, width = far.shape
    packed = pl.BlockSpec((rows, width), lambda i, s: (0, 0))
    return kernel_call(
        functools.partial(unpack_kernel, half),
        grid_spec=pltpu.PrefetchScalarGridSpec(
            num_scalar_prefetch=1,
            grid=(1,),
            in_specs=[packed, packed],
            out_specs=pl.BlockSpec((2 * rows, width), lambda i, s: (0, 0)),
        ),
        out_shape=jax.ShapeDtypeStruct((2 * rows, width), BF),
        compiler_params=pltpu.CompilerParams(vmem_limit_bytes=16 << 20),
        cost_estimate=SMALL,
        name="unpack_pieces",
    )(places, far, near)


def split_kernel(groups, half, place_ref, whole, *refs):
    depth = refs[0].shape[0] // len(groups[0])
    for group, kept, sent in zip(groups, refs[: len(groups)], refs[len(groups) :]):
        for at, i in enumerate(group):
            rows = pl.ds(at * depth, depth)
            kept[rows, :] = whole[pl.ds(pl.multiple_of(place_ref[i] * depth, depth), depth), :]
            sent[rows, :] = whole[
                pl.ds(pl.multiple_of(place_ref[half + i] * depth, depth), depth), :
            ]


def split(places, whole, half, parts=1):
    size = half // parts
    groups = [range(half - (p + 1) * size, half - p * size) for p in range(parts)]
    rows, width = whole.shape[0] // (2 * parts), whole.shape[1]
    out = pl.BlockSpec((rows, width), lambda i, s: (0, 0))
    pieces = kernel_call(
        functools.partial(split_kernel, groups, half),
        grid_spec=pltpu.PrefetchScalarGridSpec(
            num_scalar_prefetch=1,
            grid=(1,),
            in_specs=[pl.BlockSpec(whole.shape, lambda i, s: (0, 0))],
            out_specs=[out] * (2 * parts),
        ),
        out_shape=(jax.ShapeDtypeStruct((rows, width), whole.dtype),) * (2 * parts),
        compiler_params=pltpu.CompilerParams(vmem_limit_bytes=24 << 20),
        cost_estimate=SMALL,
        name="split_pieces",
    )(places, whole)
    return pieces[:parts], pieces[parts:]


def fold_kernel(kept, came, *pieces):
    depth = pieces[0].shape[0]
    for i, piece in enumerate(pieces):
        rows = pl.ds(i * depth, depth)
        piece[...] = (kept[rows, :].astype(F32) + came[rows, :].astype(F32)).astype(BF)


def fold(kept, came, half):
    rows, width = kept.shape
    depth = rows // half
    whole = pl.BlockSpec((rows, width), lambda i: (0, 0))
    return kernel_call(
        fold_kernel,
        grid=(1,),
        in_specs=[whole, whole],
        out_specs=[pl.BlockSpec((depth, width), lambda i: (0, 0))] * half,
        out_shape=(OUT((depth, width), BF),) * half,
        compiler_params=pltpu.CompilerParams(vmem_limit_bytes=24 << 20),
        cost_estimate=SMALL,
        name="fold_pieces",
    )(kept, came)


def token_gradient_kernel(own_ref, came_ref, token_ref, through_ref, out_ref):
    grad = own_ref[...] + came_ref[...].astype(F32)
    unit = token_ref[...].astype(F32)
    scale = lax.rsqrt(jnp.mean(unit * unit, axis=-1, keepdims=True) + EPS)
    unit = unit * scale
    inner = jnp.mean(grad * unit, axis=-1, keepdims=True)
    out_ref[:, 0, :] = through_ref[...] + scale * (grad - unit * inner)


def token_gradient(own, came, tokens, through):
    rows, width = own.shape
    block = 128
    part = pl.BlockSpec((block, width), lambda i: (i, 0))
    return kernel_call(
        token_gradient_kernel,
        grid=(rows // block,),
        in_specs=[part] * 4,
        out_specs=pl.BlockSpec((block, 1, width), lambda i: (i, 0, 0)),
        out_shape=jax.ShapeDtypeStruct((rows, 1, width), F32),
        compiler_params=pltpu.CompilerParams(vmem_limit_bytes=24 << 20),
        cost_estimate=SMALL,
        name="token_gradient",
    )(own, came, tokens, through)


def query_back_kernel(core_ref, a_ref, b_ref, weight_a_ref, weight_b_ref, own_ref, other_ref):
    rows = own_ref.shape[0]
    for out, core in ((other_ref, 1 - core_ref[0]), (own_ref, core_ref[0])):
        place = pl.ds(pl.multiple_of(core * rows, rows), rows)
        total = dot(a_ref[place, :], weight_a_ref[...], NT)
        out[...] = total + dot(b_ref[place, :], weight_b_ref[...], NT)


def query_back(core, a, b, weight_a, weight_b):
    rows, width = a.shape[0] // 2, weight_a.shape[0]
    whole = [pl.BlockSpec(x.shape, lambda i, s: (0, 0)) for x in (a, b, weight_a, weight_b)]
    return kernel_call(
        query_back_kernel,
        grid_spec=pltpu.PrefetchScalarGridSpec(
            num_scalar_prefetch=1,
            grid=(1,),
            in_specs=whole,
            out_specs=[pl.BlockSpec((rows, width), lambda i, s: (0, 0))] * 2,
        ),
        out_shape=(jax.ShapeDtypeStruct((rows, width), F32),) * 2,
        compiler_params=pltpu.CompilerParams(vmem_limit_bytes=36 << 20),
        cost_estimate=SMALL,
        name="query_back",
    )(core, a, b, weight_a, weight_b)


def spans(parts, block):
    counts = [part.shape[0] // block for part in parts]
    return [(sum(counts[:i]), count) for i, count in enumerate(counts)]


def part_specs(parts, block, width):
    def spec(first, count):
        return pl.BlockSpec((block, width), lambda i: (jnp.clip(i - first, 0, count - 1), 0))

    return [spec(first, count) for first, count in spans(parts, block)]


def weight_gradient_kernel(half, slot_ref, *refs):
    part = half // 2
    outs, grad_ref, parts = refs[-4:], refs[-5], refs[:-5]
    depth = outs[0].shape[0] // part
    first = 0
    total = None
    for ref in parts:
        rows = ref.shape[0]
        term = dot(ref[...], grad_ref[first : first + rows, :], TN)
        total = term if total is None else total + term
        first += rows
    total = total.astype(BF)
    count = total.shape[0] // depth
    for at in range(count):
        slot = slot_ref[pl.program_id(0) * count + at]
        k = lax.rem(slot, half)
        target = 2 * (slot // half) + 1 - k // part
        place = pl.ds(pl.multiple_of(lax.rem(k, part) * depth, depth), depth)
        for i, ref in enumerate(outs):

            @pl.when(target == i)
            def _(ref=ref, place=place, at=at):
                ref[place, :] = total[at * depth : (at + 1) * depth, :]


def weight_gradient(slots, parts, grad):
    half = slots.shape[0] // 2
    width = parts[0].shape[1]
    hidden = grad.shape[1]
    block = 384
    pieces = kernel_call(
        functools.partial(weight_gradient_kernel, half),
        grid_spec=pltpu.PrefetchScalarGridSpec(
            num_scalar_prefetch=1,
            grid=(width // block,),
            in_specs=[pl.BlockSpec((part.shape[0], block), lambda i, s: (0, i)) for part in parts]
            + [pl.BlockSpec(grad.shape, lambda i, s: (0, 0), pipeline_mode=pl.Buffered(1))],
            out_specs=[pl.BlockSpec((width // 4, hidden), lambda i, s: (0, 0))] * 4,
        ),
        out_shape=(OUT((width // 4, hidden), BF),) * 4,
        compiler_params=pltpu.CompilerParams(vmem_limit_bytes=40 << 20),
        cost_estimate=SMALL,
        name="weight_gradient",
    )(slots, *parts, grad)
    return pieces[:2], pieces[2:]


def combine_kernel(a_ref, b_ref, *outs):
    first = 0
    for out in outs:
        rows = slice(first, first + out.shape[0])
        out[...] = (a_ref[rows, :].astype(F32) + b_ref[rows, :].astype(F32)).astype(BF)
        first += out.shape[0]


def combine(a, b):
    rows, width = a.shape
    whole = pl.BlockSpec((rows, width), lambda i: (0, 0))
    return kernel_call(
        combine_kernel,
        grid=(1,),
        in_specs=[whole, whole],
        out_specs=[pl.BlockSpec((rows // 2, width), lambda i: (0, 0))] * 2,
        out_shape=(jax.ShapeDtypeStruct((rows // 2, width), BF),) * 2,
        compiler_params=pltpu.CompilerParams(vmem_limit_bytes=16 << 20),
        cost_estimate=SMALL,
        name="combine",
    )(a, b)


def gelu_parts(gate):
    square = gate * gate
    t = jnp.tanh(gate * (0.7978845608028654 + 0.035677408136300125 * square))
    half = 0.5 + 0.5 * t
    value = gate * half
    slope = half + 0.5 * gate * (1.0 - t * t) * (0.7978845608028654 + 0.10703222440890037 * square)
    return value, slope


def stream(source, whole, sems, cuts, use, axis=1):
    def at(ref, cut):
        where = pl.ds(cut[0], cut[1] - cut[0])
        return ref.at[:, where] if axis else ref.at[where, :]

    copies = [
        pltpu.make_async_copy(at(source, cut), at(whole, cut), sems.at[i])
        for i, cut in enumerate(cuts)
    ]

    @pl.when(pl.program_id(0) == 0)
    def _():
        for copy in copies:
            copy.start()
        for cut, copy in zip(cuts, copies):
            copy.wait()
            use(cut)

    @pl.when(pl.program_id(0) > 0)
    def _():
        use((0, cuts[-1][1]))


def thirds(width):
    return [(i * width // 3, (i + 1) * width // 3) for i in range(3)]


def gate_up_block(norm_ref, whole, cut, product_ref, to_gate_ref, to_up_ref):
    hidden = product_ref.shape[1]
    cols = slice(*cut)
    gate = dot(norm_ref[...], whole[:, cols])
    up = dot(norm_ref[...], whole[:, hidden + cut[0] : hidden + cut[1]])
    value, slope = gelu_parts(gate)
    product_ref[:, cols] = (value * up).astype(BF)
    to_gate_ref[:, cols] = (up * slope).astype(BF)
    to_up_ref[:, cols] = value.astype(BF)


def gate_up_kernel(places, *refs):
    parts, source = refs[: len(places)], refs[len(places)]
    outs, whole, sems = refs[-5:-2], refs[-2], refs[-1]
    hidden = outs[0].shape[1]
    step = pl.program_id(0)
    cuts = thirds(hidden)
    copies = [
        [
            pltpu.make_async_copy(
                source.at[:, pl.ds(side + a, b - a)],
                whole.at[:, pl.ds(side + a, b - a)],
                sems.at[2 * i + side // hidden],
            )
            for side in (0, hidden)
        ]
        for i, (a, b) in enumerate(cuts)
    ]

    @pl.when(step == 0)
    def _():
        for pair in copies:
            for copy in pair:
                copy.start()
        for cut, pair in zip(cuts, copies):
            for copy in pair:
                copy.wait()
            gate_up_block(parts[0], whole, cut, *outs)

    for (first, count), ref in zip(places, parts):
        inside = (step > 0) & (step >= first) & (step < first + count)
        pl.when(inside)(functools.partial(gate_up_block, ref, whole, (0, hidden), *outs))


def apply_gate_up(parts, gate_up, *earlier):
    width, hidden = gate_up.shape[0], gate_up.shape[1] // 2
    block = 256
    places = spans(parts, block)
    steps = sum(count for _, count in places)
    skip = steps if earlier else 0
    out = pl.BlockSpec((block, hidden), lambda i: (i + skip, 0))
    anywhere = pl.BlockSpec(memory_space=pl.ANY)
    return kernel_call(
        functools.partial(gate_up_kernel, places),
        grid=(steps,),
        in_specs=part_specs(parts, block, width) + [anywhere] * (1 + len(earlier)),
        out_specs=[out, out, out],
        out_shape=(OUT((2 * steps * block, hidden), BF),) * 3,
        scratch_shapes=[pltpu.VMEM(gate_up.shape, BF), pltpu.SemaphoreType.DMA((6,))],
        input_output_aliases={len(parts) + 1 + i: i for i in range(len(earlier))},
        compiler_params=pltpu.CompilerParams(vmem_limit_bytes=40 << 20),
        cost_estimate=SMALL,
        name="gate_up_rest" if earlier else "gate_up_first",
    )(*parts, gate_up, *earlier)


def product_gradient_kernel(places, *refs):
    parts = refs[: len(places)]
    to_gate_ref, to_up_ref, source, dgate_ref, dup_ref, whole, sems = refs[len(places) :]
    at = pl.program_id(0)

    def use(cut):
        cols = slice(*cut)

        def block(cot_ref):
            grad = dot(cot_ref[...], whole[:, cols])
            dgate_ref[:, cols] = (grad * to_gate_ref[:, cols].astype(F32)).astype(BF)
            dup_ref[:, cols] = (grad * to_up_ref[:, cols].astype(F32)).astype(BF)

        if cut[1] - cut[0] < whole.shape[1]:
            block(parts[0])
        else:
            for (first, count), ref in zip(places, parts):
                pl.when((at >= first) & (at < first + count))(functools.partial(block, ref))

    stream(source, whole, sems, thirds(whole.shape[1]), use)


def product_gradient(parts, to_gate, to_up, down):
    rows, hidden = to_gate.shape
    block = 256
    places = spans(parts, block)
    part = pl.BlockSpec((block, hidden), lambda i: (i, 0))
    return kernel_call(
        functools.partial(product_gradient_kernel, places),
        grid=(rows // block,),
        in_specs=part_specs(parts, block, down.shape[0])
        + [part, part, pl.BlockSpec(memory_space=pl.ANY)],
        out_specs=[part, part],
        out_shape=(OUT((rows, hidden), BF),) * 2,
        scratch_shapes=[pltpu.VMEM(down.shape, BF), pltpu.SemaphoreType.DMA((3,))],
        compiler_params=pltpu.CompilerParams(vmem_limit_bytes=32 << 20),
        cost_estimate=SMALL,
        name="product_gradient",
    )(*parts, to_gate, to_up, down)


def branch_gradients_kernel(branch_ref, mixed_ref, weight_ref, *refs):
    g_ref, grad_ref = refs[-2:]
    total = dot(branch_ref[...], mixed_ref[...], TN)
    if len(refs) > 2:
        total = total + refs[0][...]
    g_ref[...] = total.astype(g_ref.dtype)
    grad_ref[...] = dot(branch_ref[...], weight_ref[...]).astype(BF)


def branch_gradients(branch, mixed, weight, *earlier):
    operands = (branch, mixed, weight, *earlier)
    whole = [pl.BlockSpec(x.shape, lambda i: (0, 0)) for x in operands]
    return kernel_call(
        branch_gradients_kernel,
        grid=(1,),
        in_specs=whole,
        out_specs=[whole[2], whole[1]],
        out_shape=(
            jax.ShapeDtypeStruct(weight.shape, BF if earlier else F32),
            jax.ShapeDtypeStruct(mixed.shape, BF),
        ),
        compiler_params=pltpu.CompilerParams(vmem_limit_bytes=32 << 20),
        cost_estimate=SMALL,
        name="branch_gradients",
    )(*operands)


def feed_back_kernel(dgate_ref, dup_ref, source, kept_ref, sent_ref, whole, sems):
    hidden = dgate_ref.shape[1]

    def use(cut):
        cols = slice(*cut)
        total = dot(dgate_ref[...], whole[cols, :hidden], NT)
        total = (total + dot(dup_ref[...], whole[cols, hidden:], NT)).astype(BF)

        @pl.when(pl.program_id(0) < pl.num_programs(0) // 2)
        def _():
            kept_ref[:, cols] = total

        @pl.when(pl.program_id(0) >= pl.num_programs(0) // 2)
        def _():
            sent_ref[:, cols] = total

    stream(source, whole, sems, thirds(whole.shape[0]), use, 0)


def feed_back(first, rows, dgate, dup, gate_up):
    width, hidden = gate_up.shape[0], dgate.shape[1]
    block = 256
    steps = rows // block
    skip = first // block
    part = pl.BlockSpec((block, hidden), lambda i: (i + skip, 0))
    return kernel_call(
        feed_back_kernel,
        grid=(steps,),
        in_specs=[part, part, pl.BlockSpec(memory_space=pl.ANY)],
        out_specs=[
            pl.BlockSpec((block, width), lambda i: (jnp.minimum(i, steps // 2 - 1), 0)),
            pl.BlockSpec((block, width), lambda i: (jnp.maximum(i - steps // 2, 0), 0)),
        ],
        out_shape=(jax.ShapeDtypeStruct((rows // 2, width), BF),) * 2,
        scratch_shapes=[pltpu.VMEM(gate_up.shape, BF), pltpu.SemaphoreType.DMA((3,))],
        compiler_params=pltpu.CompilerParams(vmem_limit_bytes=40 << 20),
        cost_estimate=SMALL,
        name="feed_back",
    )(dgate, dup, gate_up)


class Shards:
    def __init__(self, count):
        self.count = count
        self.half = count // 2
        index = lax.axis_index("shard").astype(jnp.int32)
        hi, lo = index // 2, index % 2
        mine = [(hi ^ k) * 2 + lo for k in range(self.half)]
        partner = [(hi ^ k) * 2 + (1 - lo) for k in range(self.half)]
        self.places = jnp.stack(mine + partner)
        owner = jnp.arange(count, dtype=jnp.int32)
        self.slots = (owner // 2 ^ hi) + self.half * (owner % 2 ^ lo)

    def far(self, value, k):
        return lax.ppermute(
            value, "shard", [(i, ((i // 2) ^ k) * 2 + i % 2) for i in range(self.count)]
        )

    def near(self, value):
        return lax.ppermute(value, "shard", [(i, i ^ 1) for i in range(self.count)])


def tp_swap(value, mask):
    return lax.ppermute(value, "tp", [(i, i ^ mask) for i in range(4)])


def local(count, tokens, w_query, w_keyval, w_out, w_gate, w_up, w_down, gain_attn, gain_mlp, cotangent):
    rows, width = tokens.shape[0], tokens.shape[2]
    tp = lax.axis_index("tp").astype(jnp.int32)
    core, chip = tp % 2, tp // 2
    first_core = core == 0
    chip_table = jnp.reshape(chip, (1,))
    shards = Shards(count)

    def in_order(own, other):
        return jnp.where(
            first_core, jnp.concatenate([own, other], 0), jnp.concatenate([other, own], 0)
        )

    gain_one = gain_attn.astype(BF).astype(F32)[:, None]
    gain_two = gain_mlp.astype(BF).astype(F32)[:, None]
    own_query = w_query.astype(BF).astype(F32)
    own_keyval = w_keyval.astype(BF).astype(F32)
    own_gate = w_gate.astype(BF).astype(F32)
    own_up = w_up.astype(BF).astype(F32)
    keyval_half = jnp.where(first_core, own_keyval[:, :HD], own_keyval[:, HD:])
    send_in = (jnp.concatenate([own_query, keyval_half], 1) * gain_one).astype(BF)
    send_out = jnp.transpose(w_out).astype(BF)
    send_gate_up = (jnp.concatenate([own_gate, own_up], 1) * gain_two).astype(BF)
    send_down = jnp.transpose(w_down).astype(BF)

    heads = GROUP * HD
    half_count = shards.half
    places = shards.places
    part = half_count // 2
    token = places

    def sync(*values):
        nonlocal token
        token, *values = lax.optimization_barrier((token, *values))
        return values

    def far_all(piece):
        return [shards.far(piece, k) for k in range(1, half_count)]

    def rows_of(value, other):
        return lax.dynamic_slice_in_dim(value, (core ^ other) * rows, rows, 0)

    inputs = tokens.reshape(rows, width).astype(F32)
    scale_one = lax.rsqrt(jnp.mean(inputs * inputs, axis=-1, keepdims=True) + EPS)
    unit_own = (inputs * scale_one).astype(BF)
    far_in = far_all(send_in)
    unit_other = tp_swap(unit_own, 1)
    cot = cotangent.reshape(4, rows, width)
    cots = [lax.dynamic_index_in_dim(cot, tp ^ k, 0, keepdims=False) for k in range(4)]
    send_in, send_out, send_down, send_gate_up, unit_other, *pieces = sync(
        send_in, send_out, send_down, send_gate_up, unit_other, *cots, *far_in
    )
    cots, far_in = pieces[:4], pieces[4:]
    gate_up_full = lax.all_gather(send_gate_up, "shard", axis=0, tiled=True)

    far_out = far_all(send_out)
    far_in = pack([send_in] + far_in, send_in.shape[1])
    near_in = shards.near(far_in)
    query_far_b = tp_swap(far_in[:, :heads], 2)
    unit = in_order(unit_own, unit_other)
    unit, query_far_b, near_in, far_in, *far_out = sync(
        unit, query_far_b, near_in, far_in, *far_out
    )

    in_full = unpack(places, far_in, near_in, half_count)
    in_query = in_full[:, :heads]
    scale = HD ** (-0.5)
    column = lax.broadcasted_iota(jnp.int32, (1, in_full.shape[1]), 1)
    query_half = (
        dot(unit, in_full) * jnp.where(column < heads, scale * LOG2E, 1.0)
    ).astype(BF)
    half, query_half, in_query, query_near, *far_out = sync(
        query_half[:, heads:], query_half, in_query, near_in[:, :heads], *far_out
    )

    half_other = tp_swap(half, 1)
    before = lax.ppermute(half, "tp", [(0, 2), (1, 3)])
    far_out = pack([send_out] + far_out, heads)
    near_out = shards.near(far_out)
    half, half_other, before, far_out, query_near = sync(
        half, half_other, before, far_out, query_near
    )

    query_near_b = tp_swap(query_near, 2)
    before_other = tp_swap(before, 1)
    own_pair = jnp.concatenate([before, half], 0)
    other_pair = jnp.concatenate([before_other, half_other], 0)
    keys = jnp.where(first_core, own_pair, other_pair)
    values = jnp.where(first_core, other_pair, own_pair)
    keys_t = jnp.transpose(keys)
    values_t = jnp.transpose(values)
    mixed_a, lse_a = forward_attention(chip_table, query_half, keys, values_t)
    mixed_a, query_near_b, far_out, near_out, send_down = sync(
        mixed_a, query_near_b, far_out, near_out, send_down
    )

    down_full = lax.all_gather(send_down, "shard", axis=0, tiled=True)
    out_far_b = tp_swap(far_out, 2)
    in_query_b = unpack(places, query_far_b, query_near_b, half_count)
    query_b = (dot(unit, in_query_b) * (scale * LOG2E)).astype(BF)
    mixed_b, lse_b = forward_attention(chip_table, query_b, keys, values_t)
    mixed_a, mixed_b, out_far_b, near_out = sync(mixed_a, mixed_b, out_far_b, near_out)

    out_near_b = tp_swap(near_out, 2)
    out_full = unpack(places, far_out, near_out, half_count)
    branch_other = dot(rows_of(mixed_a, 1), out_full, NT)
    branch_own = dot(rows_of(mixed_a, 0), out_full, NT)
    branch_other, branch_own, mixed_b, out_near_b = sync(
        branch_other, branch_own, mixed_b, out_near_b
    )

    out_full_b = unpack(places, out_far_b, out_near_b, half_count)
    branch_other = (branch_other + dot(rows_of(mixed_b, 1), out_full_b, NT)).astype(BF)
    branch_came = tp_swap(branch_other, 1)
    branch_own = branch_own + dot(rows_of(mixed_b, 0), out_full_b, NT)
    hidden = inputs + (branch_own + branch_came.astype(F32))
    scale_two = lax.rsqrt(jnp.mean(hidden * hidden, axis=-1, keepdims=True) + EPS)
    norm_own = (hidden * scale_two).astype(BF)
    (norm_own,) = sync(norm_own)

    cut = rows // 2
    norm_core = tp_swap(norm_own, 1)
    norm_x1 = tp_swap(norm_own[:cut], 2)
    norm_own, norm_core, norm_x1 = sync(norm_own, norm_core, norm_x1)
    norms = [norm_own, norm_core]

    norm_x2 = tp_swap(norm_own[cut:], 2)
    norm_d1 = tp_swap(norm_x1, 1)
    product, to_gate, to_up = apply_gate_up(norms, gate_up_full)
    norm_x1, norm_x2, norm_d1, product, to_gate, to_up = sync(
        norm_x1, norm_x2, norm_d1, product, to_gate, to_up
    )

    norm_d2 = tp_swap(norm_x2, 1)
    norms += [norm_x1, norm_x2, norm_d1, norm_d2]
    product, to_gate, to_up = apply_gate_up(norms[2:], gate_up_full, product, to_gate, to_up)
    kept_down, sent_down = weight_gradient(shards.slots, cots, product)
    product, to_gate, to_up, *pieces = sync(product, to_gate, to_up, *sent_down, *cots)
    sent_down, cots = pieces[:2], pieces[2:]

    came_down = [shards.near(sent_down[0])]
    down_parts = [
        dot(product[at * rows : (at + 1) * rows], down_full, NT).astype(BF) for at in (3, 2, 1, 0)
    ][::-1]
    down_diagonal = tp_swap(down_parts[3], 1)
    dgate, dup = product_gradient(cots, after(to_gate, *down_parts), to_up, down_full)
    down_far = combine(down_parts[2], down_diagonal)
    dgate, dup, *pieces = sync(dgate, dup, sent_down[1], *down_parts, *down_far, *came_down)
    sent, down_parts, down_far, came_down = pieces[0], pieces[1:5], pieces[5:7], pieces[7:]

    others = [k for k in range(1, half_count) if k != part]
    came_down.append(shards.near(sent))
    down_came = [tp_swap(down_far[0], 2)]
    sums_down = list(fold(kept_down[0], came_down[0], part))
    far_sums = [shards.far(sums_down[0], part)]
    kept_gate, sent_gate = weight_gradient(shards.slots, norms, dgate)
    back_x, back_diagonal = feed_back(2 * rows, 2 * rows, dgate, dup, gate_up_full)
    dgate, dup, back_x, back_diagonal, came_down[1], *pieces = sync(
        dgate, dup, back_x, back_diagonal, came_down[1],
        *sent_gate, *down_came, *far_sums, *sums_down, *norms
    )
    sent_gate, down_came, far_sums, sums_down, norms = (
        pieces[:2],
        pieces[2:3],
        pieces[3:4],
        pieces[4 : 4 + part],
        pieces[4 + part :],
    )

    came_gate = [shards.near(sent_gate[0])]
    sums_down = list(fold(kept_down[1], came_down[1], part)) + sums_down
    far_sums += [shards.far(sums_down[k], k) for k in others]
    back_far = combine(back_x, tp_swap(back_diagonal, 1))
    back_came = [tp_swap(back_far[0], 2)]
    kept_up, sent_up = weight_gradient(shards.slots, norms, after(dup, *back_far))
    dgate, dup, *pieces = sync(
        dgate, dup, sent_gate[1], back_far[1], *back_came, *came_gate, *sent_up, *far_sums
    )
    sent, back_far, back_came, came_gate, sent_up, far_sums_down = (
        pieces[0],
        pieces[1],
        pieces[2:3],
        pieces[3:4],
        pieces[4:6],
        pieces[6:],
    )

    came_gate.append(shards.near(sent))
    sums_gate = list(fold(kept_gate[0], came_gate[0], part))
    far_sums = [shards.far(sums_gate[0], part)]
    back_came.append(tp_swap(back_far, 2))
    back_own, back_core = feed_back(0, 2 * rows, dgate, dup, gate_up_full)
    back_own, back_core, came_gate[1], down_far[1], *pieces = sync(
        back_own, back_core, came_gate[1], down_far[1], *back_came, *sent_up, *far_sums, *sums_gate
    )
    back_came, sent_up, far_sums, sums_gate = pieces[:2], pieces[2:4], pieces[4:5], pieces[5:]

    came_up = [shards.near(sent_up[0])]
    sums_gate = list(fold(kept_gate[1], came_gate[1], part)) + sums_gate
    far_sums += [shards.far(sums_gate[k], k) for k in others]
    down_came.append(tp_swap(down_far[1], 2))
    back_core = tp_swap(back_core, 1)
    grad_norm = (
        back_own.astype(F32)
        + back_core.astype(F32)
        + jnp.concatenate(back_came, 0).astype(F32)
    )
    unit_two = hidden * scale_two
    grad_hidden = cots[0].astype(F32) + scale_two * (
        grad_norm - unit_two * jnp.mean(grad_norm * unit_two, axis=-1, keepdims=True)
    )
    branch_own = grad_hidden.astype(BF)
    branch_other = tp_swap(branch_own, 1)
    g_own, grad_own = branch_gradients(branch_own, rows_of(mixed_b, 0), out_full_b)
    branch_other = after(branch_other, g_own, grad_own)
    g_out_b, grad_other = branch_gradients(branch_other, rows_of(mixed_b, 1), out_full_b, g_own)
    grad_mixed_b = in_order(grad_own, grad_other)
    grad_mixed_b, g_out_b, branch_own, branch_other, sent, *pieces = sync(
        grad_mixed_b, g_out_b, branch_own, branch_other, sent_up[1], *came_up, *down_came, *far_sums
    )
    came_up, down_came, far_sums_gate = pieces[:1], pieces[1:3], pieces[3:]

    came_up.append(shards.near(sent))
    sums_up = list(fold(kept_up[0], came_up[0], part))
    far_sums = [shards.far(sums_up[0], part)]
    g_out_came = tp_swap(g_out_b, 2)
    dq_b, dk_b, dv_b = backward_attention(
        chip_table, query_b, grad_mixed_b, mixed_b, lse_b, keys, keys_t, values
    )
    dq_b, dk_b, dv_b, g_out_came, branch_own, branch_other, came_up[1], *pieces = sync(
        dq_b, dk_b, dv_b, g_out_came, branch_own, branch_other, came_up[1], *far_sums, *sums_up
    )
    far_sums, sums_up = pieces[:1], list(fold(kept_up[1], came_up[1], part)) + pieces[1:]

    g_query_b = dot(unit, dq_b, TN).astype(BF)
    g_out = (
        dot(branch_own, rows_of(mixed_a, 0), TN)
        + dot(branch_other, rows_of(mixed_a, 1), TN)
        + g_out_came.astype(F32)
    )
    (kept_out,), (sent_out,) = split(places, g_out.astype(BF), half_count)
    grad_mixed_a = in_order(
        dot(branch_own, out_full).astype(BF), dot(branch_other, out_full).astype(BF)
    )
    g_query_b, sent_out, grad_mixed_a, kept_out, *sums_up = sync(
        g_query_b, sent_out, grad_mixed_a, kept_out, *sums_up
    )

    g_query_came = tp_swap(g_query_b, 2)
    far_sums += [shards.far(sums_up[k], k) for k in others]
    came_out = shards.near(sent_out)
    dq_a, dk_a, dv_a = backward_attention(
        chip_table, query_half, grad_mixed_a, mixed_a, lse_a, keys, keys_t, values
    )
    dq_a, dk_a, dv_a, g_query_came, came_out, *far_sums_up = sync(
        dq_a, dk_a, dv_a, g_query_came, came_out, *far_sums
    )

    grad_keys = (dk_a + dk_b) * LN2
    grad_values = dv_a + dv_b
    mine = jnp.where(first_core, grad_keys, grad_values)
    theirs = jnp.where(first_core, grad_values, grad_keys).astype(BF)
    theirs = tp_swap(theirs, 1)
    g_query = (dot(unit, dq_a, TN) + g_query_came.astype(F32)).astype(BF)
    (kept_query,), (sent_query,) = split(places, g_query, half_count)
    sums_out = fold(kept_out, came_out, half_count)
    mine = mine + theirs.astype(F32)
    chip_rows = mine.shape[0] // 2
    mine, own = mine[chip_rows:], mine[:chip_rows].astype(BF)
    mine, own, sent_query, dq_a, dq_b, *pieces = sync(
        mine, own, sent_query, dq_a, dq_b, *sums_out, *far_sums_gate, *far_sums_up, *far_sums_down
    )
    sums_out, pieces = pieces[:half_count], pieces[half_count:]
    far_sums_gate, far_sums_up, far_sums_down = (
        pieces[at * (half_count - 1) : (at + 1) * (half_count - 1)] for at in range(3)
    )

    def total(own, others):
        return functools.reduce(lambda t, o: t + o.astype(F32), others, own.astype(F32))

    earlier = lax.ppermute(own, "tp", [(2, 0), (3, 1)])
    came_query = shards.near(sent_query)
    far_out_sums = [shards.far(sums_out[k], k) for k in range(1, half_count)]
    back_own, back_other = query_back(jnp.reshape(core, (1,)), dq_a, dq_b, in_query, in_query_b)
    down_core = tp_swap(down_parts[1], 1)
    sum_gate = total(sums_gate[0], far_sums_gate)
    sum_up = total(sums_up[0], far_sums_up)
    grad_w_gate = sum_gate * gain_two
    grad_w_up = sum_up * gain_two
    gain_two_part = jnp.sum(own_gate * sum_gate + own_up * sum_up, axis=1)
    back_own, back_other, earlier, came_query, down_core, grad_w_gate, grad_w_up, gain_two_part, *far_out_sums = sync(
        back_own, back_other, earlier, came_query, down_core, grad_w_gate, grad_w_up, gain_two_part, *far_out_sums
    )

    grad_half = (mine + earlier.astype(F32)).astype(BF)
    g_half = dot(unit, grad_half, TN).astype(BF)
    (kept_half,), (sent_half,) = split(places, g_half, half_count)
    sums_query = fold(kept_query, came_query, half_count)
    in_half = in_full[:, heads:]
    back_other = (back_other + dot(rows_of(grad_half, 1), in_half, NT)).astype(BF)
    back_own = back_own + dot(rows_of(grad_half, 0), in_half, NT)
    back_other, back_own, kept_half, sent_half, *sums_query = sync(
        back_other, back_own, kept_half, sent_half, *sums_query
    )

    came_half = shards.near(sent_half)
    back_came = tp_swap(back_other, 1)
    far_query = [shards.far(sums_query[k], k) for k in range(1, half_count)]
    grad_tokens = token_gradient(back_own, back_came, tokens.reshape(rows, width), grad_hidden)
    grad_w_down = jnp.transpose(total(sums_down[0], far_sums_down))
    grad_w_out = jnp.transpose(total(sums_out[0], far_out_sums))
    output = (
        hidden
        + down_parts[0].astype(F32)
        + down_core.astype(F32)
        + jnp.concatenate(down_came, 0).astype(F32)
    ).astype(BF)
    came_half, grad_tokens, output, *far_query = sync(came_half, grad_tokens, output, *far_query)

    sums_half = fold(kept_half, came_half, half_count)
    far_half = [shards.far(sums_half[k], k) for k in range(1, half_count)]

    sum_query = total(sums_query[0], far_query)
    sum_half = total(sums_half[0], far_half)

    gain_one_part = jnp.sum(own_query * sum_query, axis=1) + jnp.sum(keyval_half * sum_half, axis=1)
    small = jnp.concatenate(
        [jnp.transpose(sum_half), gain_one_part[None], gain_two_part[None], jnp.zeros((6, sum_half.shape[0]), F32)], 0
    )
    small = small + tp_swap(small, 2)
    other = tp_swap(small, 1)
    gains = small[HD : HD + 2] + other[HD : HD + 2]
    sum_half = jnp.transpose(small[:HD])
    half_swapped = jnp.transpose(other[:HD])
    grad_w_keyval = (
        jnp.where(
            first_core,
            jnp.concatenate([sum_half, half_swapped], 1),
            jnp.concatenate([half_swapped, sum_half], 1),
        )
        * gain_one
    )
    return (
        output.reshape(rows, 1, width),
        grad_tokens,
        sum_query * gain_one,
        grad_w_keyval,
        grad_w_out,
        grad_w_gate,
        grad_w_up,
        grad_w_down,
        gains[0],
        gains[1],
    )


def solution(mesh):
    in_specs = (
        P("tp", "shard", None),
        P("shard", "tp"),
        P("shard", None),
        P("tp", "shard"),
        P("shard", "tp"),
        P("shard", "tp"),
        P("tp", "shard"),
        P("shard"),
        P("shard"),
        P(None, "shard", None),
    )
    out_specs = (
        P("tp", "shard", None),
        P("tp", "shard", None),
        P("shard", "tp"),
        P("shard", None),
        P("tp", "shard"),
        P("shard", "tp"),
        P("shard", "tp"),
        P("tp", "shard"),
        P("shard"),
        P("shard"),
    )
    return jax.shard_map(
        functools.partial(local, mesh.shape["shard"]),
        mesh=mesh,
        in_specs=in_specs,
        out_specs=out_specs,
        check_vma=False,
    )
```

```python
import functools

import jax
import jax.numpy as jnp
from jax import lax
from jax.experimental import pallas as pl
from jax.experimental.pallas import tpu as pltpu
from jax.sharding import PartitionSpec as P

HD = 128
WINDOW = 1024
QB = 256
GROUP = 3
EPS = 1e-06
LOG2E = 1.4426950408889634
LN2 = 0.6931471805599453
NEG = -1e30
LARGE = 1 << 20
OUT = pltpu.HBM
SMALL = pl.CostEstimate(flops=0, transcendentals=0, bytes_accessed=0)
BF = jnp.bfloat16
F32 = jnp.float32
NT = (((1,), (1,)), ((), ()))
TN = (((0,), (0,)), ((), ()))
NN = (((1,), (0,)), ((), ()))


def dot(a, b, dims=NN):
    return lax.dot_general(a, b, dims, preferred_element_type=F32)


def after(value, *others):
    return lax.optimization_barrier((value, *others))[0]


def kernel_call(*args, **kwargs):
    call = pl.pallas_call(*args, **kwargs)

    def run(*operands):
        return call(
            *(
                pltpu.with_memory_space_constraint(x, pltpu.HBM) if x.size > LARGE else x
                for x in operands
            )
        )

    return run


def forward_attention_kernel(chip_ref, q_ref, k_ref, vt_ref, o_ref, lse_ref):
    block = pl.program_id(0)
    chunks = WINDOW // QB
    key_row = lax.broadcasted_iota(jnp.int32, (QB, QB), 0)
    query_col = lax.broadcasted_iota(jnp.int32, (QB, QB), 1)

    def rows_of(chunk):
        return pl.ds(pl.multiple_of((block + chunk) * QB, QB), QB)

    def finish(head, top, total, mixed):
        cols = slice(head * HD, (head + 1) * HD)
        o_ref[:, cols] = jnp.transpose(mixed / total).astype(BF)
        lse_ref[head : head + 1, :] = top + jnp.log(total) * LOG2E

    def attend(first):
        for head in range(GROUP):
            query = q_ref[:, head * HD : (head + 1) * HD]
            scores = {}
            for chunk in range(first, chunks + 1):
                scores[chunk] = dot(k_ref[rows_of(chunk), :], query, NT)
                if chunk == 0:
                    scores[chunk] = jnp.where(key_row > query_col, scores[chunk], NEG)
                if chunk == chunks:
                    scores[chunk] = jnp.where(key_row <= query_col, scores[chunk], NEG)
            top = functools.reduce(jnp.maximum, scores.values())
            top = jnp.max(top, axis=0, keepdims=True)
            total = jnp.zeros((1, QB), F32)
            mixed = jnp.zeros((HD, QB), F32)
            for chunk, part in scores.items():
                probs = jnp.exp2(part - top)
                total = total + jnp.sum(probs, axis=0, keepdims=True)
                mixed = mixed + dot(vt_ref[:, rows_of(chunk)], probs.astype(BF))
            finish(head, top, total, mixed)

    pl.when(chip_ref[0] != 0)(functools.partial(attend, 0))
    for at in range(chunks):
        pl.when((chip_ref[0] == 0) & (block == at))(functools.partial(attend, chunks - at))


def forward_attention(chip, query, keys, values_t):
    rows = query.shape[0]
    width = GROUP * HD
    return kernel_call(
        forward_attention_kernel,
        grid_spec=pltpu.PrefetchScalarGridSpec(
            num_scalar_prefetch=1,
            grid=(rows // QB,),
            in_specs=[
                pl.BlockSpec((QB, width), lambda b, s: (b, 0)),
                pl.BlockSpec((2 * rows, HD), lambda b, s: (0, 0)),
                pl.BlockSpec((HD, 2 * rows), lambda b, s: (0, 0)),
            ],
            out_specs=[
                pl.BlockSpec((QB, width), lambda b, s: (b, 0)),
                pl.BlockSpec((8, QB), lambda b, s: (0, b)),
            ],
        ),
        out_shape=(
            jax.ShapeDtypeStruct((rows, width), BF),
            jax.ShapeDtypeStruct((8, rows), F32),
        ),
        compiler_params=pltpu.CompilerParams(vmem_limit_bytes=40 << 20),
        cost_estimate=SMALL,
        name="attention_forward",
    )(chip, query, keys, values_t)


def backward_attention_kernel(
    chip_ref, q_ref, g_ref, o_ref, lse_ref, k_ref, kt_ref, v_ref, dq_ref, dk_ref, dv_ref
):
    block = pl.program_id(0)
    chunks = WINDOW // QB
    key_row = lax.broadcasted_iota(jnp.int32, (QB, QB), 0)
    query_col = lax.broadcasted_iota(jnp.int32, (QB, QB), 1)

    @pl.when(block == 0)
    def _():
        dk_ref[...] = jnp.zeros_like(dk_ref)
        dv_ref[...] = jnp.zeros_like(dv_ref)

    def rows_of(chunk):
        return pl.ds(pl.multiple_of((block + chunk) * QB, QB), QB)

    deltas = []
    for head in range(GROUP):
        cols = slice(head * HD, (head + 1) * HD)
        both = g_ref[:, cols].astype(F32) * o_ref[:, cols].astype(F32)
        deltas.append(jnp.sum(jnp.transpose(both), axis=0, keepdims=True))

    def one_chunk(chunk, keep, totals):
        rows = rows_of(chunk)
        keys = k_ref[rows, :]
        values = v_ref[rows, :]
        keys_t = kt_ref[:, rows]
        grad_keys = jnp.zeros((QB, HD), F32)
        grad_values = jnp.zeros((QB, HD), F32)
        new = []
        for head in range(GROUP):
            cols = slice(head * HD, (head + 1) * HD)
            query = q_ref[:, cols]
            grad = g_ref[:, cols]
            probs = jnp.exp2(dot(keys, query, NT) - lse_ref[head : head + 1, :])
            if keep is not None:
                probs = jnp.where(keep, probs, 0.0)
            grad_scores = (probs * (dot(values, grad, NT) - deltas[head])).astype(BF)
            grad_values = grad_values + dot(probs.astype(BF), grad)
            grad_keys = grad_keys + dot(grad_scores, query)
            new.append(totals[head] + dot(keys_t, grad_scores))
        dk_ref[rows, :] += grad_keys
        dv_ref[rows, :] += grad_values
        return tuple(new)

    def finish(totals):
        for head in range(GROUP):
            cols = slice(head * HD, (head + 1) * HD)
            dq_ref[:, cols] = (jnp.transpose(totals[head]) * HD ** (-0.5)).astype(BF)

    zeros = tuple(jnp.zeros((HD, QB), F32) for _ in range(GROUP))

    @pl.when(chip_ref[0] != 0)
    def _():
        totals = zeros
        for chunk in range(chunks + 1):
            keep = None
            if chunk == 0:
                keep = key_row > query_col
            if chunk == chunks:
                keep = key_row <= query_col
            totals = one_chunk(chunk, keep, totals)
        finish(totals)

    @pl.when(chip_ref[0] == 0)
    def _():
        def step(chunk, totals):
            return one_chunk(chunk, (key_row <= query_col) | (chunk < chunks), totals)

        finish(lax.fori_loop(chunks - block, chunks + 1, step, zeros))


def backward_attention(chip, query, grad, mixed, lse, keys, keys_t, values):
    rows = query.shape[0]
    width = GROUP * HD
    wide = pl.BlockSpec((QB, width), lambda b, s: (b, 0))
    whole = pl.BlockSpec((2 * rows, HD), lambda b, s: (0, 0))
    return kernel_call(
        backward_attention_kernel,
        grid_spec=pltpu.PrefetchScalarGridSpec(
            num_scalar_prefetch=1,
            grid=(rows // QB,),
            in_specs=[
                wide,
                wide,
                wide,
                pl.BlockSpec((8, QB), lambda b, s: (0, b)),
                whole,
                pl.BlockSpec((HD, 2 * rows), lambda b, s: (0, 0)),
                whole,
            ],
            out_specs=[wide, whole, whole],
        ),
        out_shape=(
            jax.ShapeDtypeStruct((rows, width), BF),
            jax.ShapeDtypeStruct((2 * rows, HD), F32),
            jax.ShapeDtypeStruct((2 * rows, HD), F32),
        ),
        compiler_params=pltpu.CompilerParams(vmem_limit_bytes=40 << 20),
        cost_estimate=SMALL,
        name="attention_backward",
    )(chip, query, grad, mixed, lse, keys, keys_t, values)


def pack_kernel(*refs):
    packed = refs[-1]
    depth, width = refs[0].shape[0], packed.shape[1]
    for i, piece in enumerate(refs[:-1]):
        packed[pl.ds(i * depth, depth), :] = piece[:, :width]


def pack(pieces, width):
    depth = pieces[0].shape[0]
    rows = depth * len(pieces)
    return kernel_call(
        pack_kernel,
        grid=(1,),
        in_specs=[pl.BlockSpec(piece.shape, lambda i: (0, 0)) for piece in pieces],
        out_specs=pl.BlockSpec((rows, width), lambda i: (0, 0)),
        out_shape=jax.ShapeDtypeStruct((rows, width), BF),
        compiler_params=pltpu.CompilerParams(vmem_limit_bytes=16 << 20),
        cost_estimate=SMALL,
        name="pack_pieces",
    )(*pieces)


def unpack_kernel(half, place_ref, far, near, whole):
    depth = far.shape[0] // half
    for i in range(half):
        rows = pl.ds(i * depth, depth)
        whole[pl.ds(pl.multiple_of(place_ref[i] * depth, depth), depth), :] = far[rows, :]
        whole[pl.ds(pl.multiple_of(place_ref[half + i] * depth, depth), depth), :] = near[rows, :]


def unpack(places, far, near, half):
    rows, width = far.shape
    packed = pl.BlockSpec((rows, width), lambda i, s: (0, 0))
    return kernel_call(
        functools.partial(unpack_kernel, half),
        grid_spec=pltpu.PrefetchScalarGridSpec(
            num_scalar_prefetch=1,
            grid=(1,),
            in_specs=[packed, packed],
            out_specs=pl.BlockSpec((2 * rows, width), lambda i, s: (0, 0)),
        ),
        out_shape=jax.ShapeDtypeStruct((2 * rows, width), BF),
        compiler_params=pltpu.CompilerParams(vmem_limit_bytes=16 << 20),
        cost_estimate=SMALL,
        name="unpack_pieces",
    )(places, far, near)


def split_kernel(groups, half, place_ref, whole, *refs):
    depth = refs[0].shape[0] // len(groups[0])
    for group, kept, sent in zip(groups, refs[: len(groups)], refs[len(groups) :]):
        for at, i in enumerate(group):
            rows = pl.ds(at * depth, depth)
            kept[rows, :] = whole[pl.ds(pl.multiple_of(place_ref[i] * depth, depth), depth), :]
            sent[rows, :] = whole[
                pl.ds(pl.multiple_of(place_ref[half + i] * depth, depth), depth), :
            ]


def split(places, whole, half, parts=1):
    size = half // parts
    groups = [range(half - (p + 1) * size, half - p * size) for p in range(parts)]
    rows, width = whole.shape[0] // (2 * parts), whole.shape[1]
    out = pl.BlockSpec((rows, width), lambda i, s: (0, 0))
    pieces = kernel_call(
        functools.partial(split_kernel, groups, half),
        grid_spec=pltpu.PrefetchScalarGridSpec(
            num_scalar_prefetch=1,
            grid=(1,),
            in_specs=[pl.BlockSpec(whole.shape, lambda i, s: (0, 0))],
            out_specs=[out] * (2 * parts),
        ),
        out_shape=(jax.ShapeDtypeStruct((rows, width), whole.dtype),) * (2 * parts),
        compiler_params=pltpu.CompilerParams(vmem_limit_bytes=24 << 20),
        cost_estimate=SMALL,
        name="split_pieces",
    )(places, whole)
    return pieces[:parts], pieces[parts:]


def fold_kernel(kept, came, *pieces):
    depth = pieces[0].shape[0]
    for i, piece in enumerate(pieces):
        rows = pl.ds(i * depth, depth)
        piece[...] = (kept[rows, :].astype(F32) + came[rows, :].astype(F32)).astype(BF)


def fold(kept, came, half):
    rows, width = kept.shape
    depth = rows // half
    whole = pl.BlockSpec((rows, width), lambda i: (0, 0))
    return kernel_call(
        fold_kernel,
        grid=(1,),
        in_specs=[whole, whole],
        out_specs=[pl.BlockSpec((depth, width), lambda i: (0, 0))] * half,
        out_shape=(OUT((depth, width), BF),) * half,
        compiler_params=pltpu.CompilerParams(vmem_limit_bytes=24 << 20),
        cost_estimate=SMALL,
        name="fold_pieces",
    )(kept, came)


def token_gradient_kernel(own_ref, came_ref, token_ref, through_ref, out_ref):
    grad = own_ref[...] + came_ref[...].astype(F32)
    unit = token_ref[...].astype(F32)
    scale = lax.rsqrt(jnp.mean(unit * unit, axis=-1, keepdims=True) + EPS)
    unit = unit * scale
    inner = jnp.mean(grad * unit, axis=-1, keepdims=True)
    out_ref[:, 0, :] = through_ref[...] + scale * (grad - unit * inner)


def token_gradient(own, came, tokens, through):
    rows, width = own.shape
    block = 128
    part = pl.BlockSpec((block, width), lambda i: (i, 0))
    return kernel_call(
        token_gradient_kernel,
        grid=(rows // block,),
        in_specs=[part] * 4,
        out_specs=pl.BlockSpec((block, 1, width), lambda i: (i, 0, 0)),
        out_shape=jax.ShapeDtypeStruct((rows, 1, width), F32),
        compiler_params=pltpu.CompilerParams(vmem_limit_bytes=24 << 20),
        cost_estimate=SMALL,
        name="token_gradient",
    )(*in_memory(own, came, tokens, through))


def query_back_kernel(core_ref, a_ref, b_ref, weight_a_ref, weight_b_ref, own_ref, other_ref):
    rows = own_ref.shape[0]
    for out, core in ((other_ref, 1 - core_ref[0]), (own_ref, core_ref[0])):
        place = pl.ds(pl.multiple_of(core * rows, rows), rows)
        total = dot(a_ref[place, :], weight_a_ref[...], NT)
        out[...] = total + dot(b_ref[place, :], weight_b_ref[...], NT)


def query_back(core, a, b, weight_a, weight_b):
    rows, width = a.shape[0] // 2, weight_a.shape[0]
    whole = [pl.BlockSpec(x.shape, lambda i, s: (0, 0)) for x in (a, b, weight_a, weight_b)]
    return kernel_call(
        query_back_kernel,
        grid_spec=pltpu.PrefetchScalarGridSpec(
            num_scalar_prefetch=1,
            grid=(1,),
            in_specs=whole,
            out_specs=[pl.BlockSpec((rows, width), lambda i, s: (0, 0))] * 2,
        ),
        out_shape=(jax.ShapeDtypeStruct((rows, width), F32),) * 2,
        compiler_params=pltpu.CompilerParams(vmem_limit_bytes=36 << 20),
        cost_estimate=SMALL,
        name="query_back",
    )(core, a, b, weight_a, weight_b)


def in_memory(*operands):
    return [pltpu.with_memory_space_constraint(x, pltpu.HBM) for x in operands]


def finish_gradients_kernel(count, *refs):
    gate, up = refs[:count], refs[count : 2 * count]
    own_gate_ref, own_up_ref, gain_ref, gate_ref, up_ref, part_ref = refs[2 * count :]
    gain = gain_ref[...]
    part = 0.0
    for pieces, own, out in ((gate, own_gate_ref, gate_ref), (up, own_up_ref, up_ref)):
        total = pieces[0][...].astype(F32)
        for piece in pieces[1:]:
            total = total + piece[...].astype(F32)
        out[...] = total * gain
        part = part + jnp.sum(own[...].astype(F32) * total, axis=1, keepdims=True)
    part_ref[...] = part


def finish_gradients(gate, up, own_gate, own_up, gain):
    operands = [*gate, *up, own_gate, own_up, gain]
    whole = [pl.BlockSpec(x.shape, lambda i: (0, 0)) for x in operands]
    return kernel_call(
        functools.partial(finish_gradients_kernel, len(gate)),
        grid=(1,),
        in_specs=whole,
        out_specs=[whole[0], whole[0], whole[-1]],
        out_shape=(
            OUT(own_gate.shape, F32),
            OUT(own_gate.shape, F32),
            jax.ShapeDtypeStruct(gain.shape, F32),
        ),
        compiler_params=pltpu.CompilerParams(vmem_limit_bytes=40 << 20),
        cost_estimate=SMALL,
        name="finish_gradients",
    )(*in_memory(*operands[:-1]), gain)


def finish_output_kernel(hidden_ref, own_ref, core_ref, *refs):
    first = 0
    for ref in refs[:-1]:
        rows = slice(first, first + ref.shape[0])
        total = hidden_ref[rows, :] + own_ref[rows, :].astype(F32) + core_ref[rows, :].astype(F32)
        refs[-1][rows, :] = (total + ref[...].astype(F32)).astype(BF)
        first += ref.shape[0]


def finish_output(hidden, own, core, *came):
    operands = (hidden, own, core, *came)
    whole = [pl.BlockSpec(x.shape, lambda i: (0, 0)) for x in operands]
    return kernel_call(
        finish_output_kernel,
        grid=(1,),
        in_specs=whole,
        out_specs=whole[0],
        out_shape=OUT(hidden.shape, BF),
        compiler_params=pltpu.CompilerParams(vmem_limit_bytes=40 << 20),
        cost_estimate=SMALL,
        name="finish_output",
    )(*in_memory(*operands))


def spans(parts, block):
    counts = [part.shape[0] // block for part in parts]
    return [(sum(counts[:i]), count) for i, count in enumerate(counts)]


def part_specs(parts, block, width):
    def spec(first, count):
        return pl.BlockSpec((block, width), lambda i: (jnp.clip(i - first, 0, count - 1), 0))

    return [spec(first, count) for first, count in spans(parts, block)]


def weight_gradient_kernel(half, slot_ref, *refs):
    part = half // 2
    outs, grad_ref, parts = refs[-4:], refs[-5], refs[:-5]
    depth = outs[0].shape[0] // part
    first = 0
    total = None
    for ref in parts:
        rows = ref.shape[0]
        term = dot(ref[...], grad_ref[first : first + rows, :], TN)
        total = term if total is None else total + term
        first += rows
    total = total.astype(BF)
    count = total.shape[0] // depth
    for at in range(count):
        slot = slot_ref[pl.program_id(0) * count + at]
        k = lax.rem(slot, half)
        target = 2 * (slot // half) + 1 - k // part
        place = pl.ds(pl.multiple_of(lax.rem(k, part) * depth, depth), depth)
        for i, ref in enumerate(outs):

            @pl.when(target == i)
            def _(ref=ref, place=place, at=at):
                ref[place, :] = total[at * depth : (at + 1) * depth, :]


def weight_gradient(slots, parts, grad):
    half = slots.shape[0] // 2
    width = parts[0].shape[1]
    hidden = grad.shape[1]
    block = 384
    pieces = kernel_call(
        functools.partial(weight_gradient_kernel, half),
        grid_spec=pltpu.PrefetchScalarGridSpec(
            num_scalar_prefetch=1,
            grid=(width // block,),
            in_specs=[pl.BlockSpec((part.shape[0], block), lambda i, s: (0, i)) for part in parts]
            + [pl.BlockSpec(grad.shape, lambda i, s: (0, 0), pipeline_mode=pl.Buffered(1))],
            out_specs=[pl.BlockSpec((width // 4, hidden), lambda i, s: (0, 0))] * 4,
        ),
        out_shape=(OUT((width // 4, hidden), BF),) * 4,
        compiler_params=pltpu.CompilerParams(vmem_limit_bytes=40 << 20),
        cost_estimate=SMALL,
        name="weight_gradient",
    )(slots, *parts, grad)
    return pieces[:2], pieces[2:]


def combine_kernel(a_ref, b_ref, *outs):
    first = 0
    for out in outs:
        rows = slice(first, first + out.shape[0])
        out[...] = (a_ref[rows, :].astype(F32) + b_ref[rows, :].astype(F32)).astype(BF)
        first += out.shape[0]


def combine(a, b):
    rows, width = a.shape
    whole = pl.BlockSpec((rows, width), lambda i: (0, 0))
    return kernel_call(
        combine_kernel,
        grid=(1,),
        in_specs=[whole, whole],
        out_specs=[pl.BlockSpec((rows // 2, width), lambda i: (0, 0))] * 2,
        out_shape=(jax.ShapeDtypeStruct((rows // 2, width), BF),) * 2,
        compiler_params=pltpu.CompilerParams(vmem_limit_bytes=16 << 20),
        cost_estimate=SMALL,
        name="combine",
    )(a, b)


def gelu_parts(gate):
    square = gate * gate
    t = jnp.tanh(gate * (0.7978845608028654 + 0.035677408136300125 * square))
    half = 0.5 + 0.5 * t
    value = gate * half
    slope = half + 0.5 * gate * (1.0 - t * t) * (0.7978845608028654 + 0.10703222440890037 * square)
    return value, slope


def stream(source, whole, sems, cuts, use, axis=1):
    def at(ref, cut):
        where = pl.ds(cut[0], cut[1] - cut[0])
        return ref.at[:, where] if axis else ref.at[where, :]

    copies = [
        pltpu.make_async_copy(at(source, cut), at(whole, cut), sems.at[i])
        for i, cut in enumerate(cuts)
    ]

    @pl.when(pl.program_id(0) == 0)
    def _():
        for copy in copies:
            copy.start()
        for cut, copy in zip(cuts, copies):
            copy.wait()
            use(cut)

    @pl.when(pl.program_id(0) > 0)
    def _():
        use((0, cuts[-1][1]))


def thirds(width):
    return [(i * width // 3, (i + 1) * width // 3) for i in range(3)]


def gate_up_block(norm_ref, whole, cut, product_ref, to_gate_ref, to_up_ref):
    hidden = product_ref.shape[1]
    cols = slice(*cut)
    gate = dot(norm_ref[...], whole[:, cols])
    up = dot(norm_ref[...], whole[:, hidden + cut[0] : hidden + cut[1]])
    value, slope = gelu_parts(gate)
    product_ref[:, cols] = (value * up).astype(BF)
    to_gate_ref[:, cols] = (up * slope).astype(BF)
    to_up_ref[:, cols] = value.astype(BF)


def gate_up_kernel(places, *refs):
    parts, source = refs[: len(places)], refs[len(places)]
    outs, whole, sems = refs[-5:-2], refs[-2], refs[-1]
    hidden = outs[0].shape[1]
    step = pl.program_id(0)
    cuts = thirds(hidden)
    copies = [
        [
            pltpu.make_async_copy(
                source.at[:, pl.ds(side + a, b - a)],
                whole.at[:, pl.ds(side + a, b - a)],
                sems.at[2 * i + side // hidden],
            )
            for side in (0, hidden)
        ]
        for i, (a, b) in enumerate(cuts)
    ]

    @pl.when(step == 0)
    def _():
        for pair in copies:
            for copy in pair:
                copy.start()
        for cut, pair in zip(cuts, copies):
            for copy in pair:
                copy.wait()
            gate_up_block(parts[0], whole, cut, *outs)

    for (first, count), ref in zip(places, parts):
        inside = (step > 0) & (step >= first) & (step < first + count)
        pl.when(inside)(functools.partial(gate_up_block, ref, whole, (0, hidden), *outs))


def apply_gate_up(parts, gate_up, *earlier):
    width, hidden = gate_up.shape[0], gate_up.shape[1] // 2
    block = 256
    places = spans(parts, block)
    steps = sum(count for _, count in places)
    skip = steps if earlier else 0
    out = pl.BlockSpec((block, hidden), lambda i: (i + skip, 0))
    anywhere = pl.BlockSpec(memory_space=pl.ANY)
    return kernel_call(
        functools.partial(gate_up_kernel, places),
        grid=(steps,),
        in_specs=part_specs(parts, block, width) + [anywhere] * (1 + len(earlier)),
        out_specs=[out, out, out],
        out_shape=(OUT((2 * steps * block, hidden), BF),) * 3,
        scratch_shapes=[pltpu.VMEM(gate_up.shape, BF), pltpu.SemaphoreType.DMA((6,))],
        input_output_aliases={len(parts) + 1 + i: i for i in range(len(earlier))},
        compiler_params=pltpu.CompilerParams(vmem_limit_bytes=40 << 20),
        cost_estimate=SMALL,
        name="gate_up_rest" if earlier else "gate_up_first",
    )(*parts, gate_up, *earlier)


def product_gradient_kernel(places, *refs):
    parts = refs[: len(places)]
    to_gate_ref, to_up_ref, source, dgate_ref, dup_ref, whole, sems = refs[len(places) :]
    at = pl.program_id(0)

    def use(cut):
        cols = slice(*cut)

        def block(cot_ref):
            grad = dot(cot_ref[...], whole[:, cols])
            dgate_ref[:, cols] = (grad * to_gate_ref[:, cols].astype(F32)).astype(BF)
            dup_ref[:, cols] = (grad * to_up_ref[:, cols].astype(F32)).astype(BF)

        if cut[1] - cut[0] < whole.shape[1]:
            block(parts[0])
        else:
            for (first, count), ref in zip(places, parts):
                pl.when((at >= first) & (at < first + count))(functools.partial(block, ref))

    stream(source, whole, sems, thirds(whole.shape[1]), use)


def product_gradient(parts, to_gate, to_up, down):
    rows, hidden = to_gate.shape
    block = 256
    places = spans(parts, block)
    part = pl.BlockSpec((block, hidden), lambda i: (i, 0))
    return kernel_call(
        functools.partial(product_gradient_kernel, places),
        grid=(rows // block,),
        in_specs=part_specs(parts, block, down.shape[0])
        + [part, part, pl.BlockSpec(memory_space=pl.ANY)],
        out_specs=[part, part],
        out_shape=(OUT((rows, hidden), BF),) * 2,
        scratch_shapes=[pltpu.VMEM(down.shape, BF), pltpu.SemaphoreType.DMA((3,))],
        compiler_params=pltpu.CompilerParams(vmem_limit_bytes=32 << 20),
        cost_estimate=SMALL,
        name="product_gradient",
    )(*parts, to_gate, to_up, down)


def branch_gradients_kernel(branch_ref, mixed_ref, weight_ref, *refs):
    g_ref, grad_ref = refs[-2:]
    total = dot(branch_ref[...], mixed_ref[...], TN)
    if len(refs) > 2:
        total = total + refs[0][...]
    g_ref[...] = total.astype(g_ref.dtype)
    grad_ref[...] = dot(branch_ref[...], weight_ref[...]).astype(BF)


def branch_gradients(kind, branch, mixed, weight, *earlier):
    operands = (branch, mixed, weight, *earlier)
    whole = [pl.BlockSpec(x.shape, lambda i: (0, 0)) for x in operands]
    return kernel_call(
        branch_gradients_kernel,
        grid=(1,),
        in_specs=whole,
        out_specs=[whole[2], whole[1]],
        out_shape=(
            jax.ShapeDtypeStruct(weight.shape, kind),
            jax.ShapeDtypeStruct(mixed.shape, BF),
        ),
        compiler_params=pltpu.CompilerParams(vmem_limit_bytes=32 << 20),
        cost_estimate=SMALL,
        name="branch_gradients",
    )(*operands)


def feed_back_kernel(dgate_ref, dup_ref, source, kept_ref, sent_ref, whole, sems):
    hidden = dgate_ref.shape[1]

    def use(cut):
        cols = slice(*cut)
        total = dot(dgate_ref[...], whole[cols, :hidden], NT)
        total = (total + dot(dup_ref[...], whole[cols, hidden:], NT)).astype(BF)

        @pl.when(pl.program_id(0) < pl.num_programs(0) // 2)
        def _():
            kept_ref[:, cols] = total

        @pl.when(pl.program_id(0) >= pl.num_programs(0) // 2)
        def _():
            sent_ref[:, cols] = total

    stream(source, whole, sems, thirds(whole.shape[0]), use, 0)


def feed_back(first, rows, dgate, dup, gate_up):
    width, hidden = gate_up.shape[0], dgate.shape[1]
    block = 256
    steps = rows // block
    skip = first // block
    part = pl.BlockSpec((block, hidden), lambda i: (i + skip, 0))
    return kernel_call(
        feed_back_kernel,
        grid=(steps,),
        in_specs=[part, part, pl.BlockSpec(memory_space=pl.ANY)],
        out_specs=[
            pl.BlockSpec((block, width), lambda i: (jnp.minimum(i, steps // 2 - 1), 0)),
            pl.BlockSpec((block, width), lambda i: (jnp.maximum(i - steps // 2, 0), 0)),
        ],
        out_shape=(jax.ShapeDtypeStruct((rows // 2, width), BF),) * 2,
        scratch_shapes=[pltpu.VMEM(gate_up.shape, BF), pltpu.SemaphoreType.DMA((3,))],
        compiler_params=pltpu.CompilerParams(vmem_limit_bytes=40 << 20),
        cost_estimate=SMALL,
        name="feed_back",
    )(dgate, dup, gate_up)


class Shards:
    def __init__(self, count):
        self.count = count
        self.half = count // 2
        index = lax.axis_index("shard").astype(jnp.int32)
        hi, lo = index // 2, index % 2
        mine = [(hi ^ k) * 2 + lo for k in range(self.half)]
        partner = [(hi ^ k) * 2 + (1 - lo) for k in range(self.half)]
        self.places = jnp.stack(mine + partner)
        owner = jnp.arange(count, dtype=jnp.int32)
        self.slots = (owner // 2 ^ hi) + self.half * (owner % 2 ^ lo)

    def far(self, value, k):
        return lax.ppermute(
            value, "shard", [(i, ((i // 2) ^ k) * 2 + i % 2) for i in range(self.count)]
        )

    def near(self, value):
        return lax.ppermute(value, "shard", [(i, i ^ 1) for i in range(self.count)])


def tp_swap(value, mask):
    return lax.ppermute(value, "tp", [(i, i ^ mask) for i in range(4)])


def local(count, tokens, w_query, w_keyval, w_out, w_gate, w_up, w_down, gain_attn, gain_mlp, cotangent):
    rows, width = tokens.shape[0], tokens.shape[2]
    tp = lax.axis_index("tp").astype(jnp.int32)
    core, chip = tp % 2, tp // 2
    first_core = core == 0
    chip_table = jnp.reshape(chip, (1,))
    shards = Shards(count)

    def in_order(own, other):
        return jnp.where(
            first_core, jnp.concatenate([own, other], 0), jnp.concatenate([other, own], 0)
        )

    gain_one = gain_attn.astype(BF).astype(F32)[:, None]
    gain_two = gain_mlp.astype(BF).astype(F32)[:, None]
    own_query = w_query.astype(BF).astype(F32)
    own_keyval = w_keyval.astype(BF).astype(F32)
    own_gate = w_gate.astype(BF).astype(F32)
    own_up = w_up.astype(BF).astype(F32)
    keyval_half = jnp.where(first_core, own_keyval[:, :HD], own_keyval[:, HD:])
    send_in = (jnp.concatenate([own_query, keyval_half], 1) * gain_one).astype(BF)
    send_out = jnp.transpose(w_out).astype(BF)
    send_gate_up = (jnp.concatenate([own_gate, own_up], 1) * gain_two).astype(BF)
    send_down = jnp.transpose(w_down).astype(BF)

    heads = GROUP * HD
    half_count = shards.half
    places = shards.places
    part = half_count // 2
    token = places

    def sync(*values):
        nonlocal token
        token, *values = lax.optimization_barrier((token, *values))
        return values

    def far_all(piece):
        return [shards.far(piece, k) for k in range(1, half_count)]

    def rows_of(value, other):
        return lax.dynamic_slice_in_dim(value, (core ^ other) * rows, rows, 0)

    inputs = tokens.reshape(rows, width).astype(F32)
    scale_one = lax.rsqrt(jnp.mean(inputs * inputs, axis=-1, keepdims=True) + EPS)
    unit_own = (inputs * scale_one).astype(BF)
    far_in = far_all(send_in)
    unit_other = tp_swap(unit_own, 1)
    cot = cotangent.reshape(4, rows, width)
    cots = [lax.dynamic_index_in_dim(cot, tp ^ k, 0, keepdims=False) for k in range(4)]
    send_in, send_out, send_down, send_gate_up, unit_other, *pieces = sync(
        send_in, send_out, send_down, send_gate_up, unit_other, *cots, *far_in
    )
    cots, far_in = pieces[:4], pieces[4:]
    gate_up_full = lax.all_gather(send_gate_up, "shard", axis=0, tiled=True)

    far_out = far_all(send_out)
    far_in = pack([send_in] + far_in, send_in.shape[1])
    near_in = shards.near(far_in)
    query_far_b = tp_swap(far_in[:, :heads], 2)
    unit = in_order(unit_own, unit_other)
    unit, query_far_b, near_in, far_in, *far_out = sync(
        unit, query_far_b, near_in, far_in, *far_out
    )

    in_full = unpack(places, far_in, near_in, half_count)
    in_query = in_full[:, :heads]
    scale = HD ** (-0.5)
    column = lax.broadcasted_iota(jnp.int32, (1, in_full.shape[1]), 1)
    query_half = (
        dot(unit, in_full) * jnp.where(column < heads, scale * LOG2E, 1.0)
    ).astype(BF)
    half, query_half, in_query, query_near, *far_out = sync(
        query_half[:, heads:], query_half, in_query, near_in[:, :heads], *far_out
    )

    half_other = tp_swap(half, 1)
    before = lax.ppermute(half, "tp", [(0, 2), (1, 3)])
    far_out = pack([send_out] + far_out, heads)
    near_out = shards.near(far_out)
    query_near_b = tp_swap(query_near, 2)
    half, half_other, before, far_out, near_out, query_near_b = sync(
        half, half_other, before, far_out, near_out, query_near_b
    )

    out_far_b = tp_swap(far_out, 2)
    before_other = tp_swap(before, 1)
    own_pair = jnp.concatenate([before, half], 0)
    other_pair = jnp.concatenate([before_other, half_other], 0)
    keys = jnp.where(first_core, own_pair, other_pair)
    values = jnp.where(first_core, other_pair, own_pair)
    keys_t = jnp.transpose(keys)
    values_t = jnp.transpose(values)
    mixed_a, lse_a = forward_attention(chip_table, query_half, keys, values_t)
    mixed_a, out_far_b, send_down, keys_t = sync(mixed_a, out_far_b, send_down, keys_t)

    down_full = lax.all_gather(send_down, "shard", axis=0, tiled=True)
    out_near_b = tp_swap(near_out, 2)
    in_query_b = unpack(places, query_far_b, query_near_b, half_count)
    query_b = (dot(unit, in_query_b) * (scale * LOG2E)).astype(BF)
    mixed_b, lse_b = forward_attention(chip_table, query_b, keys, values_t)
    mixed_a, mixed_b, out_near_b = sync(mixed_a, mixed_b, out_near_b)

    out_full = unpack(places, far_out, near_out, half_count)
    branch_other = dot(rows_of(mixed_a, 1), out_full, NT)
    branch_own = dot(rows_of(mixed_a, 0), out_full, NT)

    out_full_b = unpack(places, out_far_b, out_near_b, half_count)
    branch_other = (branch_other + dot(rows_of(mixed_b, 1), out_full_b, NT)).astype(BF)
    branch_came = tp_swap(branch_other, 1)
    branch_own = branch_own + dot(rows_of(mixed_b, 0), out_full_b, NT)
    hidden = inputs + (branch_own + branch_came.astype(F32))
    scale_two = lax.rsqrt(jnp.mean(hidden * hidden, axis=-1, keepdims=True) + EPS)
    norm_own = (hidden * scale_two).astype(BF)
    (norm_own,) = sync(norm_own)

    cut = rows // 2
    norm_core = tp_swap(norm_own, 1)
    norm_x1 = tp_swap(norm_own[:cut], 2)
    norm_own, norm_core, norm_x1 = sync(norm_own, norm_core, norm_x1)
    norms = [norm_own, norm_core]

    norm_x2 = tp_swap(norm_own[cut:], 2)
    norm_d1 = tp_swap(norm_x1, 1)
    product, to_gate, to_up = apply_gate_up(norms, gate_up_full)
    norm_x1, norm_x2, norm_d1, product, to_gate, to_up = sync(
        norm_x1, norm_x2, norm_d1, product, to_gate, to_up
    )

    norm_d2 = tp_swap(norm_x2, 1)
    norms += [norm_x1, norm_x2, norm_d1, norm_d2]
    product, to_gate, to_up = apply_gate_up(norms[2:], gate_up_full, product, to_gate, to_up)
    kept_down, sent_down = weight_gradient(shards.slots, cots, product)
    product, to_gate, to_up, *pieces = sync(product, to_gate, to_up, *sent_down, *cots)
    sent_down, cots = pieces[:2], pieces[2:]

    came_down = [shards.near(sent_down[0])]
    down_parts = [
        dot(product[at * rows : (at + 1) * rows], down_full, NT).astype(BF) for at in (3, 2, 1, 0)
    ][::-1]
    down_diagonal = tp_swap(down_parts[3], 1)
    dgate, dup = product_gradient(cots, after(to_gate, *down_parts), to_up, down_full)
    down_far = combine(down_parts[2], down_diagonal)
    dgate, dup, *pieces = sync(dgate, dup, sent_down[1], *down_parts, *down_far, *came_down)
    sent, down_parts, down_far, came_down = pieces[0], pieces[1:5], pieces[5:7], pieces[7:]

    others = [k for k in range(1, half_count) if k != part]
    came_down.append(shards.near(sent))
    down_came = [tp_swap(down_far[0], 2)]
    down_core = tp_swap(down_parts[1], 1)
    sums_down = list(fold(kept_down[0], came_down[0], part))
    far_sums = [shards.far(sums_down[0], part)]
    kept_gate, sent_gate = weight_gradient(shards.slots, norms, dgate)
    back_x, back_diagonal = feed_back(2 * rows, 2 * rows, dgate, dup, gate_up_full)
    dgate, dup, back_x, back_diagonal, down_core, came_down[1], *pieces = sync(
        dgate, dup, back_x, back_diagonal, down_core, came_down[1],
        *sent_gate, *down_came, *far_sums, *sums_down, *norms
    )
    sent_gate, down_came, far_sums, sums_down, norms = (
        pieces[:2],
        pieces[2:3],
        pieces[3:4],
        pieces[4 : 4 + part],
        pieces[4 + part :],
    )

    came_gate = [shards.near(sent_gate[0])]
    sums_down = list(fold(kept_down[1], came_down[1], part)) + sums_down
    far_sums += [shards.far(sums_down[k], k) for k in others]
    back_far = combine(back_x, tp_swap(back_diagonal, 1))
    back_came = [tp_swap(back_far[0], 2)]
    kept_up, sent_up = weight_gradient(shards.slots, norms, after(dup, *back_far))
    dgate, dup, *pieces = sync(
        dgate, dup, sent_gate[1], back_far[1], *back_came, *came_gate, *sent_up, *far_sums
    )
    sent, back_far, back_came, came_gate, sent_up, far_sums_down = (
        pieces[0],
        pieces[1],
        pieces[2:3],
        pieces[3:4],
        pieces[4:6],
        pieces[6:],
    )

    came_gate.append(shards.near(sent))
    sums_gate = list(fold(kept_gate[0], came_gate[0], part))
    far_sums = [shards.far(sums_gate[0], part)]
    back_came.append(tp_swap(back_far, 2))
    back_own, back_core = feed_back(0, 2 * rows, dgate, dup, gate_up_full)
    back_own, back_core, came_gate[1], down_far[1], *pieces = sync(
        back_own, back_core, came_gate[1], down_far[1], *back_came, *sent_up, *far_sums, *sums_gate
    )
    back_came, sent_up, far_sums, sums_gate = pieces[:2], pieces[2:4], pieces[4:5], pieces[5:]

    came_up = [shards.near(sent_up[0])]
    sums_gate = list(fold(kept_gate[1], came_gate[1], part)) + sums_gate
    far_sums += [shards.far(sums_gate[k], k) for k in others]
    down_came.append(tp_swap(down_far[1], 2))
    back_core = tp_swap(back_core, 1)
    grad_norm = (
        back_own.astype(F32)
        + back_core.astype(F32)
        + jnp.concatenate(back_came, 0).astype(F32)
    )
    unit_two = hidden * scale_two
    grad_hidden = cots[0].astype(F32) + scale_two * (
        grad_norm - unit_two * jnp.mean(grad_norm * unit_two, axis=-1, keepdims=True)
    )
    branch_own = grad_hidden.astype(BF)
    branch_other = tp_swap(branch_own, 1)
    g_own, grad_own = branch_gradients(F32, branch_own, rows_of(mixed_b, 0), out_full_b)
    branch_other = after(branch_other, g_own, grad_own)
    g_out_b, grad_other = branch_gradients(
        BF, branch_other, rows_of(mixed_b, 1), out_full_b, g_own
    )
    grad_mixed_b = in_order(grad_own, grad_other)
    g_own, grad_own = branch_gradients(
        F32, branch_own, rows_of(mixed_a, 0), after(out_full, grad_other)
    )
    g_out, grad_other = branch_gradients(F32, branch_other, rows_of(mixed_a, 1), out_full, g_own)
    grad_mixed_a = in_order(grad_own, grad_other)
    grad_mixed_b, grad_mixed_a, g_out_b, g_out, sent, *pieces = sync(
        grad_mixed_b, grad_mixed_a, g_out_b, g_out, sent_up[1], *came_up, *down_came, *far_sums
    )
    came_up, down_came, far_sums_gate = pieces[:1], pieces[1:3], pieces[3:]

    came_up.append(shards.near(sent))
    sums_up = list(fold(kept_up[0], came_up[0], part))
    far_sums = [shards.far(sums_up[0], part)]
    g_out_came = tp_swap(g_out_b, 2)
    dq_b, dk_b, dv_b = backward_attention(
        chip_table, query_b, grad_mixed_b, mixed_b, lse_b, keys, keys_t, values
    )
    dq_b, dk_b, dv_b, g_out_came, came_up[1], *pieces = sync(
        dq_b, dk_b, dv_b, g_out_came, came_up[1], *far_sums, *sums_up
    )
    far_sums, sums_up = pieces[:1], list(fold(kept_up[1], came_up[1], part)) + pieces[1:]

    g_query_b = dot(unit, dq_b, TN).astype(BF)
    g_out = (g_out + g_out_came.astype(F32)).astype(BF)
    (kept_out,), (sent_out,) = split(places, g_out, half_count)
    g_query_b, sent_out, grad_mixed_a, kept_out, *sums_up = sync(
        g_query_b, sent_out, grad_mixed_a, kept_out, *sums_up
    )

    g_query_came = tp_swap(g_query_b, 2)
    far_sums += [shards.far(sums_up[k], k) for k in others]
    came_out = shards.near(sent_out)
    dq_a, dk_a, dv_a = backward_attention(
        chip_table, query_half, grad_mixed_a, mixed_a, lse_a, keys, keys_t, values
    )
    output = finish_output(hidden, down_parts[0], down_core, *down_came)
    dq_a, dk_a, dv_a, g_query_came, came_out, output, *far_sums_up = sync(
        dq_a, dk_a, dv_a, g_query_came, came_out, output, *far_sums
    )

    grad_keys = (dk_a + dk_b) * LN2
    grad_values = dv_a + dv_b
    mine = jnp.where(first_core, grad_keys, grad_values)
    theirs = jnp.where(first_core, grad_values, grad_keys).astype(BF)
    theirs = tp_swap(theirs, 1)
    g_query = (dot(unit, dq_a, TN) + g_query_came.astype(F32)).astype(BF)
    (kept_query,), (sent_query,) = split(places, g_query, half_count)
    sums_out = fold(kept_out, came_out, half_count)
    mine = mine + theirs.astype(F32)
    chip_rows = mine.shape[0] // 2
    mine, own = mine[chip_rows:], mine[:chip_rows].astype(BF)
    mine, own, sent_query, dq_a, dq_b, *pieces = sync(
        mine, own, sent_query, dq_a, dq_b, *sums_out, *far_sums_gate, *far_sums_up, *far_sums_down
    )
    sums_out, pieces = pieces[:half_count], pieces[half_count:]
    far_sums_gate, far_sums_up, far_sums_down = (
        pieces[at * (half_count - 1) : (at + 1) * (half_count - 1)] for at in range(3)
    )

    def total(own, others):
        return functools.reduce(lambda t, o: t + o.astype(F32), others, own.astype(F32))

    earlier = lax.ppermute(own, "tp", [(2, 0), (3, 1)])
    came_query = shards.near(sent_query)
    far_out_sums = [shards.far(sums_out[k], k) for k in range(1, half_count)]
    back_own, back_other = query_back(jnp.reshape(core, (1,)), dq_a, dq_b, in_query, in_query_b)
    grad_w_gate, grad_w_up, gain_two_part = finish_gradients(
        [sums_gate[0], *far_sums_gate],
        [sums_up[0], *far_sums_up],
        w_gate.astype(BF),
        w_up.astype(BF),
        gain_two,
    )
    back_own, back_other, earlier, came_query, grad_w_gate, grad_w_up, gain_two_part, *far_out_sums = sync(
        back_own,
        back_other,
        earlier,
        came_query,
        grad_w_gate,
        grad_w_up,
        gain_two_part,
        *far_out_sums,
    )

    grad_half = (mine + earlier.astype(F32)).astype(BF)
    g_half = dot(unit, grad_half, TN).astype(BF)
    (kept_half,), (sent_half,) = split(places, g_half, half_count)
    sums_query = fold(kept_query, came_query, half_count)
    back_other, back_own, grad_half, sent_half, *sums_query = sync(
        back_other, back_own, grad_half, sent_half, *sums_query
    )

    came_half = shards.near(sent_half)
    far_query = [shards.far(sums_query[k], k) for k in range(1, half_count)]
    in_half = in_full[:, heads:]
    back_other = (back_other + dot(rows_of(grad_half, 1), in_half, NT)).astype(BF)
    back_came = tp_swap(back_other, 1)
    back_own = back_own + dot(rows_of(grad_half, 0), in_half, NT)
    came_half, back_own, back_came, sums_down[0], sums_out[0], *far_query = sync(
        came_half, back_own, back_came, sums_down[0], sums_out[0], *far_query
    )

    sums_half = fold(kept_half, came_half, half_count)
    far_half = [shards.far(sums_half[k], k) for k in range(1, half_count)]
    sums_half = list(sums_half)
    sums_half[0], back_own, sums_down[0], sums_out[0], *far_half = sync(
        sums_half[0], back_own, sums_down[0], sums_out[0], *far_half
    )
    sum_query = total(sums_query[0], far_query)
    sum_half = total(sums_half[0], far_half)

    gain_one_part = jnp.sum(own_query * sum_query, axis=1) + jnp.sum(keyval_half * sum_half, axis=1)
    small = jnp.concatenate(
        [jnp.transpose(sum_half), gain_one_part[None], jnp.transpose(gain_two_part), jnp.zeros((6, sum_half.shape[0]), F32)], 0
    )
    small_came = tp_swap(small, 2)
    grad_tokens = token_gradient(back_own, back_came, tokens.reshape(rows, width), grad_hidden)
    small, small_came, grad_tokens, sums_down[0], sums_out[0] = sync(
        small, small_came, grad_tokens, sums_down[0], sums_out[0]
    )
    small = small + small_came
    other = tp_swap(small, 1)
    grad_w_down = jnp.transpose(total(sums_down[0], far_sums_down))
    grad_w_out = jnp.transpose(total(sums_out[0], far_out_sums))
    gains = small[HD : HD + 2] + other[HD : HD + 2]
    sum_half = jnp.transpose(small[:HD])
    half_swapped = jnp.transpose(other[:HD])
    grad_w_keyval = (
        jnp.where(
            first_core,
            jnp.concatenate([sum_half, half_swapped], 1),
            jnp.concatenate([half_swapped, sum_half], 1),
        )
        * gain_one
    )
    return (
        output.reshape(rows, 1, width),
        grad_tokens,
        sum_query * gain_one,
        grad_w_keyval,
        grad_w_out,
        grad_w_gate,
        grad_w_up,
        grad_w_down,
        gains[0],
        gains[1],
    )


def solution(mesh):
    in_specs = (
        P("tp", "shard", None),
        P("shard", "tp"),
        P("shard", None),
        P("tp", "shard"),
        P("shard", "tp"),
        P("shard", "tp"),
        P("tp", "shard"),
        P("shard"),
        P("shard"),
        P(None, "shard", None),
    )
    out_specs = (
        P("tp", "shard", None),
        P("tp", "shard", None),
        P("shard", "tp"),
        P("shard", None),
        P("tp", "shard"),
        P("shard", "tp"),
        P("shard", "tp"),
        P("tp", "shard"),
        P("shard"),
        P("shard"),
    )
    return jax.shard_map(
        functools.partial(local, mesh.shape["shard"]),
        mesh=mesh,
        in_specs=in_specs,
        out_specs=out_specs,
        check_vma=False,
    )
```

```python
import functools

import jax
import jax.numpy as jnp
from jax import lax
from jax.experimental import pallas as pl
from jax.experimental.pallas import tpu as pltpu
from jax.sharding import PartitionSpec as P

HD = 128
WINDOW = 1024
QB = 256
GROUP = 3
EPS = 1e-06
LOG2E = 1.4426950408889634
LN2 = 0.6931471805599453
NEG = -1e30
LARGE = 1 << 20
OUT = pltpu.HBM
SMALL = pl.CostEstimate(flops=0, transcendentals=0, bytes_accessed=0)
BF = jnp.bfloat16
F32 = jnp.float32
NT = (((1,), (1,)), ((), ()))
TN = (((0,), (0,)), ((), ()))
NN = (((1,), (0,)), ((), ()))


def dot(a, b, dims=NN):
    return lax.dot_general(a, b, dims, preferred_element_type=F32)


def after(value, *others):
    return lax.optimization_barrier((value, *others))[0]


def kernel_call(*args, **kwargs):
    call = pl.pallas_call(*args, **kwargs)

    def run(*operands):
        return call(
            *(
                pltpu.with_memory_space_constraint(x, pltpu.HBM) if x.size > LARGE else x
                for x in operands
            )
        )

    return run


def forward_attention_kernel(chip_ref, q_ref, k_ref, vt_ref, o_ref, lse_ref):
    block = pl.program_id(0)
    chunks = WINDOW // QB
    key_row = lax.broadcasted_iota(jnp.int32, (QB, QB), 0)
    query_col = lax.broadcasted_iota(jnp.int32, (QB, QB), 1)

    def rows_of(chunk):
        return pl.ds(pl.multiple_of((block + chunk) * QB, QB), QB)

    def finish(head, top, total, mixed):
        cols = slice(head * HD, (head + 1) * HD)
        o_ref[:, cols] = jnp.transpose(mixed / total).astype(BF)
        lse_ref[head : head + 1, :] = top + jnp.log(total) * LOG2E

    def attend(first):
        for head in range(GROUP):
            query = q_ref[:, head * HD : (head + 1) * HD]
            scores = {}
            for chunk in range(first, chunks + 1):
                scores[chunk] = dot(k_ref[rows_of(chunk), :], query, NT)
                if chunk == 0:
                    scores[chunk] = jnp.where(key_row > query_col, scores[chunk], NEG)
                if chunk == chunks:
                    scores[chunk] = jnp.where(key_row <= query_col, scores[chunk], NEG)
            top = functools.reduce(jnp.maximum, scores.values())
            top = jnp.max(top, axis=0, keepdims=True)
            total = jnp.zeros((1, QB), F32)
            mixed = jnp.zeros((HD, QB), F32)
            for chunk, part in scores.items():
                probs = jnp.exp2(part - top)
                total = total + jnp.sum(probs, axis=0, keepdims=True)
                mixed = mixed + dot(vt_ref[:, rows_of(chunk)], probs.astype(BF))
            finish(head, top, total, mixed)

    pl.when(chip_ref[0] != 0)(functools.partial(attend, 0))
    for at in range(chunks):
        pl.when((chip_ref[0] == 0) & (block == at))(functools.partial(attend, chunks - at))


def forward_attention(chip, query, keys, values_t):
    rows = query.shape[0]
    width = GROUP * HD
    return kernel_call(
        forward_attention_kernel,
        grid_spec=pltpu.PrefetchScalarGridSpec(
            num_scalar_prefetch=1,
            grid=(rows // QB,),
            in_specs=[
                pl.BlockSpec((QB, width), lambda b, s: (b, 0)),
                pl.BlockSpec((2 * rows, HD), lambda b, s: (0, 0)),
                pl.BlockSpec((HD, 2 * rows), lambda b, s: (0, 0)),
            ],
            out_specs=[
                pl.BlockSpec((QB, width), lambda b, s: (b, 0)),
                pl.BlockSpec((8, QB), lambda b, s: (0, b)),
            ],
        ),
        out_shape=(
            jax.ShapeDtypeStruct((rows, width), BF),
            jax.ShapeDtypeStruct((8, rows), F32),
        ),
        compiler_params=pltpu.CompilerParams(vmem_limit_bytes=40 << 20),
        cost_estimate=SMALL,
        name="attention_forward",
    )(chip, query, keys, values_t)


def backward_attention_kernel(
    chip_ref, q_ref, g_ref, o_ref, lse_ref, k_ref, kt_ref, v_ref, dq_ref, dk_ref, dv_ref
):
    block = pl.program_id(0)
    chunks = WINDOW // QB
    key_row = lax.broadcasted_iota(jnp.int32, (QB, QB), 0)
    query_col = lax.broadcasted_iota(jnp.int32, (QB, QB), 1)

    @pl.when(block == 0)
    def _():
        dk_ref[...] = jnp.zeros_like(dk_ref)
        dv_ref[...] = jnp.zeros_like(dv_ref)

    def rows_of(chunk):
        return pl.ds(pl.multiple_of((block + chunk) * QB, QB), QB)

    deltas = []
    for head in range(GROUP):
        cols = slice(head * HD, (head + 1) * HD)
        both = g_ref[:, cols].astype(F32) * o_ref[:, cols].astype(F32)
        deltas.append(jnp.sum(jnp.transpose(both), axis=0, keepdims=True))

    def one_chunk(chunk, keep, totals):
        rows = rows_of(chunk)
        keys = k_ref[rows, :]
        values = v_ref[rows, :]
        keys_t = kt_ref[:, rows]
        grad_keys = jnp.zeros((QB, HD), F32)
        grad_values = jnp.zeros((QB, HD), F32)
        new = []
        for head in range(GROUP):
            cols = slice(head * HD, (head + 1) * HD)
            query = q_ref[:, cols]
            grad = g_ref[:, cols]
            probs = jnp.exp2(dot(keys, query, NT) - lse_ref[head : head + 1, :])
            if keep is not None:
                probs = jnp.where(keep, probs, 0.0)
            grad_scores = (probs * (dot(values, grad, NT) - deltas[head])).astype(BF)
            grad_values = grad_values + dot(probs.astype(BF), grad)
            grad_keys = grad_keys + dot(grad_scores, query)
            new.append(totals[head] + dot(keys_t, grad_scores))
        dk_ref[rows, :] += grad_keys
        dv_ref[rows, :] += grad_values
        return tuple(new)

    def finish(totals):
        for head in range(GROUP):
            cols = slice(head * HD, (head + 1) * HD)
            dq_ref[:, cols] = (jnp.transpose(totals[head]) * HD ** (-0.5)).astype(BF)

    zeros = tuple(jnp.zeros((HD, QB), F32) for _ in range(GROUP))

    @pl.when(chip_ref[0] != 0)
    def _():
        totals = zeros
        for chunk in range(chunks + 1):
            keep = None
            if chunk == 0:
                keep = key_row > query_col
            if chunk == chunks:
                keep = key_row <= query_col
            totals = one_chunk(chunk, keep, totals)
        finish(totals)

    @pl.when(chip_ref[0] == 0)
    def _():
        def step(chunk, totals):
            return one_chunk(chunk, (key_row <= query_col) | (chunk < chunks), totals)

        finish(lax.fori_loop(chunks - block, chunks + 1, step, zeros))


def backward_attention(chip, query, grad, mixed, lse, keys, keys_t, values):
    rows = query.shape[0]
    width = GROUP * HD
    wide = pl.BlockSpec((QB, width), lambda b, s: (b, 0))
    whole = pl.BlockSpec((2 * rows, HD), lambda b, s: (0, 0))
    return kernel_call(
        backward_attention_kernel,
        grid_spec=pltpu.PrefetchScalarGridSpec(
            num_scalar_prefetch=1,
            grid=(rows // QB,),
            in_specs=[
                wide,
                wide,
                wide,
                pl.BlockSpec((8, QB), lambda b, s: (0, b)),
                whole,
                pl.BlockSpec((HD, 2 * rows), lambda b, s: (0, 0)),
                whole,
            ],
            out_specs=[wide, whole, whole],
        ),
        out_shape=(
            jax.ShapeDtypeStruct((rows, width), BF),
            jax.ShapeDtypeStruct((2 * rows, HD), F32),
            jax.ShapeDtypeStruct((2 * rows, HD), F32),
        ),
        compiler_params=pltpu.CompilerParams(vmem_limit_bytes=40 << 20),
        cost_estimate=SMALL,
        name="attention_backward",
    )(chip, query, grad, mixed, lse, keys, keys_t, values)


def pack_kernel(*refs):
    packed = refs[-1]
    depth, width = refs[0].shape[0], packed.shape[1]
    for i, piece in enumerate(refs[:-1]):
        packed[pl.ds(i * depth, depth), :] = piece[:, :width]


def pack(pieces, width):
    depth = pieces[0].shape[0]
    rows = depth * len(pieces)
    return kernel_call(
        pack_kernel,
        grid=(1,),
        in_specs=[pl.BlockSpec(piece.shape, lambda i: (0, 0)) for piece in pieces],
        out_specs=pl.BlockSpec((rows, width), lambda i: (0, 0)),
        out_shape=jax.ShapeDtypeStruct((rows, width), BF),
        compiler_params=pltpu.CompilerParams(vmem_limit_bytes=16 << 20),
        cost_estimate=SMALL,
        name="pack_pieces",
    )(*pieces)


def unpack_kernel(half, place_ref, far, near, whole):
    depth = far.shape[0] // half
    for i in range(half):
        rows = pl.ds(i * depth, depth)
        whole[pl.ds(pl.multiple_of(place_ref[i] * depth, depth), depth), :] = far[rows, :]
        whole[pl.ds(pl.multiple_of(place_ref[half + i] * depth, depth), depth), :] = near[rows, :]


def unpack(places, far, near, half):
    rows, width = far.shape
    packed = pl.BlockSpec((rows, width), lambda i, s: (0, 0))
    return kernel_call(
        functools.partial(unpack_kernel, half),
        grid_spec=pltpu.PrefetchScalarGridSpec(
            num_scalar_prefetch=1,
            grid=(1,),
            in_specs=[packed, packed],
            out_specs=pl.BlockSpec((2 * rows, width), lambda i, s: (0, 0)),
        ),
        out_shape=jax.ShapeDtypeStruct((2 * rows, width), BF),
        compiler_params=pltpu.CompilerParams(vmem_limit_bytes=16 << 20),
        cost_estimate=SMALL,
        name="unpack_pieces",
    )(places, far, near)


def split_kernel(groups, half, place_ref, whole, *refs):
    depth = refs[0].shape[0] // len(groups[0])
    for group, kept, sent in zip(groups, refs[: len(groups)], refs[len(groups) :]):
        for at, i in enumerate(group):
            rows = pl.ds(at * depth, depth)
            kept[rows, :] = whole[pl.ds(pl.multiple_of(place_ref[i] * depth, depth), depth), :]
            sent[rows, :] = whole[
                pl.ds(pl.multiple_of(place_ref[half + i] * depth, depth), depth), :
            ]


def split(places, whole, half, parts=1):
    size = half // parts
    groups = [range(half - (p + 1) * size, half - p * size) for p in range(parts)]
    rows, width = whole.shape[0] // (2 * parts), whole.shape[1]
    out = pl.BlockSpec((rows, width), lambda i, s: (0, 0))
    pieces = kernel_call(
        functools.partial(split_kernel, groups, half),
        grid_spec=pltpu.PrefetchScalarGridSpec(
            num_scalar_prefetch=1,
            grid=(1,),
            in_specs=[pl.BlockSpec(whole.shape, lambda i, s: (0, 0))],
            out_specs=[out] * (2 * parts),
        ),
        out_shape=(jax.ShapeDtypeStruct((rows, width), whole.dtype),) * (2 * parts),
        compiler_params=pltpu.CompilerParams(vmem_limit_bytes=24 << 20),
        cost_estimate=SMALL,
        name="split_pieces",
    )(places, whole)
    return pieces[:parts], pieces[parts:]


def fold_kernel(kept, came, *pieces):
    depth = pieces[0].shape[0]
    for i, piece in enumerate(pieces):
        rows = pl.ds(i * depth, depth)
        piece[...] = (kept[rows, :].astype(F32) + came[rows, :].astype(F32)).astype(BF)


def fold(kept, came, half):
    rows, width = kept.shape
    depth = rows // half
    whole = pl.BlockSpec((rows, width), lambda i: (0, 0))
    return kernel_call(
        fold_kernel,
        grid=(1,),
        in_specs=[whole, whole],
        out_specs=[pl.BlockSpec((depth, width), lambda i: (0, 0))] * half,
        out_shape=(OUT((depth, width), BF),) * half,
        compiler_params=pltpu.CompilerParams(vmem_limit_bytes=24 << 20),
        cost_estimate=SMALL,
        name="fold_pieces",
    )(kept, came)


def token_gradient_kernel(own_ref, came_ref, token_ref, through_ref, out_ref):
    grad = own_ref[...] + came_ref[...].astype(F32)
    unit = token_ref[...].astype(F32)
    scale = lax.rsqrt(jnp.mean(unit * unit, axis=-1, keepdims=True) + EPS)
    unit = unit * scale
    inner = jnp.mean(grad * unit, axis=-1, keepdims=True)
    out_ref[:, 0, :] = through_ref[...] + scale * (grad - unit * inner)


def token_gradient(own, came, tokens, through):
    rows, width = own.shape
    block = 128
    part = pl.BlockSpec((block, width), lambda i: (i, 0))
    return kernel_call(
        token_gradient_kernel,
        grid=(rows // block,),
        in_specs=[part] * 4,
        out_specs=pl.BlockSpec((block, 1, width), lambda i: (i, 0, 0)),
        out_shape=jax.ShapeDtypeStruct((rows, 1, width), F32),
        compiler_params=pltpu.CompilerParams(vmem_limit_bytes=24 << 20),
        cost_estimate=SMALL,
        name="token_gradient",
    )(*in_memory(own, came, tokens, through))


def query_back_kernel(core_ref, a_ref, b_ref, weight_a_ref, weight_b_ref, own_ref, other_ref):
    rows = own_ref.shape[0]
    for out, core in ((other_ref, 1 - core_ref[0]), (own_ref, core_ref[0])):
        place = pl.ds(pl.multiple_of(core * rows, rows), rows)
        total = dot(a_ref[place, :], weight_a_ref[...], NT)
        out[...] = total + dot(b_ref[place, :], weight_b_ref[...], NT)


def query_back(core, a, b, weight_a, weight_b):
    rows, width = a.shape[0] // 2, weight_a.shape[0]
    whole = [pl.BlockSpec(x.shape, lambda i, s: (0, 0)) for x in (a, b, weight_a, weight_b)]
    return kernel_call(
        query_back_kernel,
        grid_spec=pltpu.PrefetchScalarGridSpec(
            num_scalar_prefetch=1,
            grid=(1,),
            in_specs=whole,
            out_specs=[pl.BlockSpec((rows, width), lambda i, s: (0, 0))] * 2,
        ),
        out_shape=(jax.ShapeDtypeStruct((rows, width), F32),) * 2,
        compiler_params=pltpu.CompilerParams(vmem_limit_bytes=36 << 20),
        cost_estimate=SMALL,
        name="query_back",
    )(core, a, b, weight_a, weight_b)


def in_memory(*operands):
    return [pltpu.with_memory_space_constraint(x, pltpu.HBM) for x in operands]


def finish_gradients_kernel(count, *refs):
    gate, up = refs[:count], refs[count : 2 * count]
    own_gate_ref, own_up_ref, gain_ref, gate_ref, up_ref, part_ref = refs[2 * count :]
    gain = gain_ref[...]
    part = 0.0
    for pieces, own, out in ((gate, own_gate_ref, gate_ref), (up, own_up_ref, up_ref)):
        total = pieces[0][...].astype(F32)
        for piece in pieces[1:]:
            total = total + piece[...].astype(F32)
        out[...] = total * gain
        part = part + jnp.sum(own[...].astype(F32) * total, axis=1, keepdims=True)
    part_ref[...] = part


def finish_gradients(gate, up, own_gate, own_up, gain):
    operands = [*gate, *up, own_gate, own_up, gain]
    whole = [pl.BlockSpec(x.shape, lambda i: (0, 0)) for x in operands]
    return kernel_call(
        functools.partial(finish_gradients_kernel, len(gate)),
        grid=(1,),
        in_specs=whole,
        out_specs=[whole[0], whole[0], whole[-1]],
        out_shape=(
            OUT(own_gate.shape, F32),
            OUT(own_gate.shape, F32),
            jax.ShapeDtypeStruct(gain.shape, F32),
        ),
        compiler_params=pltpu.CompilerParams(vmem_limit_bytes=40 << 20),
        cost_estimate=SMALL,
        name="finish_gradients",
    )(*in_memory(*operands[:-1]), gain)


def finish_output_kernel(hidden_ref, own_ref, core_ref, *refs):
    first = 0
    for ref in refs[:-1]:
        rows = slice(first, first + ref.shape[0])
        total = hidden_ref[rows, :] + own_ref[rows, :].astype(F32) + core_ref[rows, :].astype(F32)
        refs[-1][rows, :] = (total + ref[...].astype(F32)).astype(BF)
        first += ref.shape[0]


def finish_output(hidden, own, core, *came):
    operands = (hidden, own, core, *came)
    whole = [pl.BlockSpec(x.shape, lambda i: (0, 0)) for x in operands]
    return kernel_call(
        finish_output_kernel,
        grid=(1,),
        in_specs=whole,
        out_specs=whole[0],
        out_shape=OUT(hidden.shape, BF),
        compiler_params=pltpu.CompilerParams(vmem_limit_bytes=40 << 20),
        cost_estimate=SMALL,
        name="finish_output",
    )(*in_memory(*operands))


def spans(parts, block):
    counts = [part.shape[0] // block for part in parts]
    return [(sum(counts[:i]), count) for i, count in enumerate(counts)]


def part_specs(parts, block, width):
    def spec(first, count):
        return pl.BlockSpec((block, width), lambda i: (jnp.clip(i - first, 0, count - 1), 0))

    return [spec(first, count) for first, count in spans(parts, block)]


def weight_gradient_kernel(half, slot_ref, *refs):
    part = half // 2
    outs, grad_ref, parts = refs[-4:], refs[-5], refs[:-5]
    depth = outs[0].shape[0] // part
    first = 0
    total = None
    for ref in parts:
        rows = ref.shape[0]
        term = dot(ref[...], grad_ref[first : first + rows, :], TN)
        total = term if total is None else total + term
        first += rows
    total = total.astype(BF)
    count = total.shape[0] // depth
    for at in range(count):
        slot = slot_ref[pl.program_id(0) * count + at]
        k = lax.rem(slot, half)
        target = 2 * (slot // half) + 1 - k // part
        place = pl.ds(pl.multiple_of(lax.rem(k, part) * depth, depth), depth)
        for i, ref in enumerate(outs):

            @pl.when(target == i)
            def _(ref=ref, place=place, at=at):
                ref[place, :] = total[at * depth : (at + 1) * depth, :]


def weight_gradient(slots, parts, grad):
    half = slots.shape[0] // 2
    width = parts[0].shape[1]
    hidden = grad.shape[1]
    block = 384
    pieces = kernel_call(
        functools.partial(weight_gradient_kernel, half),
        grid_spec=pltpu.PrefetchScalarGridSpec(
            num_scalar_prefetch=1,
            grid=(width // block,),
            in_specs=[pl.BlockSpec((part.shape[0], block), lambda i, s: (0, i)) for part in parts]
            + [pl.BlockSpec(grad.shape, lambda i, s: (0, 0), pipeline_mode=pl.Buffered(1))],
            out_specs=[pl.BlockSpec((width // 4, hidden), lambda i, s: (0, 0))] * 4,
        ),
        out_shape=(OUT((width // 4, hidden), BF),) * 4,
        compiler_params=pltpu.CompilerParams(vmem_limit_bytes=40 << 20),
        cost_estimate=SMALL,
        name="weight_gradient",
    )(slots, *parts, grad)
    return pieces[:2], pieces[2:]


def combine_kernel(a_ref, b_ref, *outs):
    first = 0
    for out in outs:
        rows = slice(first, first + out.shape[0])
        out[...] = (a_ref[rows, :].astype(F32) + b_ref[rows, :].astype(F32)).astype(BF)
        first += out.shape[0]


def combine(a, b):
    rows, width = a.shape
    whole = pl.BlockSpec((rows, width), lambda i: (0, 0))
    return kernel_call(
        combine_kernel,
        grid=(1,),
        in_specs=[whole, whole],
        out_specs=[pl.BlockSpec((rows // 2, width), lambda i: (0, 0))] * 2,
        out_shape=(jax.ShapeDtypeStruct((rows // 2, width), BF),) * 2,
        compiler_params=pltpu.CompilerParams(vmem_limit_bytes=16 << 20),
        cost_estimate=SMALL,
        name="combine",
    )(a, b)


def gelu_parts(gate):
    square = gate * gate
    t = jnp.tanh(gate * (0.7978845608028654 + 0.035677408136300125 * square))
    half = 0.5 + 0.5 * t
    value = gate * half
    slope = half + 0.5 * gate * (1.0 - t * t) * (0.7978845608028654 + 0.10703222440890037 * square)
    return value, slope


def stream(source, whole, sems, cuts, use, axis=1):
    def at(ref, cut):
        where = pl.ds(cut[0], cut[1] - cut[0])
        return ref.at[:, where] if axis else ref.at[where, :]

    copies = [
        pltpu.make_async_copy(at(source, cut), at(whole, cut), sems.at[i])
        for i, cut in enumerate(cuts)
    ]

    @pl.when(pl.program_id(0) == 0)
    def _():
        for copy in copies:
            copy.start()
        for cut, copy in zip(cuts, copies):
            copy.wait()
            use(cut)

    @pl.when(pl.program_id(0) > 0)
    def _():
        use((0, cuts[-1][1]))


def thirds(width):
    return [(i * width // 3, (i + 1) * width // 3) for i in range(3)]


def gate_up_block(norm_ref, whole, cut, product_ref, to_gate_ref, to_up_ref):
    hidden = product_ref.shape[1]
    cols = slice(*cut)
    gate = dot(norm_ref[...], whole[:, cols])
    up = dot(norm_ref[...], whole[:, hidden + cut[0] : hidden + cut[1]])
    value, slope = gelu_parts(gate)
    product_ref[:, cols] = (value * up).astype(BF)
    to_gate_ref[:, cols] = (up * slope).astype(BF)
    to_up_ref[:, cols] = value.astype(BF)


def gate_up_kernel(places, *refs):
    parts, source = refs[: len(places)], refs[len(places)]
    outs, whole, sems = refs[-5:-2], refs[-2], refs[-1]
    hidden = outs[0].shape[1]
    step = pl.program_id(0)
    cuts = thirds(hidden)
    copies = [
        [
            pltpu.make_async_copy(
                source.at[:, pl.ds(side + a, b - a)],
                whole.at[:, pl.ds(side + a, b - a)],
                sems.at[2 * i + side // hidden],
            )
            for side in (0, hidden)
        ]
        for i, (a, b) in enumerate(cuts)
    ]

    @pl.when(step == 0)
    def _():
        for pair in copies:
            for copy in pair:
                copy.start()
        for cut, pair in zip(cuts, copies):
            for copy in pair:
                copy.wait()
            gate_up_block(parts[0], whole, cut, *outs)

    for (first, count), ref in zip(places, parts):
        inside = (step > 0) & (step >= first) & (step < first + count)
        pl.when(inside)(functools.partial(gate_up_block, ref, whole, (0, hidden), *outs))


def apply_gate_up(parts, gate_up, *earlier):
    width, hidden = gate_up.shape[0], gate_up.shape[1] // 2
    block = 256
    places = spans(parts, block)
    steps = sum(count for _, count in places)
    skip = steps if earlier else 0
    out = pl.BlockSpec((block, hidden), lambda i: (i + skip, 0))
    anywhere = pl.BlockSpec(memory_space=pl.ANY)
    return kernel_call(
        functools.partial(gate_up_kernel, places),
        grid=(steps,),
        in_specs=part_specs(parts, block, width) + [anywhere] * (1 + len(earlier)),
        out_specs=[out, out, out],
        out_shape=(OUT((2 * steps * block, hidden), BF),) * 3,
        scratch_shapes=[pltpu.VMEM(gate_up.shape, BF), pltpu.SemaphoreType.DMA((6,))],
        input_output_aliases={len(parts) + 1 + i: i for i in range(len(earlier))},
        compiler_params=pltpu.CompilerParams(vmem_limit_bytes=40 << 20),
        cost_estimate=SMALL,
        name="gate_up_rest" if earlier else "gate_up_first",
    )(*parts, gate_up, *earlier)


def product_gradient_kernel(places, *refs):
    parts = refs[: len(places)]
    to_gate_ref, to_up_ref, source, dgate_ref, dup_ref, whole, sems = refs[len(places) :]
    at = pl.program_id(0)

    def use(cut):
        cols = slice(*cut)

        def block(cot_ref):
            grad = dot(cot_ref[...], whole[:, cols])
            dgate_ref[:, cols] = (grad * to_gate_ref[:, cols].astype(F32)).astype(BF)
            dup_ref[:, cols] = (grad * to_up_ref[:, cols].astype(F32)).astype(BF)

        if cut[1] - cut[0] < whole.shape[1]:
            block(parts[0])
        else:
            for (first, count), ref in zip(places, parts):
                pl.when((at >= first) & (at < first + count))(functools.partial(block, ref))

    stream(source, whole, sems, thirds(whole.shape[1]), use)


def product_gradient(parts, to_gate, to_up, down):
    rows, hidden = to_gate.shape
    block = 256
    places = spans(parts, block)
    part = pl.BlockSpec((block, hidden), lambda i: (i, 0))
    return kernel_call(
        functools.partial(product_gradient_kernel, places),
        grid=(rows // block,),
        in_specs=part_specs(parts, block, down.shape[0])
        + [part, part, pl.BlockSpec(memory_space=pl.ANY)],
        out_specs=[part, part],
        out_shape=(OUT((rows, hidden), BF),) * 2,
        scratch_shapes=[pltpu.VMEM(down.shape, BF), pltpu.SemaphoreType.DMA((3,))],
        compiler_params=pltpu.CompilerParams(vmem_limit_bytes=32 << 20),
        cost_estimate=SMALL,
        name="product_gradient",
    )(*parts, to_gate, to_up, down)


def branch_gradients_kernel(branch_ref, mixed_ref, weight_ref, *refs):
    g_ref, grad_ref = refs[-2:]
    total = dot(branch_ref[...], mixed_ref[...], TN)
    if len(refs) > 2:
        total = total + refs[0][...]
    g_ref[...] = total.astype(g_ref.dtype)
    grad_ref[...] = dot(branch_ref[...], weight_ref[...]).astype(BF)


def branch_gradients(kind, branch, mixed, weight, *earlier):
    operands = (branch, mixed, weight, *earlier)
    whole = [pl.BlockSpec(x.shape, lambda i: (0, 0)) for x in operands]
    return kernel_call(
        branch_gradients_kernel,
        grid=(1,),
        in_specs=whole,
        out_specs=[whole[2], whole[1]],
        out_shape=(
            jax.ShapeDtypeStruct(weight.shape, kind),
            jax.ShapeDtypeStruct(mixed.shape, BF),
        ),
        compiler_params=pltpu.CompilerParams(vmem_limit_bytes=32 << 20),
        cost_estimate=SMALL,
        name="branch_gradients",
    )(*operands)


def feed_back_kernel(dgate_ref, dup_ref, source, kept_ref, sent_ref, whole, sems):
    hidden = dgate_ref.shape[1]

    def use(cut):
        cols = slice(*cut)
        total = dot(dgate_ref[...], whole[cols, :hidden], NT)
        total = (total + dot(dup_ref[...], whole[cols, hidden:], NT)).astype(BF)

        @pl.when(pl.program_id(0) < pl.num_programs(0) // 2)
        def _():
            kept_ref[:, cols] = total

        @pl.when(pl.program_id(0) >= pl.num_programs(0) // 2)
        def _():
            sent_ref[:, cols] = total

    stream(source, whole, sems, thirds(whole.shape[0]), use, 0)


def feed_back(first, rows, dgate, dup, gate_up):
    width, hidden = gate_up.shape[0], dgate.shape[1]
    block = 256
    steps = rows // block
    skip = first // block
    part = pl.BlockSpec((block, hidden), lambda i: (i + skip, 0))
    return kernel_call(
        feed_back_kernel,
        grid=(steps,),
        in_specs=[part, part, pl.BlockSpec(memory_space=pl.ANY)],
        out_specs=[
            pl.BlockSpec((block, width), lambda i: (jnp.minimum(i, steps // 2 - 1), 0)),
            pl.BlockSpec((block, width), lambda i: (jnp.maximum(i - steps // 2, 0), 0)),
        ],
        out_shape=(jax.ShapeDtypeStruct((rows // 2, width), BF),) * 2,
        scratch_shapes=[pltpu.VMEM(gate_up.shape, BF), pltpu.SemaphoreType.DMA((3,))],
        compiler_params=pltpu.CompilerParams(vmem_limit_bytes=40 << 20),
        cost_estimate=SMALL,
        name="feed_back",
    )(dgate, dup, gate_up)


class Shards:
    def __init__(self, count):
        self.count = count
        self.half = count // 2
        index = lax.axis_index("shard").astype(jnp.int32)
        hi, lo = index // 2, index % 2
        mine = [(hi ^ k) * 2 + lo for k in range(self.half)]
        partner = [(hi ^ k) * 2 + (1 - lo) for k in range(self.half)]
        self.places = jnp.stack(mine + partner)
        owner = jnp.arange(count, dtype=jnp.int32)
        self.slots = (owner // 2 ^ hi) + self.half * (owner % 2 ^ lo)

    def far(self, value, k):
        return lax.ppermute(
            value, "shard", [(i, ((i // 2) ^ k) * 2 + i % 2) for i in range(self.count)]
        )

    def near(self, value):
        return lax.ppermute(value, "shard", [(i, i ^ 1) for i in range(self.count)])


def tp_swap(value, mask):
    return lax.ppermute(value, "tp", [(i, i ^ mask) for i in range(4)])


def local(count, tokens, w_query, w_keyval, w_out, w_gate, w_up, w_down, gain_attn, gain_mlp, cotangent):
    rows, width = tokens.shape[0], tokens.shape[2]
    tp = lax.axis_index("tp").astype(jnp.int32)
    core, chip = tp % 2, tp // 2
    first_core = core == 0
    chip_table = jnp.reshape(chip, (1,))
    shards = Shards(count)

    def in_order(own, other):
        return jnp.where(
            first_core, jnp.concatenate([own, other], 0), jnp.concatenate([other, own], 0)
        )

    gain_one = gain_attn.astype(BF).astype(F32)[:, None]
    gain_two = gain_mlp.astype(BF).astype(F32)[:, None]
    own_query = w_query.astype(BF).astype(F32)
    own_keyval = w_keyval.astype(BF).astype(F32)
    own_gate = w_gate.astype(BF).astype(F32)
    own_up = w_up.astype(BF).astype(F32)
    keyval_half = jnp.where(first_core, own_keyval[:, :HD], own_keyval[:, HD:])
    send_in = (jnp.concatenate([own_query, keyval_half], 1) * gain_one).astype(BF)
    send_out = jnp.transpose(w_out).astype(BF)
    send_gate_up = (jnp.concatenate([own_gate, own_up], 1) * gain_two).astype(BF)
    send_down = jnp.transpose(w_down).astype(BF)

    heads = GROUP * HD
    half_count = shards.half
    places = shards.places
    part = half_count // 2
    token = places

    def sync(*values):
        nonlocal token
        token, *values = lax.optimization_barrier((token, *values))
        return values

    def far_all(piece):
        return [shards.far(piece, k) for k in range(1, half_count)]

    def rows_of(value, other):
        return lax.dynamic_slice_in_dim(value, (core ^ other) * rows, rows, 0)

    inputs = tokens.reshape(rows, width).astype(F32)
    scale_one = lax.rsqrt(jnp.mean(inputs * inputs, axis=-1, keepdims=True) + EPS)
    unit_own = (inputs * scale_one).astype(BF)
    far_in = far_all(send_in)
    unit_other = tp_swap(unit_own, 1)
    cot = cotangent.reshape(4, rows, width)
    cots = [lax.dynamic_index_in_dim(cot, tp ^ k, 0, keepdims=False) for k in range(4)]
    send_in, send_out, send_gate_up, unit_other, *pieces = sync(
        send_in, send_out, send_gate_up, unit_other, *cots, *far_in
    )
    cots, far_in = pieces[:4], pieces[4:]
    gate_up_full = lax.all_gather(send_gate_up, "shard", axis=0, tiled=True)

    far_out = far_all(send_out)
    far_in = pack([send_in] + far_in, send_in.shape[1])
    near_in = shards.near(far_in)
    query_far_b = tp_swap(far_in[:, :heads], 2)
    unit = in_order(unit_own, unit_other)
    unit, query_far_b, near_in, far_in, *far_out = sync(
        unit, query_far_b, near_in, far_in, *far_out
    )

    in_full = unpack(places, far_in, near_in, half_count)
    in_query = in_full[:, :heads]
    scale = HD ** (-0.5)
    column = lax.broadcasted_iota(jnp.int32, (1, in_full.shape[1]), 1)
    query_half = (
        dot(unit, in_full) * jnp.where(column < heads, scale * LOG2E, 1.0)
    ).astype(BF)
    half, query_half, in_query, query_near, *far_out = sync(
        query_half[:, heads:], query_half, in_query, near_in[:, :heads], *far_out
    )

    half_other = tp_swap(half, 1)
    before = lax.ppermute(half, "tp", [(0, 2), (1, 3)])
    far_out = pack([send_out] + far_out, heads)
    near_out = shards.near(far_out)
    query_near_b = tp_swap(query_near, 2)
    half, half_other, before, far_out, near_out, query_near_b = sync(
        half, half_other, before, far_out, near_out, query_near_b
    )

    out_far_b = tp_swap(far_out, 2)
    before_other = tp_swap(before, 1)
    own_pair = jnp.concatenate([before, half], 0)
    other_pair = jnp.concatenate([before_other, half_other], 0)
    keys = jnp.where(first_core, own_pair, other_pair)
    values = jnp.where(first_core, other_pair, own_pair)
    keys_t = jnp.transpose(keys)
    values_t = jnp.transpose(values)
    mixed_a, lse_a = forward_attention(chip_table, query_half, keys, values_t)
    mixed_a, out_far_b, send_down, keys_t = sync(mixed_a, out_far_b, send_down, keys_t)

    down_full = lax.all_gather(send_down, "shard", axis=0, tiled=True)
    out_near_b = tp_swap(near_out, 2)
    in_query_b = unpack(places, query_far_b, query_near_b, half_count)
    query_b = (dot(unit, in_query_b) * (scale * LOG2E)).astype(BF)
    mixed_b, lse_b = forward_attention(chip_table, query_b, keys, values_t)
    mixed_a, mixed_b, out_near_b = sync(mixed_a, mixed_b, out_near_b)

    out_full = unpack(places, far_out, near_out, half_count)
    branch_other = dot(rows_of(mixed_a, 1), out_full, NT)
    branch_own = dot(rows_of(mixed_a, 0), out_full, NT)

    out_full_b = unpack(places, out_far_b, out_near_b, half_count)
    branch_other = (branch_other + dot(rows_of(mixed_b, 1), out_full_b, NT)).astype(BF)
    branch_came = tp_swap(branch_other, 1)
    branch_own = branch_own + dot(rows_of(mixed_b, 0), out_full_b, NT)
    hidden = inputs + (branch_own + branch_came.astype(F32))
    scale_two = lax.rsqrt(jnp.mean(hidden * hidden, axis=-1, keepdims=True) + EPS)
    norm_own = (hidden * scale_two).astype(BF)
    (norm_own,) = sync(norm_own)

    cut = rows // 2
    norm_core = tp_swap(norm_own, 1)
    norm_x1 = tp_swap(norm_own[:cut], 2)
    norm_own, norm_core, norm_x1 = sync(norm_own, norm_core, norm_x1)
    norms = [norm_own, norm_core]

    norm_x2 = tp_swap(norm_own[cut:], 2)
    norm_d1 = tp_swap(norm_x1, 1)
    product, to_gate, to_up = apply_gate_up(norms, gate_up_full)
    norm_x1, norm_x2, norm_d1, product, to_gate, to_up = sync(
        norm_x1, norm_x2, norm_d1, product, to_gate, to_up
    )

    norm_d2 = tp_swap(norm_x2, 1)
    norms += [norm_x1, norm_x2, norm_d1, norm_d2]
    product, to_gate, to_up = apply_gate_up(norms[2:], gate_up_full, product, to_gate, to_up)
    kept_down, sent_down = weight_gradient(shards.slots, cots, product)
    product, to_gate, to_up, *pieces = sync(product, to_gate, to_up, *sent_down, *cots)
    sent_down, cots = pieces[:2], pieces[2:]

    came_down = [shards.near(sent_down[0])]
    down_parts = [
        dot(product[at * rows : (at + 1) * rows], down_full, NT).astype(BF) for at in (3, 2)
    ]
    down_diagonal = tp_swap(down_parts[0], 1)
    dgate, dup = product_gradient(cots, after(to_gate, *down_parts), to_up, down_full)
    down_far = combine(down_parts[1], down_diagonal)
    dgate, dup, *pieces = sync(dgate, dup, sent_down[1], *down_far, *came_down)
    sent, down_far, came_down = pieces[0], pieces[1:3], pieces[3:]

    others = [k for k in range(1, half_count) if k != part]
    came_down.append(shards.near(sent))
    down_came = [tp_swap(down_far[0], 2)]
    sums_down = list(fold(kept_down[0], came_down[0], part))
    far_sums = [shards.far(sums_down[0], part)]
    kept_gate, sent_gate = weight_gradient(shards.slots, norms, dgate)
    back_x, back_diagonal = feed_back(2 * rows, 2 * rows, dgate, dup, gate_up_full)
    dgate, dup, back_x, back_diagonal, came_down[1], *pieces = sync(
        dgate, dup, back_x, back_diagonal, came_down[1],
        *sent_gate, *down_came, *far_sums, *sums_down, *norms
    )
    sent_gate, down_came, far_sums, sums_down, norms = (
        pieces[:2],
        pieces[2:3],
        pieces[3:4],
        pieces[4 : 4 + part],
        pieces[4 + part :],
    )

    came_gate = [shards.near(sent_gate[0])]
    sums_down = list(fold(kept_down[1], came_down[1], part)) + sums_down
    far_sums += [shards.far(sums_down[k], k) for k in others]
    back_far = combine(back_x, tp_swap(back_diagonal, 1))
    back_came = [tp_swap(back_far[0], 2)]
    kept_up, sent_up = weight_gradient(shards.slots, norms, after(dup, *back_far))
    dgate, dup, *pieces = sync(
        dgate, dup, sent_gate[1], back_far[1], *back_came, *came_gate, *sent_up, *far_sums
    )
    sent, back_far, back_came, came_gate, sent_up, far_sums_down = (
        pieces[0],
        pieces[1],
        pieces[2:3],
        pieces[3:4],
        pieces[4:6],
        pieces[6:],
    )

    came_gate.append(shards.near(sent))
    sums_gate = list(fold(kept_gate[0], came_gate[0], part))
    far_sums = [shards.far(sums_gate[0], part)]
    back_came.append(tp_swap(back_far, 2))
    back_own, back_core = feed_back(0, 2 * rows, dgate, dup, gate_up_full)
    back_own, back_core, product, came_gate[1], down_far[1], *pieces = sync(
        back_own, back_core, product, came_gate[1], down_far[1], *back_came, *sent_up, *far_sums, *sums_gate
    )
    back_came, sent_up, far_sums, sums_gate = pieces[:2], pieces[2:4], pieces[4:5], pieces[5:]

    came_up = [shards.near(sent_up[0])]
    sums_gate = list(fold(kept_gate[1], came_gate[1], part)) + sums_gate
    far_sums += [shards.far(sums_gate[k], k) for k in others]
    down_came.append(tp_swap(down_far[1], 2))
    back_core = tp_swap(back_core, 1)
    grad_norm = (
        back_own.astype(F32)
        + back_core.astype(F32)
        + jnp.concatenate(back_came, 0).astype(F32)
    )
    unit_two = hidden * scale_two
    grad_hidden = cots[0].astype(F32) + scale_two * (
        grad_norm - unit_two * jnp.mean(grad_norm * unit_two, axis=-1, keepdims=True)
    )
    branch_own = grad_hidden.astype(BF)
    branch_other = tp_swap(branch_own, 1)
    down_own = dot(product[:rows], down_full, NT).astype(BF)
    down_core = dot(product[rows : 2 * rows], down_full, NT).astype(BF)
    g_own, grad_own = branch_gradients(
        F32, branch_own, rows_of(mixed_b, 0), after(out_full_b, down_own, down_core)
    )
    branch_other = after(branch_other, g_own, grad_own)
    g_out_b, grad_other = branch_gradients(
        BF, branch_other, rows_of(mixed_b, 1), out_full_b, g_own
    )
    grad_mixed_b = in_order(grad_own, grad_other)
    g_own, grad_own = branch_gradients(
        F32, branch_own, rows_of(mixed_a, 0), after(out_full, grad_other)
    )
    g_out, grad_other = branch_gradients(F32, branch_other, rows_of(mixed_a, 1), out_full, g_own)
    grad_mixed_a = in_order(grad_own, grad_other)
    grad_mixed_b, grad_mixed_a, g_out_b, g_out, down_own, down_core, sent, *pieces = sync(
        grad_mixed_b, grad_mixed_a, g_out_b, g_out, down_own, down_core, sent_up[1], *came_up, *down_came, *far_sums
    )
    came_up, down_came, far_sums_gate = pieces[:1], pieces[1:3], pieces[3:]

    came_up.append(shards.near(sent))
    sums_up = list(fold(kept_up[0], came_up[0], part))
    far_sums = [shards.far(sums_up[0], part)]
    g_out_came = tp_swap(g_out_b, 2)
    down_core = tp_swap(down_core, 1)
    dq_b, dk_b, dv_b = backward_attention(
        chip_table, query_b, grad_mixed_b, mixed_b, lse_b, keys, keys_t, values
    )
    dq_b, dk_b, dv_b, g_out_came, down_core, came_up[1], *pieces = sync(
        dq_b, dk_b, dv_b, g_out_came, down_core, came_up[1], *far_sums, *sums_up
    )
    far_sums, sums_up = pieces[:1], list(fold(kept_up[1], came_up[1], part)) + pieces[1:]

    g_query_b = dot(unit, dq_b, TN).astype(BF)
    g_out = (g_out + g_out_came.astype(F32)).astype(BF)
    (kept_out,), (sent_out,) = split(places, g_out, half_count)
    g_query_b, sent_out, grad_mixed_a, kept_out, *sums_up = sync(
        g_query_b, sent_out, grad_mixed_a, kept_out, *sums_up
    )

    g_query_came = tp_swap(g_query_b, 2)
    far_sums += [shards.far(sums_up[k], k) for k in others]
    came_out = shards.near(sent_out)
    dq_a, dk_a, dv_a = backward_attention(
        chip_table, query_half, grad_mixed_a, mixed_a, lse_a, keys, keys_t, values
    )
    output = finish_output(hidden, down_own, down_core, *down_came)
    dq_a, dk_a, dv_a, g_query_came, came_out, output, *far_sums_up = sync(
        dq_a, dk_a, dv_a, g_query_came, came_out, output, *far_sums
    )

    grad_keys = (dk_a + dk_b) * LN2
    grad_values = dv_a + dv_b
    mine = jnp.where(first_core, grad_keys, grad_values)
    theirs = jnp.where(first_core, grad_values, grad_keys).astype(BF)
    theirs = tp_swap(theirs, 1)
    g_query = (dot(unit, dq_a, TN) + g_query_came.astype(F32)).astype(BF)
    (kept_query,), (sent_query,) = split(places, g_query, half_count)
    sums_out = fold(kept_out, came_out, half_count)
    mine = mine + theirs.astype(F32)
    chip_rows = mine.shape[0] // 2
    mine, own = mine[chip_rows:], mine[:chip_rows].astype(BF)
    mine, own, sent_query, dq_a, dq_b, *pieces = sync(
        mine, own, sent_query, dq_a, dq_b, *sums_out, *far_sums_gate, *far_sums_up, *far_sums_down
    )
    sums_out, pieces = pieces[:half_count], pieces[half_count:]
    far_sums_gate, far_sums_up, far_sums_down = (
        pieces[at * (half_count - 1) : (at + 1) * (half_count - 1)] for at in range(3)
    )

    def total(own, others):
        return functools.reduce(lambda t, o: t + o.astype(F32), others, own.astype(F32))

    earlier = lax.ppermute(own, "tp", [(2, 0), (3, 1)])
    came_query = shards.near(sent_query)
    far_out_sums = [shards.far(sums_out[k], k) for k in range(1, half_count)]
    back_own, back_other = query_back(jnp.reshape(core, (1,)), dq_a, dq_b, in_query, in_query_b)
    grad_w_gate, grad_w_up, gain_two_part = finish_gradients(
        [sums_gate[0], *far_sums_gate],
        [sums_up[0], *far_sums_up],
        w_gate.astype(BF),
        w_up.astype(BF),
        gain_two,
    )
    back_own, back_other, earlier, came_query, grad_w_gate, grad_w_up, gain_two_part, *far_out_sums = sync(
        back_own,
        back_other,
        earlier,
        came_query,
        grad_w_gate,
        grad_w_up,
        gain_two_part,
        *far_out_sums,
    )

    grad_half = (mine + earlier.astype(F32)).astype(BF)
    g_half = dot(unit, grad_half, TN).astype(BF)
    (kept_half,), (sent_half,) = split(places, g_half, half_count)
    sums_query = fold(kept_query, came_query, half_count)
    back_other, back_own, grad_half, sent_half, *sums_query = sync(
        back_other, back_own, grad_half, sent_half, *sums_query
    )

    came_half = shards.near(sent_half)
    far_query = [shards.far(sums_query[k], k) for k in range(1, half_count)]
    in_half = in_full[:, heads:]
    back_other = (back_other + dot(rows_of(grad_half, 1), in_half, NT)).astype(BF)
    back_came = tp_swap(back_other, 1)
    back_own = back_own + dot(rows_of(grad_half, 0), in_half, NT)
    came_half, back_own, back_came, sums_down[0], sums_out[0], *far_query = sync(
        came_half, back_own, back_came, sums_down[0], sums_out[0], *far_query
    )

    sums_half = fold(kept_half, came_half, half_count)
    far_half = [shards.far(sums_half[k], k) for k in range(1, half_count)]
    sums_half = list(sums_half)
    sums_half[0], back_own, sums_down[0], sums_out[0], *far_half = sync(
        sums_half[0], back_own, sums_down[0], sums_out[0], *far_half
    )
    sum_query = total(sums_query[0], far_query)
    sum_half = total(sums_half[0], far_half)

    gain_one_part = jnp.sum(own_query * sum_query, axis=1) + jnp.sum(keyval_half * sum_half, axis=1)
    small = jnp.concatenate(
        [jnp.transpose(sum_half), gain_one_part[None], jnp.transpose(gain_two_part), jnp.zeros((6, sum_half.shape[0]), F32)], 0
    )
    small_came = tp_swap(small, 2)
    grad_tokens = token_gradient(back_own, back_came, tokens.reshape(rows, width), grad_hidden)
    small, small_came, grad_tokens, sums_down[0], sums_out[0] = sync(
        small, small_came, grad_tokens, sums_down[0], sums_out[0]
    )
    small = small + small_came
    other = tp_swap(small, 1)
    grad_w_down = jnp.transpose(total(sums_down[0], far_sums_down))
    grad_w_out = jnp.transpose(total(sums_out[0], far_out_sums))
    gains = small[HD : HD + 2] + other[HD : HD + 2]
    sum_half = jnp.transpose(small[:HD])
    half_swapped = jnp.transpose(other[:HD])
    grad_w_keyval = (
        jnp.where(
            first_core,
            jnp.concatenate([sum_half, half_swapped], 1),
            jnp.concatenate([half_swapped, sum_half], 1),
        )
        * gain_one
    )
    return (
        output.reshape(rows, 1, width),
        grad_tokens,
        sum_query * gain_one,
        grad_w_keyval,
        grad_w_out,
        grad_w_gate,
        grad_w_up,
        grad_w_down,
        gains[0],
        gains[1],
    )


def solution(mesh):
    in_specs = (
        P("tp", "shard", None),
        P("shard", "tp"),
        P("shard", None),
        P("tp", "shard"),
        P("shard", "tp"),
        P("shard", "tp"),
        P("tp", "shard"),
        P("shard"),
        P("shard"),
        P(None, "shard", None),
    )
    out_specs = (
        P("tp", "shard", None),
        P("tp", "shard", None),
        P("shard", "tp"),
        P("shard", None),
        P("tp", "shard"),
        P("shard", "tp"),
        P("shard", "tp"),
        P("tp", "shard"),
        P("shard"),
        P("shard"),
    )
    return jax.shard_map(
        functools.partial(local, mesh.shape["shard"]),
        mesh=mesh,
        in_specs=in_specs,
        out_specs=out_specs,
        check_vma=False,
    )
```
